32 devices in a mesh: dp: 4 (over y, x), ctx: 4 (over z), tp: 2 (over core).
Axes of the slice: x: 2, y: 2, z: 4, core: 2. Of those that a mesh axis runs over, the one named last changes fastest.
Arguments:
- hidden: bfloat16 [4, 2048, 1024], P('dp', 'ctx'), may hold values from -6 to 6
- lengths: int32 [4], P('dp'), may hold values from 512 to 2048, as said below
- cotangent: bfloat16 [4, 2048, 1024], P('dp', 'ctx'), may hold values from -6 to 6
- norm_gain: float32 [1024], replicated, may hold values from 0.5 to 1.5
- proj_main: bfloat16 [1024, 2, 2048], P('dp', None, 'tp'), may hold values from -0.1875 to 0.1875
- proj_state: bfloat16 [1024, 256], P('dp'), may hold values from -0.1875 to 0.1875
- proj_delta: bfloat16 [1024, 32], P('dp', 'tp'), may hold values from -0.1875 to 0.1875
- conv_main: float32 [4, 2048], P(None, 'tp'), may hold values from -3 to 3
- conv_state: float32 [4, 256], replicated, may hold values from -3 to 3
- bias_main: float32 [2048], P('tp'), may hold values from -3 to 3
- bias_state: float32 [256], replicated, may hold values from -3 to 3
- delta_bias: float32 [32], P('tp'), may hold values from -5 to -3
- log_rate: float32 [32], P('tp'), may hold values from -5.5 to 0
- skip_gain: float32 [32], P('tp'), may hold values from 0.5 to 2
- gate_gain: float32 [2048], P('tp'), may hold values from 0.25 to 1.75
- proj_out: bfloat16 [1024, 2048], P('dp', 'tp'), may hold values from -0.125 to 0.125
Outputs:
- mixed: bfloat16 [4, 2048, 1024], P('dp', 'ctx')
- grad_hidden: float32 [4, 2048, 1024], P('dp', 'ctx')
- grad_norm_gain: float32 [1024], P(('dp', 'ctx'))
- grad_proj_main: float32 [1024, 2, 2048], P(('dp', 'ctx'), None, 'tp')
- grad_proj_state: float32 [1024, 256], P(('dp', 'ctx'))
- grad_proj_delta: float32 [1024, 32], P(('dp', 'ctx'), 'tp')
- grad_conv_main: float32 [4, 2048], P(None, 'tp')
- grad_conv_state: float32 [4, 256], replicated
- grad_bias_main: float32 [2048], P('tp')
- grad_bias_state: float32 [256], replicated
- grad_delta_bias: float32 [32], P('tp')
- grad_log_rate: float32 [32], P('tp')
- grad_skip_gain: float32 [32], P('tp')
- grad_gate_gain: float32 [2048], P('tp')
- grad_proj_out: float32 [1024, 2048], P(('dp', 'ctx'), 'tp')
The draws below stay inside these ranges and needn't reach their ends.
Inputs may be any that keep to these rules, and one draw needn't show every extreme that they name: `lengths`: each sequence's valid tokens come first, the rest is padding.
All inputs are finite; a program needn't handle non-finite values.
Results may differ from the reference program's by a relative error of at most 0.00165.
The reference program's roundings to bfloat16 on the way count: a program that leaves them out, or rounds other values in their place, can miss the bound.
Values may be sent and summed in bfloat16 or wider, within the bound.
No kernel may reach another device: no remote copies, remote signals or barrier semaphores. Data moves between devices by JAX's collectives and lax.ppermute only.
A program may use at most 192 MiB of HBM per device.

```python
import jax
import jax.numpy as jnp
from jax import lax

D = 1024
HEADS = 32
HEADDIM = 64
NSTATE = 128
INNER = 2048
KCONV = 4
BLOCK = 256
SEQLEN = 2048
SEQS = 4


def draw_lengths(key, part):
    first, second = jax.random.split(key)
    drawn = jax.random.randint(first, (SEQS,), SEQLEN // 4, SEQLEN + 1)
    order = jax.random.permutation(second, SEQS)
    drawn = drawn.at[order[0]].set(SEQLEN)
    drawn = drawn.at[order[1]].set(SEQLEN // 4)
    return drawn.astype(jnp.int32)


def draw_log_rate(key, part):
    values = jax.random.uniform(key, (HEADS,), jnp.float32, -4.6, 0.0)
    return values


def shard_levels(stream_key, shape, shards, least, top_value):
    factor_of, own = 1.0, jax.random.fold_in(stream_key, 6)
    for axis_at, parts in shards:
        draws = jnp.exp(jax.random.uniform(jax.random.fold_in(own, axis_at), (parts,), jnp.float32, least / len(shards), top_value / len(shards)))
        factor_of = factor_of * jnp.repeat(draws, shape[axis_at] // parts).reshape([-1 if axis == axis_at else 1 for axis in range(len(shape))])
    return factor_of


def scatter_about(own_key, dims, spread, most, shards=(), dtype=jnp.bfloat16):
    values = jax.random.normal(own_key, dims, jnp.float32) * spread
    if len(shards) > 0:
        values = shard_levels(own_key, dims, shards, -0.22, 0.18) * values
    return jnp.clip(values, min=-most, max=most).astype(dtype)


def setup_inputs(seed: int = 0) -> dict:
    arg_keys = jax.random.split(jax.random.key(seed), 17)
    return {
        "hidden": scatter_about(arg_keys[0], (SEQS, SEQLEN, D), 1.0, 6.0, ((0, 4), (1, 4))),
        "lengths": draw_lengths(jax.random.fold_in(arg_keys[16], 71), 0),
        "cotangent": scatter_about(arg_keys[2], (SEQS, SEQLEN, D), 1.0, 6.0, ((0, 4), (1, 4))),
        "norm_gain": jnp.clip(1.0 + 0.1 * jax.random.normal(arg_keys[3], (D,), jnp.float32), 0.5, 1.5),
        "proj_main": scatter_about(arg_keys[4], (D, 2, INNER), D ** -0.5, 0.1875, ((0, 4), (2, 2))),
        "proj_state": scatter_about(arg_keys[5], (D, 2 * NSTATE), D ** -0.5, 0.1875, ((0, 4),)),
        "proj_delta": scatter_about(arg_keys[6], (D, HEADS), D ** -0.5, 0.1875, ((0, 4), (1, 2))),
        "conv_main": scatter_about(arg_keys[7], (KCONV, INNER), KCONV ** -0.5, 3.0, ((1, 2),), jnp.float32),
        "conv_state": scatter_about(arg_keys[8], (KCONV, 2 * NSTATE), KCONV ** -0.5, 3.0, (), jnp.float32),
        "bias_main": scatter_about(arg_keys[9], (INNER,), 0.5, 3.0, ((0, 2),), jnp.float32),
        "bias_state": scatter_about(arg_keys[10], (2 * NSTATE,), 0.5, 3.0, (), jnp.float32),
        "delta_bias": jnp.clip(-5.0 + 2.0 * jax.random.uniform(arg_keys[11], (HEADS,), jnp.float32) ** shard_levels(arg_keys[11], (HEADS,), ((0, 2),), -0.2, 0.2), -5.0, -3.0),
        "log_rate": draw_log_rate(jax.random.fold_in(arg_keys[16], 71), 0),
        "skip_gain": jnp.clip(0.5 + 1.5 * jax.random.uniform(arg_keys[13], (HEADS,), jnp.float32) ** shard_levels(arg_keys[13], (HEADS,), ((0, 2),), -0.2, 0.2), 0.5, 2.0),
        "gate_gain": jnp.clip(1.0 + 0.15 * jax.random.normal(arg_keys[14], (INNER,), jnp.float32), 0.25, 1.75),
        "proj_out": scatter_about(arg_keys[15], (D, INNER), INNER ** -0.5, 0.125, ((0, 4), (1, 2))),
    }


EPS = 1e-05
HIGH = lax.Precision.HIGHEST

@jax.custom_vjp
def low(v):
    return lax.optimization_barrier(v.astype(jnp.bfloat16)).astype(jnp.float32)

@jax.custom_vjp
def low_back(v):
    return v

def low_keep(v):
    return (low(v), None)

def low_pass(kept, grad):
    return (grad,)

def back_keep(v):
    return (v, None)

def back_low(kept, grad):
    return (low(grad),)
low.defvjp(low_keep, low_pass)
low_back.defvjp(back_keep, back_low)

def matmul(left, right):
    return jnp.dot(left, right, precision=HIGH, preferred_element_type=jnp.float32)

def causal_conv(source, taps, bias):
    length = source.shape[0]
    padded = jnp.concatenate([jnp.zeros((KCONV - 1, source.shape[1]), jnp.float32), source], axis=0)
    total = bias + taps[0] * padded[0:length]
    for tap in range(1, KCONV):
        total = total + taps[tap] * padded[tap:tap + length]
    return total

def scan_blocks(signal, inject, readout, delta, rate):
    length = signal.shape[0]
    count = length // BLOCK
    lower = (jnp.arange(BLOCK)[:, None] >= jnp.arange(BLOCK)[None, :])[:, :, None]

    def step(state, block):
        signal_block, inject_block, readout_block, delta_block = block
        levels = jnp.cumsum(delta_block * rate, axis=0)
        decay = jnp.where(lower, jnp.exp(jnp.where(lower, levels[:, None, :] - levels[None, :, :], 0.0)), 0.0)
        affinity = jnp.dot(readout_block, inject_block.T, precision=HIGH, preferred_element_type=jnp.float32)
        within = jnp.einsum('qkh,khp->qhp', decay * affinity[:, :, None], signal_block * delta_block[:, :, None], precision=HIGH)
        across = jnp.einsum('qn,hpn->qhp', readout_block, state, precision=HIGH) * jnp.exp(levels)[:, :, None]
        final_level = levels[-1]
        weights = jnp.exp(final_level[None, :] - levels) * delta_block
        fresh = jnp.einsum('kh,khp,kn->hpn', weights, signal_block, inject_block, precision=HIGH)
        return (jnp.exp(final_level)[:, None, None] * state + fresh, within + across)
    blocks = (signal.reshape(count, BLOCK, HEADS, HEADDIM), inject.reshape(count, BLOCK, NSTATE), readout.reshape(count, BLOCK, NSTATE), delta.reshape(count, BLOCK, HEADS))
    start_state = jnp.zeros((HEADS, HEADDIM, NSTATE), jnp.float32)
    last_state, outputs = lax.scan(jax.checkpoint(step), start_state, blocks)
    return outputs.reshape(length, HEADS, HEADDIM)

def mixer(residual, length, parameters):
    norm_gain, proj_main, proj_state, proj_delta, conv_main, conv_state, bias_main, bias_state, delta_bias, log_rate, skip_gain, gate_gain, proj_out = parameters
    inverse = lax.rsqrt(lax.optimization_barrier(jnp.mean(residual * residual, axis=1, keepdims=True)) + EPS)
    normed = low(residual * inverse * norm_gain)
    main_pre = low_back(matmul(normed, proj_main.reshape(D, 2 * INNER)))
    state_pre = low_back(matmul(normed, proj_state))
    delta_raw = low_back(matmul(normed, proj_delta))
    gate = main_pre[:, :INNER]
    signal = jax.nn.silu(causal_conv(main_pre[:, INNER:], conv_main, bias_main)).reshape(SEQLEN, HEADS, HEADDIM)
    state_act = jax.nn.silu(causal_conv(state_pre, conv_state, bias_state))
    valid = (jnp.arange(SEQLEN) < length).astype(jnp.float32)
    delta = jax.nn.softplus(delta_raw + delta_bias) * valid[:, None]
    rate = -jnp.exp(log_rate)
    output = scan_blocks(signal, state_act[:, :NSTATE], state_act[:, NSTATE:], delta, rate) + skip_gain[:, None] * signal
    product = output.reshape(SEQLEN, INNER) * jax.nn.silu(gate)
    gated = low(product * lax.rsqrt(lax.optimization_barrier(jnp.mean(product * product, axis=1, keepdims=True)) + EPS) * gate_gain)
    branch = low_back(matmul(gated, proj_out.T))
    return residual + valid[:, None] * branch

def reference(hidden, lengths, cotangent, norm_gain, proj_main, proj_state, proj_delta, conv_main, conv_state, bias_main, bias_state, delta_bias, log_rate, skip_gain, gate_gain, proj_out):
    parameters = tuple((value.astype(jnp.float32) for value in (norm_gain, proj_main, proj_state, proj_delta, conv_main, conv_state, bias_main, bias_state, delta_bias, log_rate, skip_gain, gate_gain, proj_out)))
    residual = hidden.astype(jnp.float32)

    def forward(inputs, weights_all):
        one_sequence = jax.checkpoint(lambda item: mixer(item[0], item[1], weights_all))
        return lax.map(one_sequence, (inputs, lengths))
    mixed, pullback = jax.vjp(forward, residual, parameters)
    grad_hidden, gradients = pullback(cotangent.astype(jnp.float32))
    return (mixed.astype(jnp.bfloat16), grad_hidden, gradients[0], gradients[1], gradients[2], gradients[3], gradients[4], gradients[5], gradients[6], gradients[7], gradients[8], gradients[9], gradients[10], gradients[11], gradients[12])
```

```python
import functools

import jax
import jax.numpy as jnp
from jax import lax
from jax.experimental import pallas as pl
from jax.experimental.pallas import tpu as pltpu
from jax.sharding import PartitionSpec as P

BLOCK = 256
EPSILON = 1e-05
HIGH = lax.Precision.HIGH
HIGHEST = lax.Precision.HIGHEST
F32 = jnp.float32
BF16 = jnp.bfloat16
NN = (((1,), (0,)), ((), ()))
NT = (((1,), (1,)), ((), ()))
TN = (((0,), (0,)), ((), ()))
HEAD0 = 64
LO, CORE, BASE, LENGTH, HASPREV, HASNEXT, SLOT0 = range(7)


def mm(a, b, dims=NN, precision=None):
    return lax.dot_general(a, b, dims, precision=precision, preferred_element_type=F32)


def grid_call(body, grid, in_specs, out_specs, out_shape, scratch=(), name=None):
    return pl.pallas_call(
        body,
        grid_spec=pltpu.PrefetchScalarGridSpec(
            num_scalar_prefetch=1,
            grid=grid,
            in_specs=in_specs,
            out_specs=out_specs,
            scratch_shapes=list(scratch),
        ),
        out_shape=out_shape,
        compiler_params=pltpu.CompilerParams(dimension_semantics=("arbitrary",) * len(grid)),
        name=name,
    )


def rows_spec(width, rows=BLOCK, lane=0):
    return pl.BlockSpec((rows, width), lambda b, s: (b, lane))


def whole(shape):
    return pl.BlockSpec(shape, lambda b, s: (0,) * len(shape))


def shaped(shape, dtype=F32):
    return jax.ShapeDtypeStruct(shape, dtype)


def slope(v, sig):
    return sig * (1.0 + v * (1.0 - sig))


def lanes_of(s_ref, slot, width):
    return pl.ds(pl.multiple_of(s_ref[SLOT0 + slot] * width, width), width)


def column_mask(width=128):
    lane = lax.broadcasted_iota(jnp.int32, (1, width), 1)
    return lane


def normalize(x, gain):
    value = x.astype(F32)
    inverse = lax.rsqrt(jnp.mean(value * value, axis=1, keepdims=True) + EPSILON)
    scaled = value * inverse
    return scaled, (scaled * gain).astype(BF16)


def pick(s_ref, b, quarter, own, near, far):
    lo, core = s_ref[LO], s_ref[CORE]
    place = b // quarter
    mine = (place // 2) == lo
    from_near = (place % 2) == core
    return jnp.where(mine, own, jnp.where(from_near, near, far))


def valid_rows(s_ref, b):
    position = s_ref[BASE] + b * BLOCK + lax.broadcasted_iota(jnp.int32, (BLOCK, 1), 0)
    return (position < s_ref[LENGTH]).astype(F32)


def lower_tri():
    row = lax.broadcasted_iota(jnp.int32, (BLOCK, BLOCK), 0)
    col = lax.broadcasted_iota(jnp.int32, (BLOCK, BLOCK), 1)
    return row, col


def front_body(parts, inner, states, quarter, s_ref, own, near, far, halo, gain, taps, bias, dbias, rate,
               expand, *rest):
    ws = rest[:parts]
    (normed_ref, scaled_ref, u_ref, uh_ref, co_ref, draw_ref, delta_ref, lev_ref, hloc_ref, pre_ref) = rest[
        parts : parts + 10
    ]
    hsc, usc, state, pre = rest[parts + 10 :]
    b = pl.program_id(0)
    wide = inner + 2 * states
    shard = ws[0].shape[0]
    scaled, normed = normalize(pick(s_ref, b, quarter, own[...], near[...], far[...]), gain[...])
    scaled_ref[...] = scaled
    normed_ref[...] = normed

    @pl.when(b == 0)
    def _():
        hsc[...] = normalize(halo[...], gain[...])[1]
        edge = jnp.zeros((16, wide), F32)
        for j in range(parts):
            edge += mm(hsc[:, lanes_of(s_ref, j, shard)], ws[j][:, :wide])
        edge = jnp.where(s_ref[HASPREV] > 0, edge[8:], 0.0)
        usc[0:8] = edge
        uh_ref[...] = edge
        state[...] = jnp.zeros_like(state)
        pre[...] = jnp.zeros_like(pre)

    @pl.when(b > 0)
    def _():
        usc[0:8] = usc[BLOCK : BLOCK + 8]

    u = jnp.zeros((BLOCK, wide + 128), F32)
    for j in range(parts):
        u += mm(normed_ref[:, lanes_of(s_ref, j, shard)], ws[j][...])
    usc[8 : 8 + BLOCK] = u[:, :wide]
    u_ref[...] = u[:, :wide]
    conv = bias[...] + taps[0:1] * usc[5 : 5 + BLOCK]
    for k in range(1, 4):
        conv = conv + taps[k : k + 1] * usc[5 + k : 5 + k + BLOCK]
    co_ref[...] = conv
    raw = u[:, wide:] + dbias[...]
    draw_ref[...] = raw
    lane = column_mask()
    heads = inner // 64
    use = (lane >= HEAD0) & (lane < HEAD0 + heads)
    delta = jnp.where(use, jnp.maximum(raw, 0.0) + jnp.log1p(jnp.exp(-jnp.abs(raw))), 0.0)
    delta = delta * valid_rows(s_ref, b)
    delta_ref[...] = delta
    row, col = lower_tri()
    lower = (row >= col).astype(F32)
    level = mm(lower, delta * rate[...], precision=HIGHEST)
    lev_ref[...] = level
    level_x = mm(level, expand[...], precision=HIGHEST)
    delta_x = mm(delta, expand[...], precision=HIGHEST)
    act = conv * jax.nn.sigmoid(conv)
    last = level_x[BLOCK - 1 : BLOCK]
    weighted = jnp.exp(last - level_x) * delta_x * act[:, :inner]
    inject_t = act[:, inner : inner + states].T
    fresh = mm(inject_t, weighted, precision=HIGH)
    before = state[...]

    hloc_ref[b] = before
    pre_ref[b] = pre[...]
    after = jnp.exp(last) * before + fresh
    state[...] = after
    pre[...] = pre[...] + last

    @pl.when(b == pl.num_programs(0) - 1)
    def _():
        hloc_ref[b + 1] = after
        pre_ref[b + 1] = pre[...]


def within_body(inner, states, s_ref, co, delta, lev, expand, yw_ref):
    conv = co[...]
    act = conv * jax.nn.sigmoid(conv)
    inject = act[:, inner : inner + states]
    readout = act[:, inner + states :]
    affinity = mm(readout, inject, NT, HIGH)
    level = lev[...]
    level_t = level.T
    xs = mm(delta[...], expand[...], precision=HIGHEST) * act[:, :inner]
    row, col = lower_tri()
    keep = row >= col
    half = lax.broadcasted_iota(jnp.int32, (1, 128), 1) < 64
    for pair in range(inner // 128):
        x = xs[:, pair * 128 : pair * 128 + 128]
        total = jnp.zeros((BLOCK, 128), F32)
        for side in range(2):
            h = HEAD0 + pair * 2 + side
            diff = level[:, h : h + 1] - level_t[h : h + 1, :]
            mix = jnp.exp(jnp.where(keep, diff, -1e30)) * affinity
            total += mm(mix, jnp.where(half if side == 0 else ~half, x, 0.0), precision=HIGH)
        yw_ref[:, pair * 128 : pair * 128 + 128] = total


def gates_body(parts, quarter, s_ref, normed, own, near, far, *rest):
    ws = rest[:parts]
    gate_ref, gg_ref, bg_ref = rest[parts:]
    b = pl.program_id(0)
    shard = ws[0].shape[0]
    inner = gate_ref.shape[1]
    up = pick(s_ref, b, quarter, own[...], near[...], far[...])
    bg_ref[...] = (up.astype(F32) * valid_rows(s_ref, b)).astype(BF16)
    gate = jnp.zeros(gate_ref.shape, F32)
    gg = jnp.zeros(gg_ref.shape, F32)
    for j in range(parts):
        at = lanes_of(s_ref, j, shard)
        gate += mm(normed[:, at], ws[j][:, :inner])
        gg += mm(bg_ref[:, at], ws[j][:, inner:])
    gate_ref[...] = gate
    gg_ref[...] = gg


def entering(hloc, pre, hin):
    return hloc + jnp.exp(pre[0:1]) * hin


def output_body(inner, states, s_ref, co, lev, yw, gate, gg, hloc, pre, hin, expand, skip, ggain, y_ref, sum_ref):
    conv = co[...]
    act = conv * jax.nn.sigmoid(conv)
    readout = act[:, inner + states :]
    level_x = mm(lev[...], expand[...], precision=HIGHEST)
    held = entering(hloc[0], pre[0], hin[...])
    y = yw[...] + jnp.exp(level_x) * mm(readout, held, precision=HIGH)
    y_ref[...] = y
    out = y + skip[...] * act[:, :inner]
    g = gate[...]
    product = out * (g * jax.nn.sigmoid(g))
    ones = jnp.ones((8, inner), F32)
    sum_ref[0:8] = mm(ones, product * product, NT, HIGHEST)
    sum_ref[8:16] = mm(ones, gg[...] * ggain[...] * product, NT, HIGHEST)


def turn_body(inner, states, total, s_ref, co, lev, y, gate, gg, sums, expand, skip, ggain,
              gated_ref, ggrad_ref, og_ref, gloc_ref, cols_ref, chain):
    step = pl.program_id(0)
    conv = co[...]
    act = conv * jax.nn.sigmoid(conv)
    x = act[:, :inner]
    readout_t = act[:, inner + states :].T
    level_x = mm(lev[...], expand[...], precision=HIGHEST)
    both = sums[...].T
    ginv = lax.rsqrt(both[:, 0:1] / total + EPSILON)
    dot = ginv * both[:, 8:9] / total
    g = gate[...]
    sig = jax.nn.sigmoid(g)
    ga = g * sig
    out = y[...] + skip[...] * x
    unit = out * ga * ginv
    gated_ref[...] = (unit * ggain[...]).astype(BF16)
    grad = gg[...]
    pg = ginv * (grad * ggain[...] - unit * dot)
    og = pg * ga
    og_ref[...] = og
    ggrad_ref[...] = (pg * out * slope(g, sig)).astype(BF16)

    @pl.when(step == 0)
    def _():
        chain[...] = jnp.zeros_like(chain)
        cols_ref[...] = jnp.zeros_like(cols_ref)

    cols_ref[0:1] += jnp.sum(grad * unit, axis=0, keepdims=True)
    cols_ref[1:2] += jnp.sum(og * x, axis=0, keepdims=True)
    b = pl.num_programs(0) - 1 - step
    held = chain[...]
    gloc_ref[b + 1] = held
    last = level_x[BLOCK - 1 : BLOCK]
    held = jnp.exp(last) * held + mm(readout_t, jnp.exp(level_x) * og, precision=HIGH)
    chain[...] = held

    @pl.when(b == 0)
    def _():
        gloc_ref[0] = held


def back_body(inner, states, s_ref, co, delta, lev, og, hloc, pre, hin, expand, z_ref, dbc_ref):
    conv = co[...]
    act = conv * jax.nn.sigmoid(conv)
    inject = act[:, inner : inner + states]
    readout = act[:, inner + states :]
    affinity = mm(inject, readout, NT, HIGH)
    level = lev[...]
    level_t = level.T
    level_x = mm(level, expand[...], precision=HIGHEST)
    xs = mm(delta[...], expand[...], precision=HIGHEST) * act[:, :inner]
    row, col = lower_tri()
    keep = col >= row
    half = lax.broadcasted_iota(jnp.int32, (1, 128), 1) < 64
    grad = jnp.zeros((BLOCK, BLOCK), F32)
    for pair in range(inner // 128):
        at = slice(pair * 128, pair * 128 + 128)
        x = xs[:, at]
        g = og[:, at]
        total = jnp.zeros((BLOCK, 128), F32)
        for side in range(2):
            h = HEAD0 + pair * 2 + side
            mine = half if side == 0 else ~half
            diff = level_t[h : h + 1, :] - level[:, h : h + 1]
            fade = jnp.exp(jnp.where(keep, diff, -1e30))
            total += mm(fade * affinity, jnp.where(mine, g, 0.0), precision=HIGH)
            grad += fade * mm(jnp.where(mine, x, 0.0), g, NT, HIGH)
        z_ref[:, at] = total
    held = entering(hloc[0], pre[0], hin[...])
    dbc_ref[:, :states] = mm(grad, readout, precision=HIGH)
    dbc_ref[:, states:] = mm(grad.T, inject, precision=HIGH) + mm(
        jnp.exp(level_x) * og[...], held, NT, HIGH
    )


def join_body(inner, states, s_ref, co, delta, lev, draw, og, y, z, dbc, hloc, pre, total, gloc, gin, hin,
              expand, rate, skip, cg_ref, dbco_ref, rg_ref, cols_ref):
    step = pl.program_id(0)
    conv = co[...]
    sig = jax.nn.sigmoid(conv)
    act = conv * sig
    x = act[:, :inner]
    inject = act[:, inner : inner + states]
    level_x = mm(lev[...], expand[...], precision=HIGHEST)
    dlt = delta[...]
    delta_x = mm(dlt, expand[...], precision=HIGHEST)
    last = level_x[BLOCK - 1 : BLOCK]
    later = gloc[0] + jnp.exp(total[0, 0:1] - pre[0, 0:1]) * gin[...]
    fade = jnp.exp(last - level_x)
    zed = z[...] + fade * mm(inject, later, precision=HIGH)
    dbco_ref[:, :states] = dbc[:, :states] + mm(fade * delta_x * x, later, NT, HIGH)
    dbco_ref[:, states:] = dbc[:, states:]
    g = og[...]
    dx = delta_x * zed + skip[...] * g
    cg_ref[...] = dx * slope(conv[:, :inner], sig[:, :inner])
    direct = mm(x * zed, expand[...], NT, HIGHEST)
    read = mm(g * y[...], expand[...], NT, HIGHEST)
    held = entering(hloc[0], pre[0], hin[...])
    ends = jnp.sum(later * held, axis=0, keepdims=True)
    ends = mm(jnp.broadcast_to(ends, (8, inner)), expand[...], NT, HIGHEST)[0:1]
    row, col = lower_tri()
    upper = (col >= row).astype(F32)
    q = mm(upper, read - dlt * direct, precision=HIGHEST) + ends
    b = pl.num_programs(0) - 1 - step
    lane = column_mask()
    use = (lane >= HEAD0) & (lane < HEAD0 + inner // 64)
    rg = (direct + rate[...] * q) * valid_rows(s_ref, b) * jax.nn.sigmoid(draw[...])
    rg = jnp.where(use, rg, 0.0)
    rg_ref[...] = rg

    @pl.when(step == 0)
    def _():
        cols_ref[...] = jnp.zeros_like(cols_ref)

    cols_ref[0:1] += jnp.sum(rg, axis=0, keepdims=True)
    cols_ref[1:2] += jnp.sum(jnp.where(use, dlt * q, 0.0), axis=0, keepdims=True)


def conv_body(mix, s_ref, cg, after, ahead, u, prior, uh, taps, *rest):
    if mix:
        rg, out_ref, cols_ref, csc, usc = rest
    else:
        out_ref, cols_ref, csc, usc = rest
    b = pl.program_id(0)
    count = pl.num_programs(0)
    grad = cg[...]
    csc[0:BLOCK] = grad
    csc[BLOCK : BLOCK + 8] = jnp.where(
        b == count - 1, jnp.where(s_ref[HASNEXT] > 0, ahead[...], 0.0), after[...]
    )
    usc[0:8] = jnp.where(b == 0, uh[...], prior[...])
    usc[8 : 8 + BLOCK] = u[...]
    pre = taps[0:1] * csc[3 : 3 + BLOCK]
    for k in range(1, 4):
        pre = pre + taps[k : k + 1] * csc[3 - k : 3 - k + BLOCK]

    @pl.when(b == 0)
    def _():
        cols_ref[...] = jnp.zeros_like(cols_ref)

    for k in range(4):
        cols_ref[k : k + 1] += jnp.sum(grad * usc[5 + k : 5 + k + BLOCK], axis=0, keepdims=True)
    cols_ref[4:5] += jnp.sum(grad, axis=0, keepdims=True)
    if mix:
        turned = pltpu.roll(pre, 64, 1)
        pre = jnp.where(s_ref[CORE] > 0, turned, pre)
        lane = lax.broadcasted_iota(jnp.int32, (BLOCK, 128), 1)
        pre = jnp.where(lane < HEAD0, pre, rg[...])
    out_ref[...] = pre.astype(BF16)


def weight_body(parts, s_ref, left, right, *outs):
    j = pl.program_id(0)
    value = mm(left[...], right[...], TN)
    for k in range(parts):

        @pl.when(j == k)
        def _():
            outs[k][...] = value


def feature_body(parts, s_ref, ggrad, mg, xg, scaled, *rest):
    ws1 = rest[:parts]
    ws2 = rest[parts : 2 * parts]
    out_ref, cols_ref = rest[2 * parts :]
    b = pl.program_id(0)
    inner = ggrad.shape[1]
    shard = ws1[0].shape[0]
    for j in range(parts):
        at = lanes_of(s_ref, j, shard)
        out_ref[:, at] = (
            mm(ggrad[...], ws2[j][:, :inner], NT)
            + mm(mg[...], ws1[j][:, :inner], NT)
            + mm(xg[...], ws1[j][:, -128:], NT)
        )

    @pl.when(b == 0)
    def _():
        cols_ref[...] = jnp.zeros_like(cols_ref)

    cols_ref[0:1] += jnp.sum(out_ref[...] * scaled[...], axis=0, keepdims=True)


def branch_body(parts, s_ref, gated, *rest):
    ws2 = rest[:parts]
    out_ref = rest[parts]
    inner = gated.shape[1]
    shard = ws2[0].shape[0]
    for j in range(parts):
        out_ref[:, lanes_of(s_ref, j, shard)] = mm(gated[...], ws2[j][:, inner:], NT)


def per_device(
    hidden, lengths, cotangent, norm_gain, proj_main, proj_state, proj_delta, conv_main, conv_state,
    bias_main, bias_state, delta_bias, log_rate, skip_gain, gate_gain, proj_out,
):
    _, steps, model = hidden.shape
    hidden, cotangent = hidden[0], cotangent[0]
    dps, ctxs, tps = lax.axis_size("dp"), lax.axis_size("ctx"), lax.axis_size("tp")
    dp, z, core = lax.axis_index("dp"), lax.axis_index("ctx"), lax.axis_index("tp")
    lo, hi = z % 2, z // 2
    pairs = ctxs // 2
    tokens = 2 * steps
    count = tokens // BLOCK
    quarter = count // 4
    inner = bias_main.shape[0] // 2
    heads = delta_bias.shape[0] // 2
    states = bias_state.shape[0] // 2
    wide = inner + 2 * states

    def swap(value):
        return lax.ppermute(value, "tp", [(0, 1), (1, 0)])

    def across(value, j):
        return lax.ppermute(value, "ctx", [(i, i ^ j) for i in range(ctxs)])

    def along(value, step):
        return lax.ppermute(
            value, "ctx", [(i, i + step) for i in range(ctxs) if 0 <= i + step < ctxs]
        )

    def spread(value, j):
        return lax.ppermute(value, "dp", [(i, i ^ j) for i in range(dps)])

    def mine(value, axis, size):
        return lax.dynamic_slice_in_dim(value, lo * size, size, axis)

    def piece(value, at, size):
        return lax.dynamic_slice_in_dim(value, at * size, size, 0)

    apart = proj_main.shape[0] % 128 == 0
    parts = dps if apart else 1
    shard = proj_main.shape[0] * (dps // parts)

    def gathered(value):
        if not apart:
            return [lax.all_gather(value, "dp", axis=0, tiled=True)]
        return [value] + [spread(value, j) for j in range(1, dps)]

    scalars = jnp.stack(
        [lo, core, hi * tokens, lengths[0], (hi > 0).astype(jnp.int32), (hi < pairs - 1).astype(jnp.int32)]
        + [dp ^ j if apart else 0 * dp for j in range(parts)]
    ).astype(jnp.int32)

    main_part = mine(proj_main, 2, inner)
    state_own = lax.dynamic_slice_in_dim(proj_state, lo * states + core * (states // 2), states // 2, 1)
    delta_own = mine(proj_delta, 1, heads)
    first = jnp.concatenate(
        [main_part[:, 1], proj_state, state_own, delta_own, jnp.zeros((proj_main.shape[0], 64 - heads), BF16)], axis=1
    )
    second = jnp.concatenate([main_part[:, 0], mine(proj_out, 1, inner)], axis=1)

    edge = along(hidden[steps - 16 :], 1)
    ws1 = gathered(first)
    halfway = steps // 2
    near = across(jnp.concatenate([piece(hidden, core, halfway), edge]), 1)
    halo = jnp.where(lo == 0, edge, near[halfway:])
    near = near[:halfway]
    far = swap(near)
    cot_near = across(piece(cotangent, core, halfway), 1)
    cot_far = swap(cot_near)
    ws2 = gathered(second)

    taps_x = jnp.concatenate([mine(conv_main, 1, inner), conv_state], axis=1)
    bias_x = jnp.concatenate([mine(bias_main, 0, inner), bias_state])[None]
    rate_own = -jnp.exp(mine(log_rate, 0, heads))

    def in_heads(value):
        return jnp.pad(value, (HEAD0, 128 - HEAD0 - heads))[None]

    rate_row = in_heads(rate_own)
    dbias_row = in_heads(mine(delta_bias, 0, heads))
    skip_row = jnp.repeat(mine(skip_gain, 0, heads), inner // heads)[None]
    ggain_row = mine(gate_gain, 0, inner)[None]
    gain_row = norm_gain[None]
    expand = (
        lax.broadcasted_iota(jnp.int32, (128, inner), 0) - HEAD0
        == lax.broadcasted_iota(jnp.int32, (128, inner), 1) // (inner // heads)
    ).astype(F32)

    own_spec = pl.BlockSpec(
        (BLOCK, model), lambda b, s: (jnp.clip(b - s[LO] * 2 * quarter, 0, 2 * quarter - 1), 0)
    )
    part_spec = pl.BlockSpec((BLOCK, model), lambda b, s: (b % quarter, 0))
    state_block = pl.BlockSpec((1, states, inner), lambda b, s: (b, 0, 0))
    pre_block = pl.BlockSpec((1, 8, inner), lambda b, s: (b, 0, 0))

    normed, scaled, u, uh, conv, draw, delta, level, hloc, pre = grid_call(
        functools.partial(front_body, parts, inner, states, quarter),
        (count,),
        [own_spec, part_spec, part_spec, whole((16, model)), whole((1, model)), whole((4, wide)),
         whole((1, wide)), whole((1, 128)), whole((1, 128)), whole((128, inner))]
        + [whole((shard, wide + 128))] * parts,
        [rows_spec(model), rows_spec(model), rows_spec(wide), whole((8, wide)), rows_spec(wide),
         rows_spec(128), rows_spec(128), rows_spec(128), whole((count + 1, states, inner)),
         whole((count + 1, 8, inner))],
        [shaped((tokens, model), BF16), shaped((tokens, model)), shaped((tokens, wide)), shaped((8, wide)),
         shaped((tokens, wide)), shaped((tokens, 128)), shaped((tokens, 128)), shaped((tokens, 128)),
         shaped((count + 1, states, inner)), shaped((count + 1, 8, inner))],
        [pltpu.VMEM((16, model), BF16), pltpu.VMEM((8 + BLOCK, wide), F32), pltpu.VMEM((states, inner), F32),
         pltpu.VMEM((8, inner), F32)],
        name="front",
    )(scalars, hidden, near, far, halo, gain_row, taps_x, bias_x, dbias_row, rate_row, expand, *ws1)

    own_end = hloc[count]
    growth = jnp.exp(pre[count][0:1])
    carried = jnp.zeros_like(own_end)
    sending = own_end
    for hop in range(pairs - 1):
        carried = along(sending, 2)
        if hop < pairs - 2:
            sending = own_end + growth * carried

    (inside,) = grid_call(
        functools.partial(within_body, inner, states),
        (count,),
        [rows_spec(wide), rows_spec(128), rows_spec(128), whole((128, inner))],
        [rows_spec(inner)],
        [shaped((tokens, inner))],
        name="within",
    )(scalars, conv, delta, level, expand)

    gate, gated_grad, branch_grad = grid_call(
        functools.partial(gates_body, parts, quarter),
        (count,),
        [rows_spec(model), own_spec, part_spec, part_spec] + [whole((shard, 2 * inner))] * parts,
        [rows_spec(inner), rows_spec(inner), rows_spec(model)],
        [shaped((tokens, inner)), shaped((tokens, inner)), shaped((tokens, model), BF16)],
        name="gates",
    )(scalars, normed, cotangent, cot_near, cot_far, *ws2)

    y, sums = grid_call(
        functools.partial(output_body, inner, states),
        (count,),
        [rows_spec(wide), rows_spec(128), rows_spec(inner), rows_spec(inner), rows_spec(inner), state_block,
         pre_block, whole((states, inner)), whole((128, inner)), whole((1, inner)), whole((1, inner))],
        [rows_spec(inner), pl.BlockSpec((16, BLOCK), lambda b, s: (0, b))],
        [shaped((tokens, inner)), shaped((16, tokens))],
        name="output",
    )(scalars, conv, level, inside, gate, gated_grad, hloc, pre, carried, expand, skip_row, ggain_row)

    sums = sums + swap(sums)
    sums = sums + across(sums, 1)

    def back(width, rows=BLOCK):
        return pl.BlockSpec((rows, width), lambda b, s: (count - 1 - b, 0))

    gated, gate_grad, out_grad, gloc, turn_cols = grid_call(
        functools.partial(turn_body, inner, states, 2 * tps * inner),
        (count,),
        [back(wide), back(128), back(inner), back(inner), back(inner),
         pl.BlockSpec((16, BLOCK), lambda b, s: (0, count - 1 - b)), whole((128, inner)), whole((1, inner)),
         whole((1, inner))],
        [back(inner), back(inner), back(inner), whole((count + 1, states, inner)), whole((8, inner))],
        [shaped((tokens, inner), BF16), shaped((tokens, inner), BF16), shaped((tokens, inner)),
         shaped((count + 1, states, inner)), shaped((8, inner))],
        [pltpu.VMEM((states, inner), F32)],
        name="turn",
    )(scalars, conv, level, y, gate, gated_grad, sums, expand, skip_row, ggain_row)

    own_start = gloc[0]
    returned = jnp.zeros_like(own_start)
    sending = own_start
    for hop in range(pairs - 1):
        returned = along(sending, -2)
        if hop < pairs - 2:
            sending = own_start + growth * returned

    zed, dbc = grid_call(
        functools.partial(back_body, inner, states),
        (count,),
        [rows_spec(wide), rows_spec(128), rows_spec(128), rows_spec(inner), state_block, pre_block,
         whole((states, inner)), whole((128, inner))],
        [rows_spec(inner), rows_spec(2 * states)],
        [shaped((tokens, inner)), shaped((tokens, 2 * states))],
        name="back",
    )(scalars, conv, delta, level, out_grad, hloc, pre, carried, expand)

    later_state = pl.BlockSpec((1, states, inner), lambda b, s: (count - b, 0, 0))
    later_pre = pl.BlockSpec((1, 8, inner), lambda b, s: (count - b, 0, 0))
    conv_grad, dbc, raw_grad, head_cols = grid_call(
        functools.partial(join_body, inner, states),
        (count,),
        [back(wide), back(128), back(128), back(128), back(inner), back(inner), back(inner), back(2 * states),
         later_state, later_pre, pl.BlockSpec((1, 8, inner), lambda b, s: (count, 0, 0)), later_state,
         whole((states, inner)), whole((states, inner)), whole((128, inner)), whole((1, 128)),
         whole((1, inner))],
        [back(inner), back(2 * states), back(128), whole((8, 128))],
        [shaped((tokens, inner)), shaped((tokens, 2 * states)), shaped((tokens, 128)), shaped((8, 128))],
        name="join",
    )(scalars, conv, delta, level, draw, out_grad, y, zed, dbc, hloc, pre, pre, gloc, returned, carried, expand,
      rate_row, skip_row)

    dbc = piece(dbc, core, tokens // 2) + swap(piece(dbc, 1 - core, tokens // 2))
    dbc = mine(dbc, 1, states) + across(lax.dynamic_slice_in_dim(dbc, (1 - lo) * states, states, 1), 1)
    other = swap(dbc)
    dbc = jnp.where(core == 0, jnp.concatenate([dbc, other]), jnp.concatenate([other, dbc]))
    conv_x = lax.dynamic_slice_in_dim(conv, inner + lo * states, states, 1)
    state_cg = dbc * slope(conv_x, jax.nn.sigmoid(conv_x))

    def conv_call(grad, lanes, width, name, mixed_in=None):
        ahead = along(grad[:8], -2)
        per = BLOCK // 8
        extra = [] if mixed_in is None else [mixed_in]
        return grid_call(
            functools.partial(conv_body, mixed_in is not None),
            (count,),
            [rows_spec(width),
             pl.BlockSpec((8, width), lambda b, s: (jnp.minimum((b + 1) * per, count * per - 1), 0)),
             whole((8, width)),
             pl.BlockSpec((BLOCK, width), lambda b, s: (b, lanes(s))),
             pl.BlockSpec((8, width), lambda b, s: (jnp.maximum(b * per - 1, 0), lanes(s))),
             pl.BlockSpec((8, width), lambda b, s: (0, lanes(s))),
             pl.BlockSpec((4, width), lambda b, s: (0, lanes(s)))] + [rows_spec(128)] * len(extra),
            [rows_spec(width), whole((8, width))],
            [shaped((tokens, width), BF16), shaped((8, width))],
            [pltpu.VMEM((BLOCK + 8, width), F32), pltpu.VMEM((BLOCK + 8, width), F32)],
            name=name,
        )(scalars, grad, grad, ahead, u, u, uh, taps_x, *extra)

    signal_pre, signal_cols = conv_call(conv_grad, lambda s: 0, inner, "conv_signal")
    extra_pre, state_cols = conv_call(
        state_cg, lambda s: inner // states + s[LO], states, "conv_state", raw_grad
    )

    def weight_grad(left, right, name):
        width = right.shape[1]
        return grid_call(
            functools.partial(weight_body, parts),
            (parts,),
            [pl.BlockSpec((tokens, shard), lambda j, s: (0, s[SLOT0 + j])), whole((tokens, width))],
            [whole((shard, width))] * parts,
            [shaped((shard, width))] * parts,
            name=name,
        )(scalars, left, right)

    def over_tokens(pieces):
        total = pieces[0]
        if not apart:
            total = lax.psum_scatter(total, "dp", scatter_dimension=0, tiled=True)
        for j in range(1, parts):
            total = total + spread(pieces[j], j)
        size = total.shape[0] // ctxs
        own = piece(total, z, size)
        width = total.shape[1]
        opposite = jnp.zeros((size, width), F32)
        for j in range(1, ctxs):
            got = across(piece(total, z ^ j, size), j)
            if j % 2 == 0:
                own = own + got
            else:
                opposite = opposite + got
        return jnp.where(lo == 0, own, opposite), jnp.where(lo == 0, opposite, own)

    gate_sum = over_tokens(weight_grad(normed, gate_grad, "grad_gate"))
    out_sum = over_tokens(weight_grad(branch_grad, gated, "grad_out"))
    signal_sum = over_tokens(weight_grad(normed, signal_pre, "grad_signal"))
    extra_sum = over_tokens(weight_grad(normed, extra_pre, "grad_extra"))

    (branch,) = grid_call(
        functools.partial(branch_body, parts),
        (count,),
        [rows_spec(inner)] + [whole((shard, 2 * inner))] * parts,
        [rows_spec(model)],
        [shaped((tokens, model))],
        name="branch",
    )(scalars, gated, *ws2)

    feature, feature_cols = grid_call(
        functools.partial(feature_body, parts),
        (count,),
        [rows_spec(inner), rows_spec(inner), rows_spec(128), rows_spec(model)]
        + [whole((shard, wide + 128))] * parts + [whole((shard, 2 * inner))] * parts,
        [rows_spec(model), whole((8, model))],
        [shaped((tokens, model)), shaped((8, model))],
        name="feature",
    )(scalars, gate_grad, signal_pre, extra_pre, scaled, *ws1, *ws2)

    def over_channels(value):
        value = value.reshape(2, 2, halfway, model)
        keep = lax.dynamic_index_in_dim(value, core, 1, False)
        give = lax.dynamic_index_in_dim(value, 1 - core, 1, False)
        value = keep + swap(give)
        return lax.dynamic_index_in_dim(value, lo, 0, False) + across(
            lax.dynamic_index_in_dim(value, 1 - lo, 0, False), 1
        )

    def both_halves(value):
        other = swap(value)
        return jnp.where(core == 0, jnp.concatenate([value, other]), jnp.concatenate([other, value]))

    residual = piece(hidden, core, halfway).astype(F32)
    place = z * steps + core * halfway + lax.broadcasted_iota(jnp.int32, (halfway, 1), 0)
    valid = (place < lengths[0]).astype(F32)
    mixed = both_halves((residual + valid * over_channels(branch)).astype(BF16))

    feature_grad = over_channels(feature)
    inverse = lax.rsqrt(jnp.mean(residual * residual, axis=1, keepdims=True) + EPSILON)
    scaled_own = residual * inverse
    scaled_grad = feature_grad * norm_gain
    upstream = piece(cotangent, core, halfway).astype(F32)
    grad_hidden = both_halves(
        upstream + inverse * (scaled_grad - scaled_own * jnp.mean(scaled_grad * scaled_own, axis=1, keepdims=True))
    )

    def halves(value, axis=-1):
        blank = jnp.zeros_like(value)
        return jnp.where(
            lo == 0, jnp.concatenate([value, blank], axis), jnp.concatenate([blank, value], axis)
        )

    skip_sum = turn_cols[1].reshape(heads, inner // heads).sum(axis=1)
    head_rows = head_cols[0:2, HEAD0 : HEAD0 + heads]
    small = lax.psum(
        (
            halves(signal_cols[:5]),
            halves(state_cols[:5]),
            halves(turn_cols[0:1]),
            halves(jnp.stack([head_rows[0], head_rows[1] * rate_own, skip_sum])),
        ),
        ("dp", "ctx"),
    )
    gain_sum = lax.psum(
        lax.psum_scatter(feature_cols[0], ("dp", "ctx"), scatter_dimension=0, tiled=True), "tp"
    )

    main_sum = jnp.stack(
        [jnp.concatenate(gate_sum, axis=1), jnp.concatenate(signal_sum, axis=1)], axis=1
    )
    delta_sum = jnp.concatenate([part[:, HEAD0 : HEAD0 + heads] for part in extra_sum], axis=1)
    state_here = jnp.stack([part[:, :HEAD0] for part in extra_sum])
    state_there = swap(state_here)
    in_order = jnp.where(
        core == 0, jnp.stack([state_here, state_there], 1), jnp.stack([state_there, state_here], 1)
    )
    state_sum = jnp.transpose(in_order, (2, 0, 1, 3)).reshape(-1, 2 * states)

    return (
        mixed[None],
        grad_hidden[None],
        gain_sum,
        main_sum,
        state_sum,
        delta_sum,
        small[0][:4],
        small[1][:4],
        small[0][4],
        small[1][4],
        small[3][0],
        small[3][1],
        small[3][2],
        small[2][0],
        jnp.concatenate(out_sum, axis=1),
    )


def solution(mesh):
    in_specs = (
        P("dp", "ctx", None), P("dp"), P("dp", "ctx", None), P(), P("dp", None, "tp"), P("dp", None),
        P("dp", "tp"), P(None, "tp"), P(), P("tp"), P(), P("tp"), P("tp"), P("tp"), P("tp"), P("dp", "tp"),
    )
    out_specs = (
        P("dp", "ctx", None), P("dp", "ctx", None), P(("dp", "ctx")), P(("dp", "ctx"), None, "tp"),
        P(("dp", "ctx"), None), P(("dp", "ctx"), "tp"), P(None, "tp"), P(), P("tp"), P(), P("tp"), P("tp"),
        P("tp"), P("tp"), P(("dp", "ctx"), "tp"),
    )
    return jax.shard_map(
        per_device, mesh=mesh, in_specs=in_specs, out_specs=out_specs, check_vma=False
    )
```

```python
import functools

import jax
import jax.numpy as jnp
from jax import lax
from jax.experimental import pallas as pl
from jax.experimental.pallas import tpu as pltpu
from jax.sharding import PartitionSpec as P

BLOCK = 256
SUB = 128
EPSILON = 1e-05
HIGH = lax.Precision.HIGH
HIGHEST = lax.Precision.HIGHEST
F32 = jnp.float32
BF16 = jnp.bfloat16
NN = (((1,), (0,)), ((), ()))
NT = (((1,), (1,)), ((), ()))
TN = (((0,), (0,)), ((), ()))
HEAD0 = 64
LO, CORE, BASE, LENGTH, HASPREV, HASNEXT, SLOT0 = range(7)


def mm(a, b, dims=NN, precision=None):
    return lax.dot_general(a, b, dims, precision=precision, preferred_element_type=F32)


def grid_call(body, grid, in_specs, out_specs, out_shape, scratch=(), name=None):
    return pl.pallas_call(
        body,
        grid_spec=pltpu.PrefetchScalarGridSpec(
            num_scalar_prefetch=1,
            grid=grid,
            in_specs=in_specs,
            out_specs=out_specs,
            scratch_shapes=list(scratch),
        ),
        out_shape=out_shape,
        compiler_params=pltpu.CompilerParams(dimension_semantics=("arbitrary",) * len(grid)
        ),
        name=name,
    )


def rows_spec(width, rows=BLOCK, lane=0):
    return pl.BlockSpec((rows, width), lambda b, s: (b, lane))


def whole(shape):
    return pl.BlockSpec(shape, lambda b, s: (0,) * len(shape))


def shaped(shape, dtype=F32):
    return jax.ShapeDtypeStruct(shape, dtype)


def slope(v, sig):
    return sig * (1.0 + v * (1.0 - sig))


def lanes_of(s_ref, slot, width):
    return pl.ds(pl.multiple_of(s_ref[SLOT0 + slot] * width, width), width)


def normalize(x, gain):
    value = x.astype(F32)
    inverse = lax.rsqrt(jnp.mean(value * value, axis=1, keepdims=True) + EPSILON)
    scaled = value * inverse
    return scaled, (scaled * gain).astype(BF16)


def pick(s_ref, b, quarter, own, near, far):
    lo, core = s_ref[LO], s_ref[CORE]
    place = b // quarter
    mine = (place // 2) == lo
    from_near = (place % 2) == core
    return jnp.where(mine, own, jnp.where(from_near, near, far))


def valid_rows(s_ref, b):
    position = s_ref[BASE] + b * BLOCK + lax.broadcasted_iota(jnp.int32, (BLOCK, 1), 0)
    return (position < s_ref[LENGTH]).astype(F32)


def expander(inner):
    lane = lax.broadcasted_iota(jnp.int32, (384, inner), 0) % 128 - HEAD0
    head = lax.broadcasted_iota(jnp.int32, (384, inner), 1) // 64
    return (lane == head).astype(F32).astype(BF16)


def collector(inner):
    head = lax.broadcasted_iota(jnp.int32, (3 * inner, 128), 0) % inner // 64
    lane = lax.broadcasted_iota(jnp.int32, (3 * inner, 128), 1) - HEAD0
    return (lane == head).astype(F32).astype(BF16)


def two(x):
    high = x.astype(BF16)
    return high, (x - high.astype(F32)).astype(BF16)


def three(x, axis=1):
    high = x.astype(BF16)
    rest = x - high.astype(F32)
    middle = rest.astype(BF16)
    return jnp.concatenate([high, middle, (rest - middle.astype(F32)).astype(BF16)], axis=axis)


def running(tri, x):
    width = x.shape[1]
    wide = mm(tri, three(x))
    return wide[:, :width] + wide[:, width : 2 * width] + wide[:, 2 * width :]


def triangle(forward):
    row = lax.broadcasted_iota(jnp.int32, (BLOCK, BLOCK), 0)
    col = lax.broadcasted_iota(jnp.int32, (BLOCK, BLOCK), 1)
    same = (row // SUB) == (col // SUB)
    keep = (row >= col) if forward else (col >= row)
    return (same & keep).astype(F32).astype(BF16)


def stacked_heads(x):
    half = lax.broadcasted_iota(jnp.int32, (1, 128), 1) < 64
    return two(jnp.concatenate([jnp.where(half, x, 0.0), jnp.where(half, 0.0, x)], axis=0))


def faded(keep, level, level_t, level_x, pair, forward):
    out = []
    for side in range(2):
        h = HEAD0 + 2 * pair + side
        at = pair * 128 + side * 64
        column, row = level_x[:, at : at + 1], level_t[h : h + 1, :]
        diff = column - row if forward else row - column
        out.append(jnp.exp(jnp.where(keep, diff, -1e30)))
    return jnp.concatenate(out, axis=1)


def mixed_heads(mix, high, low):
    mh, ml = two(mix)
    wide = mm(mh, jnp.concatenate([high, low], axis=1))
    return wide[:, :128] + wide[:, 128:] + mm(ml, high)


def head_lanes(inner):
    lane = lax.broadcasted_iota(jnp.int32, (1, 128), 1)
    return (lane >= HEAD0) & (lane < HEAD0 + inner // 64)


def front_body(parts, inner, states, quarter, s_ref, own, near, far, halo, gain, taps, bias, dbias, rate,
               *rest):
    ws = rest[:parts]
    (normed_ref, u_ref, uh_ref, co_ref, draw_ref, delta_ref, lev_ref, lx_ref, dx_ref, hloc_ref,
     pre_ref, end_ref) = rest[parts : parts + 12]
    hsc, usc, state, pre, esc = rest[parts + 12 :]
    b = pl.program_id(0)
    wide = inner + 2 * states
    shard = ws[0].shape[0]
    normed_ref[...] = normalize(pick(s_ref, b, quarter, own[...], near[...], far[...]), gain[...])[1]

    @pl.when(b == 0)
    def _():
        hsc[...] = normalize(halo[...], gain[...])[1]
        edge = jnp.zeros((16, wide), F32)
        for j in range(parts):
            edge += mm(hsc[:, lanes_of(s_ref, j, shard)], ws[j][:, :wide])
        edge = jnp.where(s_ref[HASPREV] > 0, edge[8:], 0.0)
        usc[0:8] = edge
        uh_ref[...] = edge
        state[...] = jnp.zeros_like(state)
        pre[...] = jnp.zeros_like(pre)
        esc[...] = expander(inner)

    @pl.when(b > 0)
    def _():
        usc[0:8] = usc[BLOCK : BLOCK + 8]

    u = jnp.zeros((BLOCK, wide + 128), F32)
    for j in range(parts):
        u += mm(normed_ref[:, lanes_of(s_ref, j, shard)], ws[j][...])
    usc[8 : 8 + BLOCK] = u[:, :wide]
    u_ref[...] = u[:, :wide]
    conv = bias[...] + taps[0:1] * usc[5 : 5 + BLOCK]
    for k in range(1, 4):
        conv = conv + taps[k : k + 1] * usc[5 + k : 5 + k + BLOCK]
    co_ref[...] = conv
    raw = u[:, wide:] + dbias[...]
    draw_ref[...] = raw
    delta = jnp.where(head_lanes(inner), jnp.maximum(raw, 0.0) + jnp.log1p(jnp.exp(-jnp.abs(raw))), 0.0)
    delta = delta * valid_rows(s_ref, b)
    delta_ref[...] = delta
    level = running(triangle(True), delta * rate[...])
    lev_ref[...] = level
    both = mm(jnp.concatenate([three(level), three(delta)], axis=0), esc[...])
    level_x, delta_x = both[:BLOCK], both[BLOCK:]
    lx_ref[...] = level_x
    dx_ref[...] = delta_x
    act = conv * jax.nn.sigmoid(conv)
    source = delta_x * act[:, :inner]
    inject_t = act[:, inner : inner + states].T
    for i in range(BLOCK // SUB):
        at = slice(i * SUB, (i + 1) * SUB)
        last = level_x[(i + 1) * SUB - 1 : (i + 1) * SUB]
        fresh = mm(inject_t[:, at], jnp.exp(last - level_x[at]) * source[at], precision=HIGH)
        before = state[...]
        n = b * (BLOCK // SUB) + i
        hloc_ref[n] = before
        pre_ref[n] = pre[...]
        state[...] = jnp.exp(last) * before + fresh
        pre[...] = pre[...] + last

    @pl.when(b == pl.num_programs(0) - 1)
    def _():
        hloc_ref[n + 1] = state[...]
        end_ref[...] = state[...]
        pre_ref[n + 1] = pre[...]


def within_body(inner, states, s_ref, co, lev, lx, dx, yw_ref):
    conv = co[...]
    act = conv * jax.nn.sigmoid(conv)
    xs = dx[...] * act[:, :inner]
    level = lev[...]
    keep = lax.broadcasted_iota(jnp.int32, (SUB, SUB), 0) >= lax.broadcasted_iota(jnp.int32, (SUB, SUB), 1)
    for i in range(BLOCK // SUB):
        at = slice(i * SUB, (i + 1) * SUB)
        affinity = mm(act[at, inner + states :], act[at, inner : inner + states], NT, HIGH)
        affinity = jnp.concatenate([affinity, affinity], axis=1)
        level_t = level[at].T
        level_x = lx[at]
        for pair in range(inner // 128):
            lanes = slice(pair * 128, pair * 128 + 128)
            mix = faded(keep, level, level_t, level_x, pair, True) * affinity
            yw_ref[at, lanes] = mixed_heads(mix, *stacked_heads(xs[at, lanes]))


def gates_body(parts, quarter, s_ref, normed, own, near, far, *rest):
    ws = rest[:parts]
    gate_ref, gg_ref, bg_ref = rest[parts:]
    b = pl.program_id(0)
    shard = ws[0].shape[0]
    inner = gate_ref.shape[1]
    up = pick(s_ref, b, quarter, own[...], near[...], far[...])
    bg_ref[...] = (up.astype(F32) * valid_rows(s_ref, b)).astype(BF16)
    gate = jnp.zeros(gate_ref.shape, F32)
    gg = jnp.zeros(gg_ref.shape, F32)
    for j in range(parts):
        at = lanes_of(s_ref, j, shard)
        gate += mm(normed[:, at], ws[j][:, :inner])
        gg += mm(bg_ref[:, at], ws[j][:, inner:])
    gate_ref[...] = gate
    gg_ref[...] = gg


def entering(hloc, pre, hin):
    return hloc + jnp.exp(pre[0:1]) * hin


def output_body(inner, states, s_ref, co, lx, yw, gate, gg, hloc, pre, hin, skip, ggain, y_ref, sum_ref):
    conv = co[...]
    act = conv * jax.nn.sigmoid(conv)
    for i in range(BLOCK // SUB):
        at = slice(i * SUB, (i + 1) * SUB)
        held = entering(hloc[i], pre[i], hin[...])
        y_ref[at] = yw[at] + jnp.exp(lx[at]) * mm(act[at, inner + states :], held, precision=HIGH)
    out = y_ref[...] + skip[...] * act[:, :inner]
    g = gate[...]
    product = out * (g * jax.nn.sigmoid(g))
    ones = jnp.ones((8, 3 * inner), BF16)
    sum_ref[0:8] = mm(ones, three(product * product), NT)
    sum_ref[8:16] = mm(ones, three(gg[...] * ggain[...] * product), NT)


def turn_body(inner, states, total, s_ref, co, lx, y, gate, gg, sums, more, skip, ggain,
              gated_ref, ggrad_ref, og_ref, gloc_ref, start_ref, cols_ref, chain):
    step = pl.program_id(0)
    conv = co[...]
    act = conv * jax.nn.sigmoid(conv)
    x = act[:, :inner]
    readout_t = act[:, inner + states :].T
    both = (sums[...] + more[...]).T
    ginv = lax.rsqrt(both[:, 0:1] / total + EPSILON)
    dot = ginv * both[:, 8:9] / total
    g = gate[...]
    sig = jax.nn.sigmoid(g)
    ga = g * sig
    out = y[...] + skip[...] * x
    unit = out * ga * ginv
    gated_ref[...] = (unit * ggain[...]).astype(BF16)
    grad = gg[...]
    pg = ginv * (grad * ggain[...] - unit * dot)
    og = pg * ga
    og_ref[...] = og
    ggrad_ref[...] = (pg * out * slope(g, sig)).astype(BF16)

    @pl.when(step == 0)
    def _():
        chain[...] = jnp.zeros_like(chain)
        cols_ref[...] = jnp.zeros_like(cols_ref)

    cols_ref[0:1] += jnp.sum(grad * unit, axis=0, keepdims=True)
    cols_ref[1:2] += jnp.sum(og * x, axis=0, keepdims=True)
    b = pl.num_programs(0) - 1 - step
    for i in reversed(range(BLOCK // SUB)):
        at = slice(i * SUB, (i + 1) * SUB)
        held = chain[...]
        n = b * (BLOCK // SUB) + i
        gloc_ref[n + 1] = held
        level_x = lx[at]
        chain[...] = jnp.exp(level_x[SUB - 1 : SUB]) * held + mm(
            readout_t[:, at], jnp.exp(level_x) * og[at], precision=HIGH
        )

    @pl.when(b == 0)
    def _():
        gloc_ref[0] = chain[...]
        start_ref[...] = chain[...]


def back_body(inner, states, s_ref, co, lev, lx, dx, og, hloc, pre, hin, z_ref, dbc_ref):
    conv = co[...]
    act = conv * jax.nn.sigmoid(conv)
    xs = dx[...] * act[:, :inner]
    level = lev[...]
    keep = lax.broadcasted_iota(jnp.int32, (SUB, SUB), 1) >= lax.broadcasted_iota(jnp.int32, (SUB, SUB), 0)
    for i in range(BLOCK // SUB):
        at = slice(i * SUB, (i + 1) * SUB)
        inject, readout = act[at, inner : inner + states], act[at, inner + states :]
        affinity = mm(inject, readout, NT, HIGH)
        affinity = jnp.concatenate([affinity, affinity], axis=1)
        level_t = level[at].T
        level_x = lx[at]
        grad = jnp.zeros((SUB, SUB), F32)
        for pair in range(inner // 128):
            lanes = slice(pair * 128, pair * 128 + 128)
            fade = faded(keep, level, level_t, level_x, pair, False)
            g = og[at, lanes]
            z_ref[at, lanes] = mixed_heads(fade * affinity, *stacked_heads(g))
            xh, xl = stacked_heads(xs[at, lanes])
            gh, gl = two(g)
            outer = mm(
                jnp.concatenate([xh, xl], axis=1), jnp.concatenate([gh, gh], axis=1), NT
            ) + mm(xh, gl, NT)
            grad += fade[:, :SUB] * outer[:SUB] + fade[:, SUB:] * outer[SUB:]
        held = entering(hloc[i], pre[i], hin[...])
        dbc_ref[at, :states] = mm(grad, readout, precision=HIGH)
        dbc_ref[at, states:] = mm(grad.T, inject, precision=HIGH) + mm(
            jnp.exp(level_x) * og[at], held, NT, HIGH
        )


def conv_back(grad, csc, usc, taps, cols_ref):
    csc[0:BLOCK] = grad
    pre = taps[0:1] * csc[3 : 3 + BLOCK]
    for k in range(1, 4):
        pre = pre + taps[k : k + 1] * csc[3 - k : 3 - k + BLOCK]
    for k in range(4):
        cols_ref[k : k + 1] += jnp.sum(grad * usc[5 + k : 5 + k + BLOCK], axis=0, keepdims=True)
    cols_ref[4:5] += jnp.sum(grad, axis=0, keepdims=True)
    csc[BLOCK : BLOCK + 8] = grad[0:8]
    return pre


def join_body(inner, states, s_ref, co, delta, lx, dx, draw, og, y, z, dbc, hloc, pre, gloc, gin, hin, u, prior,
              uh, taps, rate, skip, mg_ref, tail_ref, head_ref, keep_ref, give_ref, rg_ref, cols_ref, sig_ref,
              col_sc, csc, usc):
    step = pl.program_id(0)
    subs = BLOCK // SUB
    count = pl.num_programs(0)
    b = count - 1 - step

    @pl.when(step == 0)
    def _():
        cols_ref[...] = jnp.zeros_like(cols_ref)
        sig_ref[...] = jnp.zeros_like(sig_ref)
        col_sc[...] = collector(inner)
        csc[BLOCK : BLOCK + 8] = jnp.zeros((8, inner), F32)

    conv = co[...]
    sig = jax.nn.sigmoid(conv)
    act = conv * sig
    x = act[:, :inner]
    delta_x = dx[...]
    ends = []
    zeds = []
    inject_grads = []
    for i in range(subs):
        at = slice(i * SUB, (i + 1) * SUB)
        n = b * subs + i + 1
        level_x = lx[at]
        later = gloc[n] + jnp.exp(pre[subs * count][0:1] - pre[n][0:1]) * gin[...]
        fade = jnp.exp(level_x[SUB - 1 : SUB] - level_x)
        zeds.append(z[at] + fade * mm(act[at, inner : inner + states], later, precision=HIGH))
        inject_grads.append(dbc[at, :states] + mm(fade * delta_x[at] * x[at], later, NT, HIGH))
        held = entering(hloc[n], pre[n], hin[...])
        ends.append(jnp.sum(later * held, axis=0, keepdims=True))
    zed = jnp.concatenate(zeds, axis=0)
    inject_grad = jnp.concatenate(inject_grads, axis=0)
    half = count // 2
    rows = pl.ds(pl.multiple_of((b % half) * BLOCK, BLOCK), BLOCK)

    @pl.when(b // half == s_ref[CORE])
    def _():
        keep_ref[rows, :states] = inject_grad
        keep_ref[rows, states:] = dbc[:, states:]

    @pl.when(b // half != s_ref[CORE])
    def _():
        give_ref[rows, :states] = inject_grad
        give_ref[rows, states:] = dbc[:, states:]

    g = og[...]
    ends = jnp.concatenate(ends + [jnp.zeros((8 - subs, inner), F32)], axis=0)
    sums = mm(three(jnp.concatenate([x * zed, g * y[...], ends], axis=0)), col_sc[...])
    direct, read, ends = sums[:BLOCK], sums[BLOCK : 2 * BLOCK], sums[2 * BLOCK :]
    dlt = delta[...]
    q = running(triangle(False), read - dlt * direct)
    q = jnp.concatenate([q[i * SUB : (i + 1) * SUB] + ends[i : i + 1] for i in range(subs)], axis=0)
    rg = (direct + rate[...] * q) * valid_rows(s_ref, b) * jax.nn.sigmoid(draw[...])
    rg = jnp.where(head_lanes(inner), rg, 0.0)
    rg_ref[...] = rg
    cols_ref[0:1] += jnp.sum(rg, axis=0, keepdims=True)
    cols_ref[1:2] += jnp.sum(dlt * q, axis=0, keepdims=True)

    usc[0:8] = jnp.where(b == 0, uh[...], prior[...])
    usc[8 : 8 + BLOCK] = u[...]
    grad = (delta_x * zed + skip[...] * g) * slope(conv[:, :inner], sig[:, :inner])
    pre_grad = conv_back(grad, csc, usc, taps, sig_ref)
    mg_ref[...] = pre_grad.astype(BF16)
    head_ref[...] = grad[0:8]

    @pl.when(step == 0)
    def _():
        tail_ref[...] = pre_grad[BLOCK - 8 :]


def early_body(parts, s_ref, left1, right1, left2, right2, *outs):
    j = pl.program_id(0)
    width = right1.shape[1]
    first = mm(left1[...], right1[...], TN)
    second = mm(left2[...], right2[...], TN)
    for k in range(parts):

        @pl.when(j == k)
        def _():
            outs[k][:, :width] = first
            outs[k][:, width:] = second


def late_body(parts, s_ref, left, right1, right2, small, *outs):
    j = pl.program_id(0)
    width = right1.shape[1]
    rows = left.shape[1]
    first = mm(left[...], right1[...], TN)
    second = mm(left[...], right2[...], TN)
    for k in range(parts):

        @pl.when(j == k)
        def _():
            outs[k][:rows, :width] = first
            outs[k][:rows, width:] = second
            outs[k][rows:] = small[...]


def deal(s_ref, b, quarter, value, outs):
    place = b // quarter
    rows = pl.ds(pl.multiple_of((b % quarter) * BLOCK, BLOCK), BLOCK)
    at = (place % 2 != s_ref[CORE]).astype(jnp.int32) * 2 + (place // 2 != s_ref[LO]).astype(jnp.int32)
    for k in range(4):

        @pl.when(at == k)
        def _():
            outs[k][rows] = value


def feature_body(parts, quarter, s_ref, own, near, far, ggrad, mg, rg, dbc, dbc_other, co, u, prior, uh, ahead,
                 taps, *rest):
    ws1 = rest[:parts]
    ws2 = rest[parts : 2 * parts]
    outs = rest[2 * parts : 2 * parts + 4]
    xg_ref, cols_ref, state_ref, whole_sc, csc, usc = rest[2 * parts + 4 :]
    step = pl.program_id(0)
    count = pl.num_programs(0)
    b = count - 1 - step
    inner = ggrad.shape[1]
    shard = ws1[0].shape[0]

    @pl.when(step == 0)
    def _():
        cols_ref[...] = jnp.zeros_like(cols_ref)
        state_ref[...] = jnp.zeros_like(state_ref)
        csc[BLOCK : BLOCK + 8] = jnp.where(s_ref[HASNEXT] > 0, ahead[...], 0.0)

    usc[0:8] = jnp.where(b == 0, uh[...], prior[...])
    usc[8 : 8 + BLOCK] = u[...]
    conv = co[...]
    grad = jnp.where(b // (count // 2) == s_ref[CORE], dbc[...], dbc_other[...])
    grad = grad * slope(conv, jax.nn.sigmoid(conv))
    pre = conv_back(grad, csc, usc, taps, state_ref)
    pre = jnp.where(s_ref[CORE] > 0, pltpu.roll(pre, 64, 1), pre)
    lane = lax.broadcasted_iota(jnp.int32, (BLOCK, 128), 1)
    xg = jnp.where(lane < HEAD0, pre, rg[...]).astype(BF16)
    xg_ref[...] = xg
    for j in range(parts):
        at = lanes_of(s_ref, j, shard)
        whole_sc[:, at] = (
            mm(ggrad[...], ws2[j][:, :inner], NT)
            + mm(mg[...], ws1[j][:, :inner], NT)
            + mm(xg, ws1[j][:, -128:], NT)
        )
    value = whole_sc[...]
    scaled = normalize(pick(s_ref, b, quarter, own[...], near[...], far[...]), 1.0)[0]
    cols_ref[0:1] += jnp.sum(value * scaled, axis=0, keepdims=True)
    deal(s_ref, b, quarter, value, outs)


def branch_body(parts, quarter, s_ref, gated, *rest):
    ws2 = rest[:parts]
    outs = rest[parts : parts + 4]
    whole_sc = rest[parts + 4]
    inner = gated.shape[1]
    shard = ws2[0].shape[0]
    for j in range(parts):
        whole_sc[:, lanes_of(s_ref, j, shard)] = mm(gated[...], ws2[j][:, inner:], NT)
    deal(s_ref, pl.program_id(0), quarter, whole_sc[...], outs)


def per_device(
    hidden, lengths, cotangent, norm_gain, proj_main, proj_state, proj_delta, conv_main, conv_state,
    bias_main, bias_state, delta_bias, log_rate, skip_gain, gate_gain, proj_out,
):
    _, steps, model = hidden.shape
    hidden, cotangent = hidden[0], cotangent[0]
    dps, ctxs, tps = lax.axis_size("dp"), lax.axis_size("ctx"), lax.axis_size("tp")
    dp, z, core = lax.axis_index("dp"), lax.axis_index("ctx"), lax.axis_index("tp")
    lo, hi = z % 2, z // 2
    pairs = ctxs // 2
    tokens = 2 * steps
    count = tokens // BLOCK
    quarter = count // 4
    inner = bias_main.shape[0] // 2
    heads = delta_bias.shape[0] // 2
    states = bias_state.shape[0] // 2
    wide = inner + 2 * states

    def swap(value):
        return lax.ppermute(value, "tp", [(0, 1), (1, 0)])

    def across(value, j):
        return lax.ppermute(value, "ctx", [(i, i ^ j) for i in range(ctxs)])

    def along(value, step):
        return lax.ppermute(
            value, "ctx", [(i, i + step) for i in range(ctxs) if 0 <= i + step < ctxs]
        )

    def spread(value, j):
        return lax.ppermute(value, "dp", [(i, i ^ j) for i in range(dps)])

    def mine(value, axis, size):
        return lax.dynamic_slice_in_dim(value, lo * size, size, axis)

    def piece(value, at, size):
        return lax.dynamic_slice_in_dim(value, at * size, size, 0)

    apart = proj_main.shape[0] % 128 == 0
    parts = dps if apart else 1
    shard = proj_main.shape[0] * (dps // parts)

    def gathered(value):
        if not apart:
            return [lax.all_gather(value, "dp", axis=0, tiled=True)]
        return [value] + [spread(value, j) for j in range(1, dps)]

    scalars = jnp.stack(
        [lo, core, hi * tokens, lengths[0], (hi > 0).astype(jnp.int32), (hi < pairs - 1).astype(jnp.int32)]
        + [dp ^ j if apart else 0 * dp for j in range(parts)]
    ).astype(jnp.int32)

    state_own = lax.dynamic_slice_in_dim(proj_state, lo * states + core * (states // 2), states // 2, 1)
    delta_own = mine(proj_delta, 1, heads)
    main_part = mine(proj_main, 2, inner)
    first = jnp.concatenate(
        [main_part[:, 1], proj_state, state_own, delta_own,
         jnp.zeros((proj_main.shape[0], 64 - heads), BF16)], axis=1
    )
    halfway = steps // 2
    near = across(piece(hidden, core, halfway), 1)
    far = swap(near)
    edge, _ = lax.optimization_barrier((hidden[steps - 16 :], first))
    halo = jnp.where(lo == 0, along(edge, 1), along(edge, 2))
    ws1 = gathered(first)
    ws1, near, main_gate, out_later, cot_later = lax.optimization_barrier(
        (ws1, near, main_part[:, 0], proj_out, cotangent)
    )
    second = jnp.concatenate([main_gate, mine(out_later, 1, inner)], axis=1)
    cot_near = across(piece(cot_later, core, halfway), 1)
    ws2 = gathered(second)

    def over_sequences(pieces):
        return [spread(pieces[j], j) for j in range(1, parts)]

    def chunks(pieces, got, extra=0):
        total = pieces[0]
        rows = total.shape[0] - extra
        if not apart:
            shared = [lax.psum(total[rows:], "dp")] if extra else []
            total = jnp.concatenate(
                [lax.psum_scatter(total[:rows], "dp", scatter_dimension=0, tiled=True)] + shared
            )
            rows = total.shape[0] - extra
        for part in got:
            total = total + part
        size = rows // ctxs

        def chunk(j):
            part = piece(total, z ^ j, size)
            return jnp.concatenate([part, total[rows:]]) if extra else part

        return [chunk(j) for j in range(ctxs)]

    def over_positions(cut):
        return [across(cut[j], j) for j in range(1, ctxs)]

    def settled(cut, got, extra=0):
        own, opposite = cut[0], got[0]
        for j in range(2, ctxs):
            if j % 2 == 0:
                own = own + got[j - 1]
            else:
                opposite = opposite + got[j - 1]
        size = own.shape[0] - extra
        own, opposite = jnp.where(lo == 0, own, opposite), jnp.where(lo == 0, opposite, own)
        return (own[:size], opposite[:size]), (own[size:], opposite[size:])

    taps_x = jnp.concatenate([mine(conv_main, 1, inner), conv_state], axis=1)
    bias_x = jnp.concatenate([mine(bias_main, 0, inner), bias_state])[None]
    rate_own = -jnp.exp(mine(log_rate, 0, heads))

    def in_heads(value):
        return jnp.pad(value, (HEAD0, 128 - HEAD0 - heads))[None]

    rate_row = in_heads(rate_own)
    dbias_row = in_heads(mine(delta_bias, 0, heads))
    skip_row = jnp.repeat(mine(skip_gain, 0, heads), inner // heads)[None]
    ggain_row = mine(gate_gain, 0, inner)[None]
    gain_row = norm_gain[None]
    own_spec = pl.BlockSpec(
        (BLOCK, model), lambda b, s: (jnp.clip(b - s[LO] * 2 * quarter, 0, 2 * quarter - 1), 0)
    )
    part_spec = pl.BlockSpec((BLOCK, model), lambda b, s: (b % quarter, 0))
    subs = BLOCK // SUB
    last = count * subs
    state_block = pl.BlockSpec((subs, states, inner), lambda b, s: (b, 0, 0))
    pre_block = pl.BlockSpec((subs, 8, inner), lambda b, s: (b, 0, 0))

    normed, u, uh, conv, draw, delta, level, level_x, delta_x, hloc, pre, own_end = grid_call(
        functools.partial(front_body, parts, inner, states, quarter),
        (count,),
        [own_spec, part_spec, part_spec, whole((16, model)), whole((1, model)), whole((4, wide)),
         whole((1, wide)), whole((1, 128)), whole((1, 128))] + [whole((shard, wide + 128))] * parts,
        [rows_spec(model), rows_spec(wide), whole((8, wide)), rows_spec(wide), rows_spec(128), rows_spec(128),
         rows_spec(128), rows_spec(inner), rows_spec(inner), whole((last + 1, states, inner)),
         whole((last + 1, 8, inner)), whole((states, inner))],
        [shaped((tokens, model), BF16), shaped((tokens, wide)), shaped((8, wide)), shaped((tokens, wide)),
         shaped((tokens, 128)), shaped((tokens, 128)), shaped((tokens, 128)), shaped((tokens, inner)),
         shaped((tokens, inner)), shaped((last + 1, states, inner)), shaped((last + 1, 8, inner)), shaped((states, inner))],
        [pltpu.VMEM((16, model), BF16), pltpu.VMEM((8 + BLOCK, wide), F32), pltpu.VMEM((states, inner), F32),
         pltpu.VMEM((8, inner), F32), pltpu.VMEM((384, inner), BF16)],
        name="front",
    )(scalars, hidden, near, far, halo, gain_row, taps_x, bias_x, dbias_row, rate_row, *ws1)

    cot_near, own_end = lax.optimization_barrier((cot_near, own_end))
    cot_far = swap(cot_near)
    growth = jnp.exp(pre[last][0:1])
    carried = jnp.zeros_like(own_end)
    sending = own_end
    for hop in range(pairs - 1):
        carried = along(sending, 2)
        if hop < pairs - 2:
            sending = own_end + growth * carried

    (inside,) = grid_call(
        functools.partial(within_body, inner, states),
        (count,),
        [rows_spec(wide), rows_spec(128), rows_spec(inner), rows_spec(inner)],
        [rows_spec(inner)],
        [shaped((tokens, inner))],
        name="within",
    )(scalars, conv, level, level_x, delta_x)

    gate, gated_grad, branch_grad = grid_call(
        functools.partial(gates_body, parts, quarter),
        (count,),
        [rows_spec(model), own_spec, part_spec, part_spec] + [whole((shard, 2 * inner))] * parts,
        [rows_spec(inner), rows_spec(inner), rows_spec(model)],
        [shaped((tokens, inner)), shaped((tokens, inner)), shaped((tokens, model), BF16)],
        name="gates",
    )(scalars, normed, cotangent, cot_near, cot_far, *ws2)

    y, sums = grid_call(
        functools.partial(output_body, inner, states),
        (count,),
        [rows_spec(wide), rows_spec(inner), rows_spec(inner), rows_spec(inner), rows_spec(inner), state_block,
         pre_block, whole((states, inner)), whole((1, inner)), whole((1, inner))],
        [rows_spec(inner), pl.BlockSpec((16, BLOCK), lambda b, s: (0, b))],
        [shaped((tokens, inner)), shaped((16, tokens))],
        name="output",
    )(scalars, conv, level_x, inside, gate, gated_grad, hloc, pre, carried, skip_row, ggain_row)

    sums = sums + swap(sums)
    more_sums = across(sums, 1)

    def back(width, rows=BLOCK):
        return pl.BlockSpec((rows, width), lambda b, s: (count - 1 - b, 0))

    back_sums = pl.BlockSpec((16, BLOCK), lambda b, s: (0, count - 1 - b))
    gated, gate_grad, out_grad, gloc, own_start, turn_cols = grid_call(
        functools.partial(turn_body, inner, states, 2 * tps * inner),
        (count,),
        [back(wide), back(inner), back(inner), back(inner), back(inner),
         back_sums, back_sums, whole((1, inner)), whole((1, inner))],
        [back(inner), back(inner), back(inner), whole((last + 1, states, inner)), whole((states, inner)),
         whole((8, inner))],
        [shaped((tokens, inner), BF16), shaped((tokens, inner), BF16), shaped((tokens, inner)),
         shaped((last + 1, states, inner)), shaped((states, inner)), shaped((8, inner))],
        [pltpu.VMEM((states, inner), F32)],
        name="turn",
    )(scalars, conv, level_x, y, gate, gated_grad, sums, more_sums, skip_row, ggain_row)

    returned = jnp.zeros_like(own_start)
    sending = own_start
    for hop in range(pairs - 1):
        returned = along(sending, -2)
        if hop < pairs - 2:
            sending = own_start + growth * returned

    turned = pl.BlockSpec((tokens, shard), lambda j, s: (0, s[SLOT0 + j]))
    early = grid_call(
        functools.partial(early_body, parts),
        (parts,),
        [turned, whole((tokens, inner)), turned, whole((tokens, inner))],
        [whole((shard, 2 * inner))] * parts,
        [shaped((shard, 2 * inner))] * parts,
        name="grad_early",
    )(scalars, normed, gate_grad, branch_grad, gated)

    early, out_grad = lax.optimization_barrier((early, out_grad))
    early_got = over_sequences(early)

    zed, dbc = grid_call(
        functools.partial(back_body, inner, states),
        (count,),
        [rows_spec(wide), rows_spec(128), rows_spec(inner), rows_spec(inner), rows_spec(inner), state_block,
         pre_block, whole((states, inner))],
        [rows_spec(inner), rows_spec(2 * states)],
        [shaped((tokens, inner)), shaped((tokens, 2 * states))],
        name="back",
    )(scalars, conv, level, level_x, delta_x, out_grad, hloc, pre, carried)

    all_states = whole((last + 1, states, inner))
    all_pre = whole((last + 1, 8, inner))
    per = BLOCK // 8
    half_rows = tokens // 2

    def back_lanes(width, lanes):
        return [
            pl.BlockSpec((BLOCK, width), lambda b, s: (count - 1 - b, lanes(s))),
            pl.BlockSpec((8, width), lambda b, s: (jnp.maximum((count - 1 - b) * per - 1, 0), lanes(s))),
            pl.BlockSpec((8, width), lambda b, s: (0, lanes(s))),
        ]

    def table(rows, width, lanes):
        return pl.BlockSpec((rows, width), lambda b, s: (0, lanes(s)))

    signal_pre, tail, head, dbc_keep, dbc_give, raw_grad, head_cols, signal_cols = grid_call(
        functools.partial(join_body, inner, states),
        (count,),
        [back(wide), back(128), back(inner), back(inner), back(128), back(inner), back(inner), back(inner),
         back(2 * states), all_states, all_pre, all_states, whole((states, inner)), whole((states, inner))]
        + back_lanes(inner, lambda s: 0)
        + [table(4, inner, lambda s: 0), whole((1, 128)), whole((1, inner))],
        [back(inner), whole((8, inner)), whole((8, inner)), whole((half_rows, 2 * states)),
         whole((half_rows, 2 * states)), back(128), whole((8, 128)), whole((8, inner))],
        [shaped((tokens, inner), BF16), shaped((8, inner)), shaped((8, inner)), shaped((half_rows, 2 * states)),
         shaped((half_rows, 2 * states)), shaped((tokens, 128)), shaped((8, 128)), shaped((8, inner))],
        [pltpu.VMEM((3 * inner, 128), BF16), pltpu.VMEM((BLOCK + 8, inner), F32),
         pltpu.VMEM((BLOCK + 8, inner), F32)],
        name="join",
    )(scalars, conv, delta, level_x, delta_x, draw, out_grad, y, zed, dbc, hloc, pre, gloc, returned, carried,
      u, u, uh, taps_x, rate_row, skip_row)

    ahead = jnp.where(hi < pairs - 1, along(head, -2), 0.0)
    for k in range(3):
        tail = tail + taps_x[k, :inner] * jnp.concatenate([jnp.zeros((5 + k, inner), F32), ahead[: 3 - k]])
    signal_pre = lax.dynamic_update_slice_in_dim(signal_pre, tail.astype(BF16), tokens - 8, 0)

    dbc = dbc_keep + swap(dbc_give)
    dbc_back = across(lax.dynamic_slice_in_dim(dbc, (1 - lo) * states, states, 1), 1)
    gated_later, early_got, _ = lax.optimization_barrier((gated, early_got, dbc))
    branch = grid_call(
        functools.partial(branch_body, parts, quarter),
        (count,),
        [rows_spec(inner)] + [whole((shard, 2 * inner))] * parts,
        [whole((halfway, model))] * 4,
        [shaped((halfway, model))] * 4,
        [pltpu.VMEM((BLOCK, model), F32)],
        name="branch",
    )(scalars, gated_later, *ws2)

    def over_cores(dealt):
        return dealt[0] + swap(dealt[2]), dealt[1] + swap(dealt[3])

    branch_mine, branch_theirs = over_cores(branch)

    dbc = mine(dbc, 1, states) + dbc_back
    dbc_other = swap(dbc)
    head_rows = jnp.where(core == 0, dbc[:8], dbc_other[:8])
    head_conv = lax.dynamic_slice(conv, (0, inner + lo * states), (8, states))
    state_ahead = along(head_rows * slope(head_conv, jax.nn.sigmoid(head_conv)), -2)
    early_cut = chunks(early, early_got)
    branch_theirs, early_cut, state_ahead = lax.optimization_barrier((branch_theirs, early_cut, state_ahead))
    branch_back = across(branch_theirs, 1)
    early_far = over_positions(early_cut)

    def back_own(b, s):
        return jnp.clip(count - 1 - b - s[LO] * 2 * quarter, 0, 2 * quarter - 1), 0

    def state_lanes(s):
        return inner // states + s[LO]

    back_part = pl.BlockSpec((BLOCK, model), lambda b, s: ((count - 1 - b) % quarter, 0))
    back_half = pl.BlockSpec((BLOCK, states), lambda b, s: ((count - 1 - b) % (count // 2), 0))
    state_side = back_lanes(states, state_lanes)
    *feature, extra_pre, feature_cols, state_cols = grid_call(
        functools.partial(feature_body, parts, quarter),
        (count,),
        [pl.BlockSpec((BLOCK, model), back_own), back_part, back_part, back(inner), back(inner), back(128),
         back_half, back_half, state_side[0]] + state_side
        + [whole((8, states)), table(4, states, state_lanes)]
        + [whole((shard, wide + 128))] * parts + [whole((shard, 2 * inner))] * parts,
        [whole((halfway, model))] * 4 + [back(128), whole((8, model)), whole((8, states))],
        [shaped((halfway, model))] * 4 + [shaped((tokens, 128), BF16), shaped((8, model)), shaped((8, states))],
        [pltpu.VMEM((BLOCK, model), F32), pltpu.VMEM((BLOCK + 8, states), F32),
         pltpu.VMEM((BLOCK + 8, states), F32)],
        name="feature",
    )(scalars, hidden, near, far, gate_grad, signal_pre, raw_grad, dbc, dbc_other, conv, u, u, uh, state_ahead,
      taps_x, *ws1, *ws2)
    feature_mine, feature_theirs = over_cores(feature)

    folds = model // inner
    small = jnp.concatenate(
        [
            jnp.concatenate([signal_cols, state_cols], axis=1),
            jnp.concatenate([turn_cols[:2], head_cols[:2]], axis=1),
            jnp.pad(feature_cols[0].reshape(folds, inner), ((0, 6 - folds), (0, 128))),
        ]
    )
    late = grid_call(
        functools.partial(late_body, parts),
        (parts,),
        [turned, whole((tokens, inner)), whole((tokens, 128)), whole((16, inner + 128))],
        [whole((shard + 16, inner + 128))] * parts,
        [shaped((shard + 16, inner + 128))] * parts,
        name="grad_late",
    )(scalars, normed, signal_pre, extra_pre, small)
    late, feature_theirs, early_far, branch_back = lax.optimization_barrier(
        (late, feature_theirs, early_far, branch_back)
    )
    early_sum, _ = settled(early_cut, early_far)
    late_got, feature_back = lax.optimization_barrier((over_sequences(late), across(feature_theirs, 1)))
    late_cut = chunks(late, late_got, 16)
    late_sum, small_sum = settled(late_cut, over_positions(late_cut), 16)

    def both_halves(value):
        other = swap(value)
        return jnp.where(core == 0, jnp.concatenate([value, other]), jnp.concatenate([other, value]))

    residual = piece(hidden, core, halfway).astype(F32)
    place = z * steps + core * halfway + lax.broadcasted_iota(jnp.int32, (halfway, 1), 0)
    valid = (place < lengths[0]).astype(F32)
    mixed = both_halves((residual + valid * (branch_mine + branch_back)).astype(BF16))

    feature_grad = feature_mine + feature_back
    inverse = lax.rsqrt(jnp.mean(residual * residual, axis=1, keepdims=True) + EPSILON)
    scaled_own = residual * inverse
    scaled_grad = feature_grad * norm_gain
    upstream = piece(cotangent, core, halfway).astype(F32)
    grad_hidden = both_halves(
        upstream + inverse * (scaled_grad - scaled_own * jnp.mean(scaled_grad * scaled_own, axis=1, keepdims=True))
    )

    def side_by_side(pair):
        return jnp.concatenate(pair, axis=-1)

    signal_small = side_by_side([part[:, :inner] for part in small_sum])
    state_small = side_by_side([part[:8, inner:] for part in small_sum])
    heads_small = [part[8:10, inner + HEAD0 : inner + HEAD0 + heads] for part in small_sum]
    rate_all = -jnp.exp(log_rate)
    skip_sum = signal_small[9].reshape(2 * heads, inner // heads).sum(axis=1)
    gain_here = (small_sum[0] + small_sum[1])[10 : 10 + folds, :inner].reshape(model)
    state_here = jnp.stack([part[:, inner : inner + HEAD0] for part in late_sum])
    gain_there, state_there = swap(gain_here), swap(state_here)
    gain_size = model // (dps * ctxs)
    gain_sum = piece(gain_here + gain_there, dp * ctxs + z, gain_size)
    in_order = jnp.where(
        core == 0, jnp.stack([state_here, state_there], 1), jnp.stack([state_there, state_here], 1)
    )
    state_sum = jnp.transpose(in_order, (2, 0, 1, 3)).reshape(-1, 2 * states)
    main_sum = jnp.stack(
        [side_by_side([part[:, :inner] for part in early_sum]), side_by_side([part[:, :inner] for part in late_sum])],
        axis=1,
    )
    delta_sum = side_by_side([part[:, inner + HEAD0 : inner + HEAD0 + heads] for part in late_sum])

    return (
        mixed[None],
        grad_hidden[None],
        gain_sum,
        main_sum,
        state_sum,
        delta_sum,
        signal_small[:4],
        state_small[:4],
        signal_small[4],
        state_small[4],
        side_by_side([part[0] for part in heads_small]),
        side_by_side([part[1] for part in heads_small]) * rate_all,
        skip_sum,
        signal_small[8],
        side_by_side([part[:, inner:] for part in early_sum]),
    )


def solution(mesh):
    in_specs = (
        P("dp", "ctx", None), P("dp"), P("dp", "ctx", None), P(), P("dp", None, "tp"), P("dp", None),
        P("dp", "tp"), P(None, "tp"), P(), P("tp"), P(), P("tp"), P("tp"), P("tp"), P("tp"), P("dp", "tp"),
    )
    out_specs = (
        P("dp", "ctx", None), P("dp", "ctx", None), P(("dp", "ctx")), P(("dp", "ctx"), None, "tp"),
        P(("dp", "ctx"), None), P(("dp", "ctx"), "tp"), P(None, "tp"), P(), P("tp"), P(), P("tp"), P("tp"),
        P("tp"), P("tp"), P(("dp", "ctx"), "tp"),
    )
    return jax.shard_map(
        per_device, mesh=mesh, in_specs=in_specs, out_specs=out_specs, check_vma=False
    )
```

```python
import functools

import jax
import jax.numpy as jnp
from jax import lax
from jax.experimental import pallas as pl
from jax.experimental.pallas import tpu as pltpu
from jax.sharding import PartitionSpec as P

BLOCK = 256
SUB = 128
EPSILON = 1e-05
HIGH = lax.Precision.HIGH
HIGHEST = lax.Precision.HIGHEST
F32 = jnp.float32
BF16 = jnp.bfloat16
F16 = jnp.float16
NN = (((1,), (0,)), ((), ()))
NT = (((1,), (1,)), ((), ()))
TN = (((0,), (0,)), ((), ()))
HEAD0 = 64
LO, CORE, BASE, LENGTH, HASPREV, HASNEXT, SLOT0 = range(7)


def mm(a, b, dims=NN, precision=None):
    return lax.dot_general(a, b, dims, precision=precision, preferred_element_type=F32)


def grid_call(body, grid, in_specs, out_specs, out_shape, scratch=(), name=None, limit=None):
    return pl.pallas_call(
        body,
        grid_spec=pltpu.PrefetchScalarGridSpec(
            num_scalar_prefetch=1,
            grid=grid,
            in_specs=in_specs,
            out_specs=out_specs,
            scratch_shapes=list(scratch),
        ),
        out_shape=out_shape,
        compiler_params=pltpu.CompilerParams(
            dimension_semantics=("arbitrary",) * len(grid), vmem_limit_bytes=limit
        ),
        name=name,
    )


def streamed(*arrays):
    return [pltpu.with_memory_space_constraint(array, pltpu.HBM) for array in arrays]


def rows_spec(width, rows=BLOCK, lane=0):
    return pl.BlockSpec((rows, width), lambda b, s: (b, lane))


def whole(shape):
    return pl.BlockSpec(shape, lambda b, s: (0,) * len(shape))


def shaped(shape, dtype=F32):
    return jax.ShapeDtypeStruct(shape, dtype)


def kept(shape, dtype=F32):
    return pltpu.HBM(shape, dtype)


def slope(v, sig):
    return sig * (1.0 + v * (1.0 - sig))


def lanes_of(s_ref, slot, width):
    return pl.ds(pl.multiple_of(s_ref[SLOT0 + slot] * width, width), width)


def normalize(x, gain):
    value = x.astype(F32)
    inverse = lax.rsqrt(jnp.mean(value * value, axis=1, keepdims=True) + EPSILON)
    scaled = value * inverse
    return scaled, (scaled * gain).astype(BF16)


def pick(s_ref, b, quarter, own, near, far):
    lo, core = s_ref[LO], s_ref[CORE]
    place = b // quarter
    mine = (place // 2) == lo
    from_near = (place % 2) == core
    return jnp.where(mine, own, jnp.where(from_near, near, far))


def valid_rows(s_ref, b):
    position = s_ref[BASE] + b * BLOCK + lax.broadcasted_iota(jnp.int32, (BLOCK, 1), 0)
    return (position < s_ref[LENGTH]).astype(F32)


def expander(inner):
    lane = lax.broadcasted_iota(jnp.int32, (384, inner), 0) % 128 - HEAD0
    head = lax.broadcasted_iota(jnp.int32, (384, inner), 1) // 64
    return (lane == head).astype(F32).astype(BF16)


def collector(inner):
    head = lax.broadcasted_iota(jnp.int32, (3 * inner, 128), 0) % inner // 64
    lane = lax.broadcasted_iota(jnp.int32, (3 * inner, 128), 1) - HEAD0
    return (lane == head).astype(F32).astype(BF16)


def two(x):
    high = x.astype(BF16)
    return high, (x - high.astype(F32)).astype(BF16)


def three(x, axis=1):
    high = x.astype(BF16)
    rest = x - high.astype(F32)
    middle = rest.astype(BF16)
    return jnp.concatenate([high, middle, (rest - middle.astype(F32)).astype(BF16)], axis=axis)


def running(tri, x):
    width = x.shape[1]
    wide = mm(tri, three(x))
    return wide[:, :width] + wide[:, width : 2 * width] + wide[:, 2 * width :]


def triangle(forward):
    row = lax.broadcasted_iota(jnp.int32, (BLOCK, BLOCK), 0)
    col = lax.broadcasted_iota(jnp.int32, (BLOCK, BLOCK), 1)
    same = (row // SUB) == (col // SUB)
    keep = (row >= col) if forward else (col >= row)
    return (same & keep).astype(F32).astype(BF16)


def stacked_heads(x):
    half = lax.broadcasted_iota(jnp.int32, (1, 128), 1) < 64
    return two(jnp.concatenate([jnp.where(half, x, 0.0), jnp.where(half, 0.0, x)], axis=0))


def faded(keep, level, level_t, level_x, pair, forward):
    out = []
    for side in range(2):
        h = HEAD0 + 2 * pair + side
        at = pair * 128 + side * 64
        column, row = level_x[:, at : at + 1], level_t[h : h + 1, :]
        diff = column - row if forward else row - column
        out.append(jnp.exp(jnp.where(keep, diff, -1e30)))
    return jnp.concatenate(out, axis=1)


def mixed_heads(mix, high, low):
    mh, ml = two(mix)
    wide = mm(mh, jnp.concatenate([high, low], axis=1))
    return wide[:, :128] + wide[:, 128:] + mm(ml, high)


def head_lanes(inner):
    lane = lax.broadcasted_iota(jnp.int32, (1, 128), 1)
    return (lane >= HEAD0) & (lane < HEAD0 + inner // 64)


def front_body(parts, inner, states, quarter, s_ref, own, near, far, halo, gain, taps, bias, dbias, rate,
               *rest):
    ws = rest[:parts]
    (normed_ref, u_ref, uh_ref, co_ref, draw_ref, delta_ref, lev_ref, lx_ref, dx_ref, hloc_ref,
     pre_ref, end_ref) = rest[parts : parts + 12]
    hsc, usc, state, pre, esc = rest[parts + 12 :]
    b = pl.program_id(0)
    wide = inner + 2 * states
    shard = ws[0].shape[0]
    normed_ref[...] = normalize(pick(s_ref, b, quarter, own[...], near[...], far[...]), gain[...])[1]

    @pl.when(b == 0)
    def _():
        hsc[...] = normalize(halo[...], gain[...])[1]
        edge = jnp.zeros((16, wide), F32)
        for j in range(parts):
            edge += mm(hsc[:, lanes_of(s_ref, j, shard)], ws[j][:, :wide])
        edge = jnp.where(s_ref[HASPREV] > 0, edge[8:], 0.0)
        usc[0:8] = edge
        uh_ref[...] = edge
        state[...] = jnp.zeros_like(state)
        pre[...] = jnp.zeros_like(pre)
        esc[...] = expander(inner)

    @pl.when(b > 0)
    def _():
        usc[0:8] = usc[BLOCK : BLOCK + 8]

    u = jnp.zeros((BLOCK, wide + 128), F32)
    for j in range(parts):
        u += mm(normed_ref[:, lanes_of(s_ref, j, shard)], ws[j][...])
    usc[8 : 8 + BLOCK] = u[:, :wide]
    u_ref[...] = u[:, :wide]
    conv = bias[...] + taps[0:1] * usc[5 : 5 + BLOCK]
    for k in range(1, 4):
        conv = conv + taps[k : k + 1] * usc[5 + k : 5 + k + BLOCK]
    co_ref[...] = conv
    raw = u[:, wide:] + dbias[...]
    draw_ref[...] = raw
    delta = jnp.where(head_lanes(inner), jnp.maximum(raw, 0.0) + jnp.log1p(jnp.exp(-jnp.abs(raw))), 0.0)
    delta = delta * valid_rows(s_ref, b)
    delta_ref[...] = delta
    level = running(triangle(True), delta * rate[...])
    lev_ref[...] = level
    both = mm(jnp.concatenate([three(level), three(delta)], axis=0), esc[...])
    level_x, delta_x = both[:BLOCK], both[BLOCK:]
    lx_ref[...] = level_x
    dx_ref[...] = delta_x
    act = conv * jax.nn.sigmoid(conv)
    source = delta_x * act[:, :inner]
    inject_t = act[:, inner : inner + states].T
    for i in range(BLOCK // SUB):
        at = slice(i * SUB, (i + 1) * SUB)
        last = level_x[(i + 1) * SUB - 1 : (i + 1) * SUB]
        fresh = mm(inject_t[:, at], jnp.exp(last - level_x[at]) * source[at], precision=HIGH)
        before = state[...]
        n = b * (BLOCK // SUB) + i
        hloc_ref[n] = before
        pre_ref[n] = pre[...]
        state[...] = jnp.exp(last) * before + fresh
        pre[...] = pre[...] + last

    @pl.when(b == pl.num_programs(0) - 1)
    def _():
        hloc_ref[n + 1] = state[...]
        end_ref[...] = state[...]
        pre_ref[n + 1] = pre[...]


def within_body(inner, states, s_ref, co, lev, lx, dx, yw_ref):
    conv = co[...]
    act = conv * jax.nn.sigmoid(conv)
    xs = dx[...] * act[:, :inner]
    level = lev[...]
    keep = lax.broadcasted_iota(jnp.int32, (SUB, SUB), 0) >= lax.broadcasted_iota(jnp.int32, (SUB, SUB), 1)
    for i in range(BLOCK // SUB):
        at = slice(i * SUB, (i + 1) * SUB)
        affinity = mm(act[at, inner + states :], act[at, inner : inner + states], NT, HIGH)
        affinity = jnp.concatenate([affinity, affinity], axis=1)
        level_t = level[at].T
        level_x = lx[at]
        for pair in range(inner // 128):
            lanes = slice(pair * 128, pair * 128 + 128)
            mix = faded(keep, level, level_t, level_x, pair, True) * affinity
            yw_ref[at, lanes] = mixed_heads(mix, *stacked_heads(xs[at, lanes]))


def gates_body(parts, quarter, s_ref, normed, own, near, far, *rest):
    ws = rest[:parts]
    gate_ref, gg_ref, bg_ref = rest[parts:]
    b = pl.program_id(0)
    shard = ws[0].shape[0]
    inner = gate_ref.shape[1]
    up = pick(s_ref, b, quarter, own[...], near[...], far[...])
    bg_ref[...] = (up.astype(F32) * valid_rows(s_ref, b)).astype(BF16)
    gate = jnp.zeros(gate_ref.shape, F32)
    gg = jnp.zeros(gg_ref.shape, F32)
    for j in range(parts):
        at = lanes_of(s_ref, j, shard)
        gate += mm(normed[:, at], ws[j][:, :inner])
        gg += mm(bg_ref[:, at], ws[j][:, inner:])
    gate_ref[...] = gate
    gg_ref[...] = gg


def entering(hloc, pre, hin):
    return hloc + jnp.exp(pre[0:1]) * hin


def output_body(inner, states, s_ref, co, lx, yw, gate, gg, hloc, pre, hin, skip, ggain, y_ref, sum_ref):
    conv = co[...]
    act = conv * jax.nn.sigmoid(conv)
    for i in range(BLOCK // SUB):
        at = slice(i * SUB, (i + 1) * SUB)
        held = entering(hloc[i], pre[i], hin[...])
        y_ref[at] = yw[at] + jnp.exp(lx[at]) * mm(act[at, inner + states :], held, precision=HIGH)
    out = y_ref[...] + skip[...] * act[:, :inner]
    g = gate[...]
    product = out * (g * jax.nn.sigmoid(g))
    ones = jnp.ones((8, 3 * inner), BF16)
    sum_ref[0:8] = mm(ones, three(product * product), NT)
    sum_ref[8:16] = mm(ones, three(gg[...] * ggain[...] * product), NT)


def turn_body(inner, states, total, s_ref, co, lx, y, gate, gg, sums, sums1, sums2, sums3, skip, ggain,
              gated_ref, ggrad_ref, og_ref, gloc_ref, start_ref, cols_ref, chain):
    step = pl.program_id(0)
    conv = co[...]
    act = conv * jax.nn.sigmoid(conv)
    x = act[:, :inner]
    readout_t = act[:, inner + states :].T
    both = (sums[...] + sums1[...] + sums2[...] + sums3[...]).T
    ginv = lax.rsqrt(both[:, 0:1] / total + EPSILON)
    dot = ginv * both[:, 8:9] / total
    g = gate[...]
    sig = jax.nn.sigmoid(g)
    ga = g * sig
    out = y[...] + skip[...] * x
    unit = out * ga * ginv
    gated_ref[...] = (unit * ggain[...]).astype(BF16)
    grad = gg[...]
    pg = ginv * (grad * ggain[...] - unit * dot)
    og = pg * ga
    og_ref[...] = og
    ggrad_ref[...] = (pg * out * slope(g, sig)).astype(BF16)

    @pl.when(step == 0)
    def _():
        chain[...] = jnp.zeros_like(chain)
        cols_ref[...] = jnp.zeros_like(cols_ref)

    cols_ref[0:1] += jnp.sum(grad * unit, axis=0, keepdims=True)
    cols_ref[1:2] += jnp.sum(og * x, axis=0, keepdims=True)
    b = pl.num_programs(0) - 1 - step
    for i in reversed(range(BLOCK // SUB)):
        at = slice(i * SUB, (i + 1) * SUB)
        held = chain[...]
        n = b * (BLOCK // SUB) + i
        gloc_ref[n + 1] = held
        level_x = lx[at]
        chain[...] = jnp.exp(level_x[SUB - 1 : SUB]) * held + mm(
            readout_t[:, at], jnp.exp(level_x) * og[at], precision=HIGH
        )

    @pl.when(b == 0)
    def _():
        gloc_ref[0] = chain[...]
        start_ref[...] = chain[...]


def back_body(inner, states, s_ref, co, lev, lx, dx, og, hloc, pre, hin, z_ref, dbc_ref):
    conv = co[...]
    act = conv * jax.nn.sigmoid(conv)
    xs = dx[...] * act[:, :inner]
    level = lev[...]
    keep = lax.broadcasted_iota(jnp.int32, (SUB, SUB), 1) >= lax.broadcasted_iota(jnp.int32, (SUB, SUB), 0)
    for i in range(BLOCK // SUB):
        at = slice(i * SUB, (i + 1) * SUB)
        inject, readout = act[at, inner : inner + states], act[at, inner + states :]
        affinity = mm(inject, readout, NT, HIGH)
        affinity = jnp.concatenate([affinity, affinity], axis=1)
        level_t = level[at].T
        level_x = lx[at]
        grad = jnp.zeros((SUB, SUB), F32)
        for pair in range(inner // 128):
            lanes = slice(pair * 128, pair * 128 + 128)
            fade = faded(keep, level, level_t, level_x, pair, False)
            g = og[at, lanes]
            z_ref[at, lanes] = mixed_heads(fade * affinity, *stacked_heads(g))
            xh, xl = stacked_heads(xs[at, lanes])
            gh, gl = two(g)
            outer = mm(
                jnp.concatenate([xh, xl], axis=1), jnp.concatenate([gh, gh], axis=1), NT
            ) + mm(xh, gl, NT)
            grad += fade[:, :SUB] * outer[:SUB] + fade[:, SUB:] * outer[SUB:]
        held = entering(hloc[i], pre[i], hin[...])
        dbc_ref[at, :states] = mm(grad, readout, precision=HIGH)
        dbc_ref[at, states:] = mm(grad.T, inject, precision=HIGH) + mm(
            jnp.exp(level_x) * og[at], held, NT, HIGH
        )


def conv_back(grad, csc, usc, taps, cols_ref):
    csc[0:BLOCK] = grad
    pre = taps[0:1] * csc[3 : 3 + BLOCK]
    for k in range(1, 4):
        pre = pre + taps[k : k + 1] * csc[3 - k : 3 - k + BLOCK]
    for k in range(4):
        cols_ref[k : k + 1] += jnp.sum(grad * usc[5 + k : 5 + k + BLOCK], axis=0, keepdims=True)
    cols_ref[4:5] += jnp.sum(grad, axis=0, keepdims=True)
    csc[BLOCK : BLOCK + 8] = grad[0:8]
    return pre


def meet_body(inner, states, s_ref, co, lx, dx, z, dbc, hloc, pre, gloc, gin, hin, zed_ref, ends_ref, keep_ref,
              give_ref):
    subs = BLOCK // SUB
    count = pl.num_programs(0)
    b = pl.program_id(0)
    conv = co[...]
    act = conv * jax.nn.sigmoid(conv)
    source = dx[...] * act[:, :inner]
    ends = []
    inject_grads = []
    for i in range(subs):
        at = slice(i * SUB, (i + 1) * SUB)
        n = b * subs + i + 1
        level_x = lx[at]
        later = gloc[n] + jnp.exp(pre[subs * count][0:1] - pre[n][0:1]) * gin[...]
        fade = jnp.exp(level_x[SUB - 1 : SUB] - level_x)
        zed_ref[at] = z[at] + fade * mm(act[at, inner : inner + states], later, precision=HIGH)
        inject_grads.append(dbc[at, :states] + mm(fade * source[at], later, NT, HIGH))
        ends.append(jnp.sum(later * entering(hloc[n], pre[n], hin[...]), axis=0, keepdims=True))
    ends_ref[...] = jnp.concatenate(ends + [jnp.zeros((8 - subs, inner), F32)], axis=0)
    inject_grad = jnp.concatenate(inject_grads, axis=0)
    half = count // 2
    rows = pl.ds(pl.multiple_of((b % half) * BLOCK, BLOCK), BLOCK)

    @pl.when(b // half == s_ref[CORE])
    def _():
        keep_ref[rows, :states] = inject_grad
        keep_ref[rows, states:] = dbc[:, states:]

    @pl.when(b // half != s_ref[CORE])
    def _():
        give_ref[rows, :states] = inject_grad
        give_ref[rows, states:] = dbc[:, states:]


def join_body(inner, s_ref, co, delta, dx, draw, og, y, zed_in, ends_in, u, prior, uh, taps, rate, skip, mg_ref,
              tail_ref, head_ref, rg_ref, cols_ref, sig_ref, col_sc, csc, usc):
    step = pl.program_id(0)
    subs = BLOCK // SUB
    count = pl.num_programs(0)
    b = count - 1 - step

    @pl.when(step == 0)
    def _():
        cols_ref[...] = jnp.zeros_like(cols_ref)
        sig_ref[...] = jnp.zeros_like(sig_ref)
        col_sc[...] = collector(inner)
        csc[BLOCK : BLOCK + 8] = jnp.zeros((8, inner), F32)

    conv = co[...]
    sig = jax.nn.sigmoid(conv)
    x = conv * sig
    delta_x = dx[...]
    zed = zed_in[...]
    ends = ends_in[...]
    g = og[...]
    sums = mm(three(jnp.concatenate([x * zed, g * y[...], ends], axis=0)), col_sc[...])
    direct, read, ends = sums[:BLOCK], sums[BLOCK : 2 * BLOCK], sums[2 * BLOCK :]
    dlt = delta[...]
    q = running(triangle(False), read - dlt * direct)
    q = jnp.concatenate([q[i * SUB : (i + 1) * SUB] + ends[i : i + 1] for i in range(subs)], axis=0)
    rg = (direct + rate[...] * q) * valid_rows(s_ref, b) * jax.nn.sigmoid(draw[...])
    rg = jnp.where(head_lanes(inner), rg, 0.0)
    rg_ref[...] = rg
    cols_ref[0:1] += jnp.sum(rg, axis=0, keepdims=True)
    cols_ref[1:2] += jnp.sum(dlt * q, axis=0, keepdims=True)

    usc[0:8] = jnp.where(b == 0, uh[...], prior[...])
    usc[8 : 8 + BLOCK] = u[...]
    grad = (delta_x * zed + skip[...] * g) * slope(conv, sig)
    pre_grad = conv_back(grad, csc, usc, taps, sig_ref)
    mg_ref[...] = pre_grad.astype(BF16)
    head_ref[...] = grad[0:8]

    @pl.when(step == 0)
    def _():
        tail_ref[...] = pre_grad[BLOCK - 8 :]


def exponents(peak):
    return jnp.clip(jnp.ceil(jnp.log(jnp.maximum(peak, 1e-36)) * 1.4426950408889634) - 14.0, -100.0, 100.0)


def packed(value, power, inverse, riders=()):
    rows = [(value * inverse).astype(F16), jnp.broadcast_to(power, (16, value.shape[1])).astype(F16)]
    for more in riders:
        each = exponents(jnp.abs(more))
        rows += [(more * jnp.exp2(-each)).astype(F16), each.astype(F16)]
    return jnp.concatenate(rows)


def unpacked(sent, counts=()):
    rows = sent.shape[0] - 16 - 2 * sum(counts)
    power = sent[rows : rows + 1].astype(F32)
    more = []
    at = rows + 16
    for size in counts:
        more.append(sent[at : at + size].astype(F32) * jnp.exp2(sent[at + size : at + 2 * size].astype(F32)))
        at += 2 * size
    return sent[:rows].astype(F32) * jnp.exp2(power), power, more


def grads_body(parts, pairs, s_ref, *refs):
    inputs = 1 + max(max(pair) for pair in pairs)
    outs, scale, peak = refs[inputs : inputs + parts], refs[inputs + parts], refs[inputs + parts + 1]
    j = pl.program_id(0)

    @pl.when(j == 0)
    def _():
        peak[...] = jnp.zeros_like(peak)

    at = 0
    for left, right in pairs:
        value = mm(refs[left][...], refs[right][...], TN)
        lanes = slice(at, at + value.shape[1])
        at += value.shape[1]
        peak[0:1, lanes] = jnp.maximum(peak[0:1, lanes], jnp.max(jnp.abs(value), axis=0, keepdims=True))
        for k in range(parts):

            @pl.when(j == k)
            def _():
                outs[k][:, lanes] = value

    @pl.when(j == parts - 1)
    def _():
        power = exponents(peak[...])
        scale[0:8] = jnp.broadcast_to(power[0:1], (8, at))
        scale[8:16] = jnp.broadcast_to(jnp.exp2(-power[0:1]), (8, at))


def deal(s_ref, b, quarter, value, outs):
    place = b // quarter
    rows = pl.ds(pl.multiple_of((b % quarter) * BLOCK, BLOCK), BLOCK)
    at = (place % 2 != s_ref[CORE]).astype(jnp.int32) * 2 + (place // 2 != s_ref[LO]).astype(jnp.int32)
    for k in range(4):

        @pl.when(at == k)
        def _():
            outs[k][rows] = value


def feature_body(parts, quarter, s_ref, own, near, far, ggrad, mg, rg, dbc, dbc_other, co, u, prior, uh, ahead,
                 taps, *rest):
    ws1 = rest[:parts]
    ws2 = rest[parts : 2 * parts]
    outs = rest[2 * parts : 2 * parts + 4]
    xg_ref, cols_ref, state_ref, whole_sc, csc, usc = rest[2 * parts + 4 :]
    step = pl.program_id(0)
    count = pl.num_programs(0)
    b = count - 1 - step
    inner = ggrad.shape[1]
    shard = ws1[0].shape[0]

    @pl.when(step == 0)
    def _():
        cols_ref[...] = jnp.zeros_like(cols_ref)
        state_ref[...] = jnp.zeros_like(state_ref)
        csc[BLOCK : BLOCK + 8] = jnp.where(s_ref[HASNEXT] > 0, ahead[...], 0.0)

    usc[0:8] = jnp.where(b == 0, uh[...], prior[...])
    usc[8 : 8 + BLOCK] = u[...]
    conv = co[...]
    grad = jnp.where(b // (count // 2) == s_ref[CORE], dbc[...], dbc_other[...])
    grad = grad * slope(conv, jax.nn.sigmoid(conv))
    pre = conv_back(grad, csc, usc, taps, state_ref)
    pre = jnp.where(s_ref[CORE] > 0, pltpu.roll(pre, 64, 1), pre)
    lane = lax.broadcasted_iota(jnp.int32, (BLOCK, 128), 1)
    xg = jnp.where(lane < HEAD0, pre, rg[...]).astype(BF16)
    xg_ref[...] = xg
    for j in range(parts):
        at = lanes_of(s_ref, j, shard)
        whole_sc[:, at] = (
            mm(ggrad[...], ws2[j][:, :inner], NT)
            + mm(mg[...], ws1[j][:, :inner], NT)
            + mm(xg, ws1[j][:, -128:], NT)
        )
    value = whole_sc[...]
    scaled = normalize(pick(s_ref, b, quarter, own[...], near[...], far[...]), 1.0)[0]
    cols_ref[0:1] += jnp.sum(value * scaled, axis=0, keepdims=True)
    deal(s_ref, b, quarter, value, outs)


def branch_body(parts, quarter, s_ref, gated, *rest):
    ws2 = rest[:parts]
    outs = rest[parts : parts + 4]
    whole_sc = rest[parts + 4]
    inner = gated.shape[1]
    shard = ws2[0].shape[0]
    for j in range(parts):
        whole_sc[:, lanes_of(s_ref, j, shard)] = mm(gated[...], ws2[j][:, inner:], NT)
    deal(s_ref, pl.program_id(0), quarter, whole_sc[...], outs)


def per_device(
    hidden, lengths, cotangent, norm_gain, proj_main, proj_state, proj_delta, conv_main, conv_state,
    bias_main, bias_state, delta_bias, log_rate, skip_gain, gate_gain, proj_out,
):
    _, steps, model = hidden.shape
    hidden, cotangent = hidden[0], cotangent[0]
    dps, ctxs, tps = lax.axis_size("dp"), lax.axis_size("ctx"), lax.axis_size("tp")
    dp, z, core = lax.axis_index("dp"), lax.axis_index("ctx"), lax.axis_index("tp")
    lo, hi = z % 2, z // 2
    pairs = ctxs // 2
    tokens = 2 * steps
    count = tokens // BLOCK
    quarter = count // 4
    inner = bias_main.shape[0] // 2
    heads = delta_bias.shape[0] // 2
    states = bias_state.shape[0] // 2
    wide = inner + 2 * states

    def swap(value):
        return lax.ppermute(value, "tp", [(0, 1), (1, 0)])

    def across(value, j):
        return lax.ppermute(value, "ctx", [(i, i ^ j) for i in range(ctxs)])

    def along(value, step):
        return lax.ppermute(
            value, "ctx", [(i, i + step) for i in range(ctxs) if 0 <= i + step < ctxs]
        )

    def spread(value, j):
        return lax.ppermute(value, "dp", [(i, i ^ j) for i in range(dps)])

    def mine(value, axis, size):
        return lax.dynamic_slice_in_dim(value, lo * size, size, axis)

    def piece(value, at, size):
        return lax.dynamic_slice_in_dim(value, at * size, size, 0)

    apart = proj_main.shape[0] % 128 == 0
    parts = dps if apart else 1
    shard = proj_main.shape[0] * (dps // parts)

    def gathered(value):
        if not apart:
            return [lax.all_gather(value, "dp", axis=0, tiled=True)]
        return [value] + [spread(value, j) for j in range(1, dps)]

    scalars = jnp.stack(
        [lo, core, hi * tokens, lengths[0], (hi > 0).astype(jnp.int32), (hi < pairs - 1).astype(jnp.int32)]
        + [dp ^ j if apart else 0 * dp for j in range(parts)]
    ).astype(jnp.int32)

    state_own = lax.dynamic_slice_in_dim(proj_state, lo * states + core * (states // 2), states // 2, 1)
    delta_own = mine(proj_delta, 1, heads)
    main_part = mine(proj_main, 2, inner)
    first = jnp.concatenate(
        [main_part[:, 1], proj_state, state_own, delta_own,
         jnp.zeros((proj_main.shape[0], 64 - heads), BF16)], axis=1
    )
    halfway = steps // 2
    near = across(piece(hidden, core, halfway), 1)
    far = swap(near)
    ws1 = gathered(first)

    def over_sequences(pieces, scale, riders=()):
        return [spread(packed(pieces[j], scale[0:1], scale[8:9], riders), j) for j in range(1, parts)]

    def chunks(pieces, scale, got, riders=()):
        total, power = pieces[0], scale[0:1]
        if not apart:
            total = lax.psum_scatter(total, "dp", scatter_dimension=0, tiled=True)
            power = exponents(jnp.max(jnp.abs(total), axis=0, keepdims=True))
            riders = [lax.psum(value, "dp") for value in riders]
        for sent in got:
            value, other, more = unpacked(sent, [rider.shape[0] for rider in riders])
            total, power = total + value, jnp.maximum(power, other)
            riders = [one + two for one, two in zip(riders, more)]
        power = power + (parts - 1).bit_length()
        size = total.shape[0] // ctxs
        rows = [piece(total, z ^ j, size) for j in range(ctxs)]
        return rows[:1] + [packed(value, power, jnp.exp2(-power), riders) for value in rows[1:]], riders

    def over_positions(cut):
        return [across(cut[j], j) for j in range(1, ctxs)]

    def settled(own, got):
        opposite = got[0]
        for j in range(2, ctxs):
            if j % 2 == 0:
                own = own + got[j - 1]
            else:
                opposite = opposite + got[j - 1]
        return jnp.where(lo == 0, own, opposite), jnp.where(lo == 0, opposite, own)

    def decoded(got, counts=()):
        return [unpacked(sent, counts)[0] for sent in got]

    def ridden(got, counts):
        return [unpacked(sent, counts)[2][0] for sent in got]

    taps_x = jnp.concatenate([mine(conv_main, 1, inner), conv_state], axis=1)
    bias_x = jnp.concatenate([mine(bias_main, 0, inner), bias_state])[None]
    rate_own = -jnp.exp(mine(log_rate, 0, heads))

    def in_heads(value):
        return jnp.pad(value, (HEAD0, 128 - HEAD0 - heads))[None]

    rate_row = in_heads(rate_own)
    dbias_row = in_heads(mine(delta_bias, 0, heads))
    skip_row = jnp.repeat(mine(skip_gain, 0, heads), inner // heads)[None]
    ggain_row = mine(gate_gain, 0, inner)[None]
    gain_row = norm_gain[None]
    edge, scalars, taps_x, bias_x, rate_row, dbias_row, _ = lax.optimization_barrier(
        (hidden[steps - 16 :], scalars, taps_x, bias_x, rate_row, dbias_row, first)
    )
    route = [
        ((z0 - 1) * tps + c, (z0 + c) * tps + c) for z0 in range(2, ctxs, 2) for c in range(2)
    ]
    edge = lax.ppermute(edge, ("ctx", "tp"), route)
    halo = jnp.where(core == lo, edge, swap(edge))

    ws1, near, main_gate, out_later, cot_later = lax.optimization_barrier(
        (ws1, near, main_part[:, 0], proj_out, cotangent)
    )
    second = jnp.concatenate([main_gate, mine(out_later, 1, inner)], axis=1)
    ws2 = gathered(second)
    cot_near = across(piece(cot_later, core, halfway), 1)

    own_spec = pl.BlockSpec(
        (BLOCK, model), lambda b, s: (jnp.clip(b - s[LO] * 2 * quarter, 0, 2 * quarter - 1), 0)
    )
    part_spec = pl.BlockSpec((BLOCK, model), lambda b, s: (b % quarter, 0))
    subs = BLOCK // SUB
    last = count * subs
    state_block = pl.BlockSpec((subs, states, inner), lambda b, s: (b, 0, 0))
    pre_block = pl.BlockSpec((subs, 8, inner), lambda b, s: (b, 0, 0))

    normed, u, uh, conv, draw, delta, level, level_x, delta_x, hloc, pre, own_end = grid_call(
        functools.partial(front_body, parts, inner, states, quarter),
        (count,),
        [own_spec, part_spec, part_spec, whole((16, model)), whole((1, model)), whole((4, wide)),
         whole((1, wide)), whole((1, 128)), whole((1, 128))] + [whole((shard, wide + 128))] * parts,
        [rows_spec(model), rows_spec(wide), whole((8, wide)), rows_spec(wide), rows_spec(128), rows_spec(128),
         rows_spec(128), rows_spec(inner), rows_spec(inner), whole((last + 1, states, inner)),
         whole((last + 1, 8, inner)), whole((states, inner))],
        [shaped((tokens, model), BF16), shaped((tokens, wide)), shaped((8, wide)), shaped((tokens, wide)),
         shaped((tokens, 128)), shaped((tokens, 128)), shaped((tokens, 128)), shaped((tokens, inner)),
         shaped((tokens, inner)), shaped((last + 1, states, inner)), shaped((last + 1, 8, inner)), shaped((states, inner))],
        [pltpu.VMEM((16, model), BF16), pltpu.VMEM((8 + BLOCK, wide), F32), pltpu.VMEM((states, inner), F32),
         pltpu.VMEM((8, inner), F32), pltpu.VMEM((384, inner), BF16)],
        name="front",
    )(scalars, hidden, near, far, halo, gain_row, taps_x, bias_x, dbias_row, rate_row, *ws1)

    cot_near, own_end = lax.optimization_barrier((cot_near, own_end))
    cot_far = swap(cot_near)
    growth = jnp.exp(pre[last][0:1])
    carried = jnp.zeros_like(own_end)
    sending = own_end
    for hop in range(pairs - 1):
        carried = along(sending, 2)
        if hop < pairs - 2:
            sending = own_end + growth * carried

    (inside,) = grid_call(
        functools.partial(within_body, inner, states),
        (count,),
        [rows_spec(wide), rows_spec(128), rows_spec(inner), rows_spec(inner)],
        [rows_spec(inner)],
        [shaped((tokens, inner))],
        name="within",
        limit=20 << 20,
    )(scalars, *streamed(conv, level, level_x, delta_x))

    gate, gated_grad, branch_grad = grid_call(
        functools.partial(gates_body, parts, quarter),
        (count,),
        [rows_spec(model), own_spec, part_spec, part_spec] + [whole((shard, 2 * inner))] * parts,
        [rows_spec(inner), rows_spec(inner), rows_spec(model)],
        [shaped((tokens, inner)), shaped((tokens, inner)), shaped((tokens, model), BF16)],
        name="gates",
        limit=20 << 20,
    )(scalars, *streamed(normed, cotangent, cot_near, cot_far, *ws2))

    y, sums = grid_call(
        functools.partial(output_body, inner, states),
        (count,),
        [rows_spec(wide), rows_spec(inner), rows_spec(inner), rows_spec(inner), rows_spec(inner), state_block,
         pre_block, whole((states, inner)), whole((1, inner)), whole((1, inner))],
        [rows_spec(inner), pl.BlockSpec((16, BLOCK), lambda b, s: (0, b))],
        [shaped((tokens, inner)), shaped((16, tokens))],
        name="output",
        limit=20 << 20,
    )(scalars, *streamed(conv, level_x), inside, gate, gated_grad, *streamed(hloc), pre, carried, skip_row, ggain_row)

    corner = [(n, ((n // tps) ^ 1) * tps + (n % tps + 1) % tps) for n in range(ctxs * tps)]
    all_sums = [sums, swap(sums), across(sums, 1), lax.ppermute(sums, ("ctx", "tp"), corner)]

    def back(width, rows=BLOCK):
        return pl.BlockSpec((rows, width), lambda b, s: (count - 1 - b, 0))

    back_sums = pl.BlockSpec((16, BLOCK), lambda b, s: (0, count - 1 - b))
    gated, gate_grad, out_grad, gloc, own_start, turn_cols = grid_call(
        functools.partial(turn_body, inner, states, 2 * tps * inner),
        (count,),
        [back(wide), back(inner), back(inner), back(inner), back(inner),
         back_sums, back_sums, back_sums, back_sums, whole((1, inner)), whole((1, inner))],
        [back(inner), back(inner), back(inner), whole((last + 1, states, inner)), whole((states, inner)),
         whole((8, inner))],
        [kept((tokens, inner), BF16), kept((tokens, inner), BF16), kept((tokens, inner)),
         kept((last + 1, states, inner)), shaped((states, inner)), shaped((8, inner))],
        [pltpu.VMEM((states, inner), F32)],
        name="turn",
        limit=20 << 20,
    )(scalars, *streamed(conv, level_x), y, gate, gated_grad, *all_sums, skip_row, ggain_row)

    returned = jnp.zeros_like(own_start)
    sending = own_start
    for hop in range(pairs - 1):
        returned = along(sending, -2)
        if hop < pairs - 2:
            sending = own_start + growth * returned

    turned = pl.BlockSpec((tokens, shard), lambda j, s: (0, s[SLOT0 + j]))
    dealt_specs = [whole((halfway, model))] * 4
    dealt_shapes = [shaped((halfway, model))] * 4
    def grads(lefts, rights, name):
        sources = []
        for left, right in zip(lefts, rights):
            sources += [left, right]
        width = sum(right.shape[1] for right in rights)
        specs = [turned if n % 2 == 0 else whole(source.shape) for n, source in enumerate(sources)]
        *pieces, scale = grid_call(
            functools.partial(grads_body, parts, [(n, n + 1) for n in range(0, len(sources), 2)]),
            (parts,),
            specs,
            [whole((shard, width))] * parts + [whole((16, width))],
            [shaped((shard, width))] * parts + [shaped((16, width))],
            [pltpu.VMEM((8, width), F32)],
            name=name,
        )(scalars, *sources)
        return pieces, scale

    early, early_scale = grads([normed, branch_grad], [gate_grad, gated], "grad_early")
    early_got = over_sequences(early, early_scale)
    early, out_grad = lax.optimization_barrier((early, out_grad))

    zed, dbc = grid_call(
        functools.partial(back_body, inner, states),
        (count,),
        [rows_spec(wide), rows_spec(128), rows_spec(inner), rows_spec(inner), rows_spec(inner), state_block,
         pre_block, whole((states, inner))],
        [rows_spec(inner), rows_spec(2 * states)],
        [shaped((tokens, inner)), shaped((tokens, 2 * states))],
        name="back",
    )(scalars, conv, level, level_x, delta_x, out_grad, hloc, pre, carried)

    gated_later, zed = lax.optimization_barrier((gated, zed))
    branch = grid_call(
        functools.partial(branch_body, parts, quarter),
        (count,),
        [rows_spec(inner)] + [whole((shard, 2 * inner))] * parts,
        dealt_specs,
        dealt_shapes,
        [pltpu.VMEM((BLOCK, model), F32)],
        name="branch",
    )(scalars, gated_later, *ws2)

    returned, early_got, branch = lax.optimization_barrier((returned, early_got, branch))
    front_rows = halfway // 2
    branch_give = swap(branch[3])
    branch_theirs = [branch[1][:front_rows] + branch_give[:front_rows], branch[1][front_rows:] + branch_give[front_rows:]]
    returned, branch_theirs = lax.optimization_barrier((returned, branch_theirs))
    branch_back = [across(branch_theirs[0], 1)]
    all_states = whole((last + 1, states, inner))
    all_pre = whole((last + 1, 8, inner))
    per = BLOCK // 8
    half_rows = tokens // 2

    def back_lanes(width, lanes):
        return [
            pl.BlockSpec((BLOCK, width), lambda b, s: (count - 1 - b, lanes(s))),
            pl.BlockSpec((8, width), lambda b, s: (jnp.maximum((count - 1 - b) * per - 1, 0), lanes(s))),
            pl.BlockSpec((8, width), lambda b, s: (0, lanes(s))),
        ]

    def table(rows, width, lanes):
        return pl.BlockSpec((rows, width), lambda b, s: (0, lanes(s)))

    zed, ends, dbc_keep, dbc_give = grid_call(
        functools.partial(meet_body, inner, states),
        (count,),
        [rows_spec(wide), rows_spec(inner), rows_spec(inner), rows_spec(inner), rows_spec(2 * states), all_states,
         all_pre, all_states, whole((states, inner)), whole((states, inner))],
        [rows_spec(inner), rows_spec(inner, 8), whole((half_rows, 2 * states)), whole((half_rows, 2 * states))],
        [shaped((tokens, inner)), shaped((8 * count, inner)), shaped((half_rows, 2 * states)),
         shaped((half_rows, 2 * states))],
        name="meet",
        limit=20 << 20,
    )(scalars, *streamed(conv, level_x, delta_x, zed, dbc, hloc, pre, gloc), returned, carried)

    zed, ends, dbc_keep, dbc_give, branch_back = lax.optimization_barrier((zed, ends, dbc_keep, dbc_give, branch_back))
    early_cut, _ = chunks(early, early_scale, early_got)
    early_far = over_positions(early_cut)
    signal_pre, tail, head, raw_grad, head_cols, signal_cols = grid_call(
        functools.partial(join_body, inner),
        (count,),
        [back(inner), back(128), back(inner), back(128), back(inner), back(inner), back(inner), back(inner, 8)]
        + back_lanes(inner, lambda s: 0)
        + [table(4, inner, lambda s: 0), whole((1, 128)), whole((1, inner))],
        [back(inner), whole((8, inner)), whole((8, inner)), back(128), whole((8, 128)), whole((8, inner))],
        [shaped((tokens, inner), BF16), shaped((8, inner)), shaped((8, inner)), shaped((tokens, 128)),
         shaped((8, 128)), shaped((8, inner))],
        [pltpu.VMEM((3 * inner, 128), BF16), pltpu.VMEM((BLOCK + 8, inner), F32),
         pltpu.VMEM((BLOCK + 8, inner), F32)],
        name="join",
        limit=20 << 20,
    )(scalars, *streamed(conv, delta, delta_x, draw, out_grad, y), zed, ends, *streamed(u, u), uh, taps_x, rate_row, skip_row)

    head, early_far = lax.optimization_barrier((head, early_far))

    ahead = jnp.where(hi < pairs - 1, along(head, -2), 0.0)
    for k in range(3):
        tail = tail + taps_x[k, :inner] * jnp.concatenate([jnp.zeros((5 + k, inner), F32), ahead[: 3 - k]])
    signal_pre = lax.dynamic_update_slice_in_dim(signal_pre, tail.astype(BF16), tokens - 8, 0)

    signal_small = jnp.concatenate([signal_cols, turn_cols])
    signal, signal_scale = grads([normed], [signal_pre], "grad_signal")
    signal_got = over_sequences(signal, signal_scale, [signal_small])

    dbc = dbc_keep + swap(dbc_give)
    dbc_back = across(lax.dynamic_slice_in_dim(dbc, (1 - lo) * states, states, 1), 1)
    branch_later, dbc_back = lax.optimization_barrier((branch_theirs[1], dbc_back))
    dbc = mine(dbc, 1, states) + dbc_back
    dbc_other = swap(dbc)
    head_rows = jnp.where(core == 0, dbc[:8], dbc_other[:8])
    head_conv = lax.dynamic_slice(conv, (0, inner + lo * states), (8, states))
    state_ahead = along(head_rows * slope(head_conv, jax.nn.sigmoid(head_conv)), -2)
    def back_own(b, s):
        return jnp.clip(count - 1 - b - s[LO] * 2 * quarter, 0, 2 * quarter - 1), 0

    def state_lanes(s):
        return inner // states + s[LO]

    back_part = pl.BlockSpec((BLOCK, model), lambda b, s: ((count - 1 - b) % quarter, 0))
    back_half = pl.BlockSpec((BLOCK, states), lambda b, s: ((count - 1 - b) % (count // 2), 0))
    state_side = back_lanes(states, state_lanes)
    *feature, extra_pre, feature_cols, state_cols = grid_call(
        functools.partial(feature_body, parts, quarter),
        (count,),
        [pl.BlockSpec((BLOCK, model), back_own), back_part, back_part, back(inner), back(inner), back(128),
         back_half, back_half, state_side[0]] + state_side
        + [whole((8, states)), table(4, states, state_lanes)]
        + [whole((shard, wide + 128))] * parts + [whole((shard, 2 * inner))] * parts,
        dealt_specs + [back(128), whole((8, model)), whole((8, states))],
        dealt_shapes + [shaped((tokens, 128), BF16), shaped((8, model)), shaped((8, states))],
        [pltpu.VMEM((BLOCK, model), F32), pltpu.VMEM((BLOCK + 8, states), F32),
         pltpu.VMEM((BLOCK + 8, states), F32)],
        name="feature",
    )(scalars, hidden, near, far, gate_grad, signal_pre, raw_grad, dbc, dbc_other, conv, u, u, uh, state_ahead,
      taps_x, *ws1, *ws2)
    feature, branch_rest, signal_got = lax.optimization_barrier((feature, across(branch_later, 1), signal_got))
    branch_back = jnp.concatenate(branch_back + [branch_rest])
    feature_theirs = feature[1] + swap(feature[3])
    feature_mine = feature[0] + swap(feature[2])

    folds = model // 128
    extra_small = jnp.concatenate(
        [state_cols, head_cols, feature_cols[0].reshape(folds, 128), jnp.zeros((16 - folds % 16, 128), F32)]
    )
    extra, extra_scale = grads([normed], [extra_pre], "grad_extra")
    extra, feature_theirs = lax.optimization_barrier((extra, feature_theirs))
    feature_power = exponents(jnp.max(jnp.abs(feature_theirs), axis=0, keepdims=True))
    feature_back = across(packed(feature_theirs, feature_power, jnp.exp2(-feature_power)), 1)
    extra_got = over_sequences(extra, extra_scale, [extra_small])
    extra_got, feature_back = lax.optimization_barrier((extra_got, feature_back))
    signal_got, extra_got = lax.optimization_barrier((signal_got, extra_got))
    signal_cut, (signal_here,) = chunks(signal, signal_scale, signal_got, [signal_small])
    signal_far = over_positions(signal_cut)
    extra_cut, (extra_here,) = chunks(extra, extra_scale, extra_got, [extra_small])
    extra_far = over_positions(extra_cut)
    early_sum = settled(early_cut[0], decoded(early_far))
    signal_sum = settled(signal_cut[0], decoded(signal_far, [16]))
    signal_small = settled(signal_here, ridden(signal_far, [16]))
    extra_rows = extra_small.shape[0]
    extra_sum = settled(extra_cut[0], decoded(extra_far, [extra_rows]))
    extra_small = settled(extra_here, ridden(extra_far, [extra_rows]))
    feature_back = unpacked(feature_back)[0]

    def both_halves(value):
        other = swap(value)
        return jnp.where(core == 0, jnp.concatenate([value, other]), jnp.concatenate([other, value]))

    residual = piece(hidden, core, halfway).astype(F32)
    place = z * steps + core * halfway + lax.broadcasted_iota(jnp.int32, (halfway, 1), 0)
    valid = (place < lengths[0]).astype(F32)
    mixed = both_halves((residual + valid * (branch[0] + swap(branch[2]) + branch_back)).astype(BF16))

    feature_grad = feature_mine + feature_back
    inverse = lax.rsqrt(jnp.mean(residual * residual, axis=1, keepdims=True) + EPSILON)
    scaled_own = residual * inverse
    scaled_grad = feature_grad * norm_gain
    upstream = piece(cotangent, core, halfway).astype(F32)
    grad_hidden = both_halves(
        upstream + inverse * (scaled_grad - scaled_own * jnp.mean(scaled_grad * scaled_own, axis=1, keepdims=True))
    )

    def side_by_side(pair):
        return jnp.concatenate(pair, axis=-1)

    signal_small = side_by_side(signal_small)
    state_small = side_by_side([part[:8] for part in extra_small])
    heads_small = [part[8:10, HEAD0 : HEAD0 + heads] for part in extra_small]
    rate_all = -jnp.exp(log_rate)
    skip_sum = signal_small[9].reshape(2 * heads, inner // heads).sum(axis=1)
    gain_here = (extra_small[0] + extra_small[1])[16 : 16 + folds].reshape(model)
    state_here = jnp.stack([part[:, :HEAD0] for part in extra_sum])
    gain_there, state_there = swap(gain_here), swap(state_here)
    gain_size = model // (dps * ctxs)
    gain_sum = piece(gain_here + gain_there, dp * ctxs + z, gain_size)
    in_order = jnp.where(
        core == 0, jnp.stack([state_here, state_there], 1), jnp.stack([state_there, state_here], 1)
    )
    state_sum = jnp.transpose(in_order, (2, 0, 1, 3)).reshape(-1, 2 * states)
    main_sum = jnp.stack([side_by_side([part[:, :inner] for part in early_sum]), side_by_side(signal_sum)], axis=1)
    delta_sum = side_by_side([part[:, HEAD0 : HEAD0 + heads] for part in extra_sum])

    return (
        mixed[None],
        grad_hidden[None],
        gain_sum,
        main_sum,
        state_sum,
        delta_sum,
        signal_small[:4],
        state_small[:4],
        signal_small[4],
        state_small[4],
        side_by_side([part[0] for part in heads_small]),
        side_by_side([part[1] for part in heads_small]) * rate_all,
        skip_sum,
        signal_small[8],
        side_by_side([part[:, inner:] for part in early_sum]),
    )


def solution(mesh):
    in_specs = (
        P("dp", "ctx", None), P("dp"), P("dp", "ctx", None), P(), P("dp", None, "tp"), P("dp", None),
        P("dp", "tp"), P(None, "tp"), P(), P("tp"), P(), P("tp"), P("tp"), P("tp"), P("tp"), P("dp", "tp"),
    )
    out_specs = (
        P("dp", "ctx", None), P("dp", "ctx", None), P(("dp", "ctx")), P(("dp", "ctx"), None, "tp"),
        P(("dp", "ctx"), None), P(("dp", "ctx"), "tp"), P(None, "tp"), P(), P("tp"), P(), P("tp"), P("tp"),
        P("tp"), P("tp"), P(("dp", "ctx"), "tp"),
    )
    return jax.shard_map(
        per_device, mesh=mesh, in_specs=in_specs, out_specs=out_specs, check_vma=False
    )
```

```python
import functools

import jax
import jax.numpy as jnp
from jax import lax
from jax.experimental import pallas as pl
from jax.experimental.pallas import tpu as pltpu
from jax.sharding import PartitionSpec as P

BLOCK = 256
SUB = 128
EPSILON = 1e-05
HIGH = lax.Precision.HIGH
HIGHEST = lax.Precision.HIGHEST
F32 = jnp.float32
BF16 = jnp.bfloat16
F16 = jnp.float16
NN = (((1,), (0,)), ((), ()))
NT = (((1,), (1,)), ((), ()))
TN = (((0,), (0,)), ((), ()))
HEAD0 = 64
STEP = 16
LO, CORE, BASE, LENGTH, HASPREV, HASNEXT, SLOT0 = range(7)


def mm(a, b, dims=NN, precision=None):
    return lax.dot_general(a, b, dims, precision=precision, preferred_element_type=F32)


def grid_call(body, grid, in_specs, out_specs, out_shape, scratch=(), name=None, limit=None):
    return pl.pallas_call(
        body,
        grid_spec=pltpu.PrefetchScalarGridSpec(
            num_scalar_prefetch=1,
            grid=grid,
            in_specs=in_specs,
            out_specs=out_specs,
            scratch_shapes=list(scratch),
        ),
        out_shape=out_shape,
        compiler_params=pltpu.CompilerParams(
            dimension_semantics=("arbitrary",) * len(grid), vmem_limit_bytes=limit
        ),
        name=name,
    )


def streamed(*arrays):
    return [pltpu.with_memory_space_constraint(array, pltpu.HBM) for array in arrays]


def rows_spec(width, rows=BLOCK, lane=0):
    return pl.BlockSpec((rows, width), lambda b, s: (b, lane))


def whole(shape):
    return pl.BlockSpec(shape, lambda b, s: (0,) * len(shape))


def shaped(shape, dtype=F32):
    return jax.ShapeDtypeStruct(shape, dtype)


def kept(shape, dtype=F32):
    return pltpu.HBM(shape, dtype)


def slope(v, sig):
    return sig * (1.0 + v * (1.0 - sig))


def lanes_of(s_ref, slot, width):
    return pl.ds(pl.multiple_of(s_ref[SLOT0 + slot] * width, width), width)


def normalize(x, gain):
    value = x.astype(F32)
    inverse = lax.rsqrt(jnp.mean(value * value, axis=1, keepdims=True) + EPSILON)
    scaled = value * inverse
    return scaled, (scaled * gain).astype(BF16)


def pick(s_ref, b, quarter, own, near, far):
    lo, core = s_ref[LO], s_ref[CORE]
    place = b // quarter
    mine = (place // 2) == lo
    from_near = (place % 2) == core
    return jnp.where(mine, own, jnp.where(from_near, near, far))


def valid_rows(s_ref, b):
    position = s_ref[BASE] + b * BLOCK + lax.broadcasted_iota(jnp.int32, (BLOCK, 1), 0)
    return (position < s_ref[LENGTH]).astype(F32)


def expander(inner, shift=0):
    lane = lax.broadcasted_iota(jnp.int32, (384, inner), 0) % 128 - HEAD0 - shift
    head = lax.broadcasted_iota(jnp.int32, (384, inner), 1) // 64
    return (lane == head).astype(F32).astype(BF16)


def collector(inner):
    head = lax.broadcasted_iota(jnp.int32, (3 * inner, 128), 0) % inner // 64
    lane = lax.broadcasted_iota(jnp.int32, (3 * inner, 128), 1) - HEAD0
    return (lane == head).astype(F32).astype(BF16)


def two(x):
    high = x.astype(BF16)
    return high, (x - high.astype(F32)).astype(BF16)


def three(x, axis=1):
    high = x.astype(BF16)
    rest = x - high.astype(F32)
    middle = rest.astype(BF16)
    return jnp.concatenate([high, middle, (rest - middle.astype(F32)).astype(BF16)], axis=axis)


def running(tri, x):
    width = x.shape[1]
    wide = mm(tri, three(x))
    return wide[:, :width] + wide[:, width : 2 * width] + wide[:, 2 * width :]


def triangle(forward):
    row = lax.broadcasted_iota(jnp.int32, (BLOCK, BLOCK), 0)
    col = lax.broadcasted_iota(jnp.int32, (BLOCK, BLOCK), 1)
    same = (row // SUB) == (col // SUB)
    keep = (row >= col) if forward else (col >= row)
    return (same & keep).astype(F32).astype(BF16)


def stacked_heads(x):
    half = lax.broadcasted_iota(jnp.int32, (1, 128), 1) < 64
    return two(jnp.concatenate([jnp.where(half, x, 0.0), jnp.where(half, 0.0, x)], axis=0))


def faded(keep, level, level_t, level_x, pair, forward):
    out = []
    for side in range(2):
        h = HEAD0 + 2 * pair + side
        at = pair * 128 + side * 64
        column, row = level_x[:, at : at + 1], level_t[h : h + 1, :]
        diff = column - row if forward else row - column
        out.append(jnp.exp(jnp.where(keep, diff, -1e30)))
    return jnp.concatenate(out, axis=1)


def mixed_heads(mix, high, low):
    mh, ml = two(mix)
    wide = mm(mh, jnp.concatenate([high, low], axis=1))
    return wide[:, :128] + wide[:, 128:] + mm(ml, high)


def head_lanes(inner):
    lane = lax.broadcasted_iota(jnp.int32, (1, 128), 1)
    return (lane >= HEAD0) & (lane < HEAD0 + inner // 64)


def front_body(parts, inner, states, quarter, s_ref, own, near, far, halo, gain, taps, bias, dbias, rate,
               *rest):
    ws = rest[:parts]
    normed_ref, u_ref, uh_ref, co_ref, hd_ref, hloc_ref, pre_ref, end_ref = rest[parts : parts + 8]
    hsc, usc, state, pre, esc = rest[parts + 8 :]
    b = pl.program_id(0)
    wide = inner + 2 * states
    shard = ws[0].shape[0]
    normed_ref[...] = normalize(pick(s_ref, b, quarter, own[...], near[...], far[...]), gain[...])[1]

    @pl.when(b == 0)
    def _():
        hsc[...] = normalize(halo[...], gain[...])[1]
        edge = jnp.zeros((16, wide), F32)
        for j in range(parts):
            edge += mm(hsc[:, lanes_of(s_ref, j, shard)], ws[j][:, :wide])
        edge = jnp.where(s_ref[HASPREV] > 0, edge[8:], 0.0)
        usc[0:8] = edge
        uh_ref[...] = edge
        state[...] = jnp.zeros_like(state)
        pre[...] = jnp.zeros_like(pre)
        esc[...] = expander(inner)

    @pl.when(b > 0)
    def _():
        usc[0:8] = usc[BLOCK : BLOCK + 8]

    u = jnp.zeros((BLOCK, wide + 128), F32)
    for j in range(parts):
        u += mm(normed_ref[:, lanes_of(s_ref, j, shard)], ws[j][...])
    usc[8 : 8 + BLOCK] = u[:, :wide]
    u_ref[...] = u[:, :wide]
    conv = bias[...] + taps[0:1] * usc[5 : 5 + BLOCK]
    for k in range(1, 4):
        conv = conv + taps[k : k + 1] * usc[5 + k : 5 + k + BLOCK]
    co_ref[...] = conv
    raw = u[:, wide:] + dbias[...]
    delta = jnp.where(head_lanes(inner), jnp.maximum(raw, 0.0) + jnp.log1p(jnp.exp(-jnp.abs(raw))), 0.0)
    delta = delta * valid_rows(s_ref, b)
    level = running(triangle(True), delta * rate[...])
    raw = jnp.where(head_lanes(inner), raw, 0.0)
    hd_ref[...] = level + pltpu.roll(delta, STEP, 1) + pltpu.roll(raw, 2 * STEP, 1)
    both = mm(jnp.concatenate([three(level), three(delta)], axis=0), esc[...])
    level_x, delta_x = both[:BLOCK], both[BLOCK:]
    act = conv * jax.nn.sigmoid(conv)
    source = delta_x * act[:, :inner]
    inject_t = act[:, inner : inner + states].T
    for i in range(BLOCK // SUB):
        at = slice(i * SUB, (i + 1) * SUB)
        last = level_x[(i + 1) * SUB - 1 : (i + 1) * SUB]
        fresh = mm(inject_t[:, at], jnp.exp(last - level_x[at]) * source[at], precision=HIGH)
        before = state[...]
        n = b * (BLOCK // SUB) + i
        hloc_ref[n] = before
        pre_ref[n] = pre[...]
        state[...] = jnp.exp(last) * before + fresh
        pre[...] = pre[...] + last

    @pl.when(b == pl.num_programs(0) - 1)
    def _():
        hloc_ref[n + 1] = state[...]
        end_ref[...] = state[...]
        pre_ref[n + 1] = pre[...]


def start_expanders(inner, *scs):
    @pl.when(pl.program_id(0) == 0)
    def _():
        for shift, sc in scs:
            sc[...] = expander(inner, shift)


def within_body(inner, states, s_ref, co, hd, yw_ref, lsc, dsc):
    start_expanders(inner, (0, lsc), (STEP, dsc))
    conv = co[...]
    act = conv * jax.nn.sigmoid(conv)
    level = hd[...]
    exact = three(level)
    lx = mm(exact, lsc[...])
    xs = mm(exact, dsc[...]) * act[:, :inner]
    keep = lax.broadcasted_iota(jnp.int32, (SUB, SUB), 0) >= lax.broadcasted_iota(jnp.int32, (SUB, SUB), 1)
    for i in range(BLOCK // SUB):
        at = slice(i * SUB, (i + 1) * SUB)
        affinity = mm(act[at, inner + states :], act[at, inner : inner + states], NT, HIGH)
        affinity = jnp.concatenate([affinity, affinity], axis=1)
        level_t = level[at].T
        level_x = lx[at]
        for pair in range(inner // 128):
            lanes = slice(pair * 128, pair * 128 + 128)
            mix = faded(keep, level, level_t, level_x, pair, True) * affinity
            yw_ref[at, lanes] = mixed_heads(mix, *stacked_heads(xs[at, lanes]))


def gates_body(parts, quarter, s_ref, normed, own, near, far, *rest):
    ws = rest[:parts]
    gate_ref, gg_ref, bg_ref = rest[parts:]
    b = pl.program_id(0)
    shard = ws[0].shape[0]
    inner = gate_ref.shape[1]
    up = pick(s_ref, b, quarter, own[...], near[...], far[...])
    bg_ref[...] = (up.astype(F32) * valid_rows(s_ref, b)).astype(BF16)
    gate = jnp.zeros(gate_ref.shape, F32)
    gg = jnp.zeros(gg_ref.shape, F32)
    for j in range(parts):
        at = lanes_of(s_ref, j, shard)
        gate += mm(normed[:, at], ws[j][:, :inner])
        gg += mm(bg_ref[:, at], ws[j][:, inner:])
    gate_ref[...] = gate
    gg_ref[...] = gg


def entering(hloc, pre, hin):
    return hloc + jnp.exp(pre[0:1]) * hin


def output_body(inner, states, s_ref, co, hd, yw, gate, gg, hloc, pre, hin, skip, ggain, y_ref, sum_ref, lsc):
    start_expanders(inner, (0, lsc))
    lx = mm(three(hd[...]), lsc[...])
    conv = co[...]
    act = conv * jax.nn.sigmoid(conv)
    for i in range(BLOCK // SUB):
        at = slice(i * SUB, (i + 1) * SUB)
        held = entering(hloc[i], pre[i], hin[...])
        y_ref[at] = yw[at] + jnp.exp(lx[at]) * mm(act[at, inner + states :], held, precision=HIGH)
    out = y_ref[...] + skip[...] * act[:, :inner]
    g = gate[...]
    product = out * (g * jax.nn.sigmoid(g))
    ones = jnp.ones((8, 3 * inner), BF16)
    sum_ref[0:8] = mm(ones, three(product * product), NT)
    sum_ref[8:16] = mm(ones, three(gg[...] * ggain[...] * product), NT)


def turn_body(inner, states, total, s_ref, co, hd, y, gate, gg, sums, sums1, sums2, sums3, skip, ggain,
              gated_ref, ggrad_ref, og_ref, gloc_ref, start_ref, cols_ref, chain, lsc):
    start_expanders(inner, (0, lsc))
    lx = mm(three(hd[...]), lsc[...])
    step = pl.program_id(0)
    conv = co[...]
    act = conv * jax.nn.sigmoid(conv)
    x = act[:, :inner]
    readout_t = act[:, inner + states :].T
    both = (sums[...] + sums1[...] + sums2[...] + sums3[...]).T
    ginv = lax.rsqrt(both[:, 0:1] / total + EPSILON)
    dot = ginv * both[:, 8:9] / total
    g = gate[...]
    sig = jax.nn.sigmoid(g)
    ga = g * sig
    out = y[...] + skip[...] * x
    unit = out * ga * ginv
    gated_ref[...] = (unit * ggain[...]).astype(BF16)
    grad = gg[...]
    pg = ginv * (grad * ggain[...] - unit * dot)
    og = pg * ga
    og_ref[...] = og
    ggrad_ref[...] = (pg * out * slope(g, sig)).astype(BF16)

    @pl.when(step == 0)
    def _():
        chain[...] = jnp.zeros_like(chain)
        cols_ref[...] = jnp.zeros_like(cols_ref)

    cols_ref[0:1] += jnp.sum(grad * unit, axis=0, keepdims=True)
    cols_ref[1:2] += jnp.sum(og * x, axis=0, keepdims=True)
    b = pl.num_programs(0) - 1 - step
    for i in reversed(range(BLOCK // SUB)):
        at = slice(i * SUB, (i + 1) * SUB)
        held = chain[...]
        n = b * (BLOCK // SUB) + i
        gloc_ref[n + 1] = held
        level_x = lx[at]
        chain[...] = jnp.exp(level_x[SUB - 1 : SUB]) * held + mm(
            readout_t[:, at], jnp.exp(level_x) * og[at], precision=HIGH
        )

    @pl.when(b == 0)
    def _():
        gloc_ref[0] = chain[...]
        start_ref[...] = chain[...]


def back_body(inner, states, s_ref, co, hd, og, hloc, pre, hin, z_ref, dbc_ref, lsc, dsc):
    start_expanders(inner, (0, lsc), (STEP, dsc))
    conv = co[...]
    act = conv * jax.nn.sigmoid(conv)
    level = hd[...]
    exact = three(level)
    lx = mm(exact, lsc[...])
    xs = mm(exact, dsc[...]) * act[:, :inner]
    keep = lax.broadcasted_iota(jnp.int32, (SUB, SUB), 1) >= lax.broadcasted_iota(jnp.int32, (SUB, SUB), 0)
    for i in range(BLOCK // SUB):
        at = slice(i * SUB, (i + 1) * SUB)
        inject, readout = act[at, inner : inner + states], act[at, inner + states :]
        affinity = mm(inject, readout, NT, HIGH)
        affinity = jnp.concatenate([affinity, affinity], axis=1)
        level_t = level[at].T
        level_x = lx[at]
        grad = jnp.zeros((SUB, SUB), F32)
        for pair in range(inner // 128):
            lanes = slice(pair * 128, pair * 128 + 128)
            fade = faded(keep, level, level_t, level_x, pair, False)
            g = og[at, lanes]
            z_ref[at, lanes] = mixed_heads(fade * affinity, *stacked_heads(g))
            xh, xl = stacked_heads(xs[at, lanes])
            gh, gl = two(g)
            outer = mm(
                jnp.concatenate([xh, xl], axis=1), jnp.concatenate([gh, gh], axis=1), NT
            ) + mm(xh, gl, NT)
            grad += fade[:, :SUB] * outer[:SUB] + fade[:, SUB:] * outer[SUB:]
        held = entering(hloc[i], pre[i], hin[...])
        dbc_ref[at, :states] = mm(grad, readout, precision=HIGH)
        dbc_ref[at, states:] = mm(grad.T, inject, precision=HIGH) + mm(
            jnp.exp(level_x) * og[at], held, NT, HIGH
        )


def conv_back(grad, csc, usc, taps, cols_ref):
    csc[0:BLOCK] = grad
    pre = taps[0:1] * csc[3 : 3 + BLOCK]
    for k in range(1, 4):
        pre = pre + taps[k : k + 1] * csc[3 - k : 3 - k + BLOCK]
    for k in range(4):
        cols_ref[k : k + 1] += jnp.sum(grad * usc[5 + k : 5 + k + BLOCK], axis=0, keepdims=True)
    cols_ref[4:5] += jnp.sum(grad, axis=0, keepdims=True)
    csc[BLOCK : BLOCK + 8] = grad[0:8]
    return pre


def meet_body(inner, states, s_ref, co, hd, z, dbc, hloc, pre, gloc, gin, hin, zed_ref, ends_ref, keep_ref,
              give_ref, lsc, dsc):
    start_expanders(inner, (0, lsc), (STEP, dsc))
    exact = three(hd[...])
    lx = mm(exact, lsc[...])
    subs = BLOCK // SUB
    count = pl.num_programs(0)
    b = pl.program_id(0)
    conv = co[...]
    act = conv * jax.nn.sigmoid(conv)
    source = mm(exact, dsc[...]) * act[:, :inner]
    ends = []
    inject_grads = []
    for i in range(subs):
        at = slice(i * SUB, (i + 1) * SUB)
        n = b * subs + i + 1
        level_x = lx[at]
        later = gloc[n] + jnp.exp(pre[subs * count][0:1] - pre[n][0:1]) * gin[...]
        fade = jnp.exp(level_x[SUB - 1 : SUB] - level_x)
        zed_ref[at] = z[at] + fade * mm(act[at, inner : inner + states], later, precision=HIGH)
        inject_grads.append(dbc[at, :states] + mm(fade * source[at], later, NT, HIGH))
        ends.append(jnp.sum(later * entering(hloc[n], pre[n], hin[...]), axis=0, keepdims=True))
    ends_ref[...] = jnp.concatenate(ends + [jnp.zeros((8 - subs, inner), F32)], axis=0)
    inject_grad = jnp.concatenate(inject_grads, axis=0)
    half = count // 2
    rows = pl.ds(pl.multiple_of((b % half) * BLOCK, BLOCK), BLOCK)

    @pl.when(b // half == s_ref[CORE])
    def _():
        keep_ref[rows, :states] = inject_grad
        keep_ref[rows, states:] = dbc[:, states:]

    @pl.when(b // half != s_ref[CORE])
    def _():
        give_ref[rows, :states] = inject_grad
        give_ref[rows, states:] = dbc[:, states:]


def join_body(inner, s_ref, co, hd, og, y, zed_in, ends_in, u, prior, uh, taps, rate, skip, mg_ref,
              tail_ref, head_ref, rg_ref, cols_ref, sig_ref, col_sc, csc, usc, dsc):
    start_expanders(inner, (STEP, dsc))
    step = pl.program_id(0)
    subs = BLOCK // SUB
    count = pl.num_programs(0)
    b = count - 1 - step

    @pl.when(step == 0)
    def _():
        cols_ref[...] = jnp.zeros_like(cols_ref)
        sig_ref[...] = jnp.zeros_like(sig_ref)
        col_sc[...] = collector(inner)
        csc[BLOCK : BLOCK + 8] = jnp.zeros((8, inner), F32)

    conv = co[...]
    sig = jax.nn.sigmoid(conv)
    x = conv * sig
    packed_heads = hd[...]
    delta_x = mm(three(packed_heads), dsc[...])
    zed = zed_in[...]
    ends = ends_in[...]
    g = og[...]
    sums = mm(three(jnp.concatenate([x * zed, g * y[...], ends], axis=0)), col_sc[...])
    direct, read, ends = sums[:BLOCK], sums[BLOCK : 2 * BLOCK], sums[2 * BLOCK :]
    dlt = jnp.where(head_lanes(inner), pltpu.roll(packed_heads, 128 - STEP, 1), 0.0)
    draw = pltpu.roll(packed_heads, 128 - 2 * STEP, 1)
    q = running(triangle(False), read - dlt * direct)
    q = jnp.concatenate([q[i * SUB : (i + 1) * SUB] + ends[i : i + 1] for i in range(subs)], axis=0)
    rg = (direct + rate[...] * q) * valid_rows(s_ref, b) * jax.nn.sigmoid(draw)
    rg = jnp.where(head_lanes(inner), rg, 0.0)
    rg_ref[...] = rg
    cols_ref[0:1] += jnp.sum(rg, axis=0, keepdims=True)
    cols_ref[1:2] += jnp.sum(dlt * q, axis=0, keepdims=True)

    usc[0:8] = jnp.where(b == 0, uh[...], prior[...])
    usc[8 : 8 + BLOCK] = u[...]
    grad = (delta_x * zed + skip[...] * g) * slope(conv, sig)
    pre_grad = conv_back(grad, csc, usc, taps, sig_ref)
    mg_ref[...] = pre_grad.astype(BF16)
    head_ref[...] = grad[0:8]

    @pl.when(step == 0)
    def _():
        tail_ref[...] = pre_grad[BLOCK - 8 :]


def exponents(peak):
    return jnp.clip(jnp.ceil(jnp.log(jnp.maximum(peak, 1e-36)) * 1.4426950408889634) - 14.0, -100.0, 100.0)


def packed(value, power, inverse, riders=()):
    rows = [(value * inverse).astype(F16), jnp.broadcast_to(power, (16, value.shape[1])).astype(F16)]
    for more in riders:
        each = exponents(jnp.abs(more))
        rows += [(more * jnp.exp2(-each)).astype(F16), each.astype(F16)]
    return jnp.concatenate(rows)


def unpacked(sent, counts=()):
    rows = sent.shape[0] - 16 - 2 * sum(counts)
    power = sent[rows : rows + 1].astype(F32)
    more = []
    at = rows + 16
    for size in counts:
        more.append(sent[at : at + size].astype(F32) * jnp.exp2(sent[at + size : at + 2 * size].astype(F32)))
        at += 2 * size
    return sent[:rows].astype(F32) * jnp.exp2(power), power, more


def grads_body(parts, pairs, s_ref, *refs):
    inputs = 1 + max(max(pair) for pair in pairs)
    outs = refs[inputs : inputs + parts]
    powers, inverse, peak = refs[inputs + parts :]
    j = pl.program_id(0)

    @pl.when(j == 0)
    def _():
        peak[...] = jnp.zeros_like(peak)

    at = 0
    for left, right in pairs:
        value = mm(refs[left][...], refs[right][...], TN)
        lanes = slice(at, at + value.shape[1])
        at += value.shape[1]
        peak[0:1, lanes] = jnp.maximum(peak[0:1, lanes], jnp.max(jnp.abs(value), axis=0, keepdims=True))
        for k in range(parts):

            @pl.when(j == k)
            def _():
                outs[k][:, lanes] = value

    @pl.when(j == parts - 1)
    def _():
        power = exponents(peak[...])
        powers[...] = jnp.broadcast_to(power[0:1], (16, at))
        inverse[...] = jnp.exp2(-power[0:1])


def deal(s_ref, b, quarter, value, outs):
    place = b // quarter
    rows = pl.ds(pl.multiple_of((b % quarter) * BLOCK, BLOCK), BLOCK)
    at = (place % 2 != s_ref[CORE]).astype(jnp.int32) * 2 + (place // 2 != s_ref[LO]).astype(jnp.int32)
    for k in range(4):

        @pl.when(at == k)
        def _():
            outs[k][rows] = value


def feature_body(parts, quarter, s_ref, own, near, far, ggrad, mg, rg, dbc, dbc_other, co, u, prior, uh, ahead,
                 taps, *rest):
    ws1 = rest[:parts]
    ws2 = rest[parts : 2 * parts]
    outs = rest[2 * parts : 2 * parts + 4]
    xg_ref, cols_ref, state_ref, whole_sc, csc, usc = rest[2 * parts + 4 :]
    step = pl.program_id(0)
    count = pl.num_programs(0)
    b = count - 1 - step
    inner = ggrad.shape[1]
    shard = ws1[0].shape[0]

    @pl.when(step == 0)
    def _():
        cols_ref[...] = jnp.zeros_like(cols_ref)
        state_ref[...] = jnp.zeros_like(state_ref)
        csc[BLOCK : BLOCK + 8] = jnp.where(s_ref[HASNEXT] > 0, ahead[...], 0.0)

    usc[0:8] = jnp.where(b == 0, uh[...], prior[...])
    usc[8 : 8 + BLOCK] = u[...]
    conv = co[...]
    grad = jnp.where(b // (count // 2) == s_ref[CORE], dbc[...], dbc_other[...])
    grad = grad * slope(conv, jax.nn.sigmoid(conv))
    pre = conv_back(grad, csc, usc, taps, state_ref)
    pre = jnp.where(s_ref[CORE] > 0, pltpu.roll(pre, 64, 1), pre)
    lane = lax.broadcasted_iota(jnp.int32, (BLOCK, 128), 1)
    xg = jnp.where(lane < HEAD0, pre, rg[...]).astype(BF16)
    xg_ref[...] = xg
    for j in range(parts):
        at = lanes_of(s_ref, j, shard)
        whole_sc[:, at] = (
            mm(ggrad[...], ws2[j][:, :inner], NT)
            + mm(mg[...], ws1[j][:, :inner], NT)
            + mm(xg, ws1[j][:, -128:], NT)
        )
    value = whole_sc[...]
    scaled = normalize(pick(s_ref, b, quarter, own[...], near[...], far[...]), 1.0)[0]
    cols_ref[0:1] += jnp.sum(value * scaled, axis=0, keepdims=True)
    deal(s_ref, b, quarter, value, outs)


def branch_body(parts, quarter, s_ref, gated, *rest):
    ws2 = rest[:parts]
    outs = rest[parts : parts + 4]
    whole_sc = rest[parts + 4]
    inner = gated.shape[1]
    shard = ws2[0].shape[0]
    for j in range(parts):
        whole_sc[:, lanes_of(s_ref, j, shard)] = mm(gated[...], ws2[j][:, inner:], NT)
    deal(s_ref, pl.program_id(0), quarter, whole_sc[...], outs)


def per_device(
    hidden, lengths, cotangent, norm_gain, proj_main, proj_state, proj_delta, conv_main, conv_state,
    bias_main, bias_state, delta_bias, log_rate, skip_gain, gate_gain, proj_out,
):
    _, steps, model = hidden.shape
    hidden, cotangent = hidden[0], cotangent[0]
    dps, ctxs, tps = lax.axis_size("dp"), lax.axis_size("ctx"), lax.axis_size("tp")
    dp, z, core = lax.axis_index("dp"), lax.axis_index("ctx"), lax.axis_index("tp")
    lo, hi = z % 2, z // 2
    pairs = ctxs // 2
    tokens = 2 * steps
    count = tokens // BLOCK
    quarter = count // 4
    inner = bias_main.shape[0] // 2
    heads = delta_bias.shape[0] // 2
    states = bias_state.shape[0] // 2
    wide = inner + 2 * states

    def swap(value):
        return lax.ppermute(value, "tp", [(0, 1), (1, 0)])

    def across(value, j):
        return lax.ppermute(value, "ctx", [(i, i ^ j) for i in range(ctxs)])

    def along(value, step):
        return lax.ppermute(
            value, "ctx", [(i, i + step) for i in range(ctxs) if 0 <= i + step < ctxs]
        )

    def spread(value, j):
        return lax.ppermute(value, "dp", [(i, i ^ j) for i in range(dps)])

    def mine(value, axis, size):
        return lax.dynamic_slice_in_dim(value, lo * size, size, axis)

    def piece(value, at, size):
        return lax.dynamic_slice_in_dim(value, at * size, size, 0)

    apart = proj_main.shape[0] % 128 == 0
    parts = dps if apart else 1
    shard = proj_main.shape[0] * (dps // parts)

    def gathered(value):
        if not apart:
            return [lax.all_gather(value, "dp", axis=0, tiled=True)]
        return [value] + [spread(value, j) for j in range(1, dps)]

    scalars = jnp.stack(
        [lo, core, hi * tokens, lengths[0], (hi > 0).astype(jnp.int32), (hi < pairs - 1).astype(jnp.int32)]
        + [dp ^ j if apart else 0 * dp for j in range(parts)]
    ).astype(jnp.int32)

    state_own = lax.dynamic_slice_in_dim(proj_state, lo * states + core * (states // 2), states // 2, 1)
    delta_own = mine(proj_delta, 1, heads)
    main_part = mine(proj_main, 2, inner)
    first = jnp.concatenate(
        [main_part[:, 1], proj_state, state_own, delta_own,
         jnp.zeros((proj_main.shape[0], 64 - heads), BF16)], axis=1
    )
    halfway = steps // 2
    near = across(piece(hidden, core, halfway), 1)
    far = swap(near)
    ws1 = gathered(first)

    def payloads(pieces, scale, riders=()):
        return [packed(pieces[j], scale[0], scale[1], riders) for j in range(1, parts)]

    def over_sequences(payload):
        return [spread(payload[j - 1], j) for j in range(1, parts)]

    def totalled(pieces, scale, got, riders=()):
        total, power = pieces[0], scale[0][0:1]
        if not apart:
            total = lax.psum_scatter(total, "dp", scatter_dimension=0, tiled=True)
            power = exponents(jnp.max(jnp.abs(total), axis=0, keepdims=True))
            riders = [lax.psum(value, "dp") for value in riders]
        for sent in got:
            value, other, more = unpacked(sent, [rider.shape[0] for rider in riders])
            total, power = total + value, jnp.maximum(power, other)
            riders = [one + two for one, two in zip(riders, more)]
        return total, power + (parts - 1).bit_length(), riders

    def chunks(totals, power, riders=()):
        size = totals[0].shape[0] // ctxs
        rows = [jnp.concatenate([piece(total, z ^ j, size) for total in totals], axis=1) for j in range(ctxs)]
        return rows[:1] + [packed(value, power, jnp.exp2(-power), riders) for value in rows[1:]]

    def over_positions(cut):
        return [across(cut[j], j) for j in range(1, ctxs)]

    def settled(own, got):
        opposite = got[0]
        for j in range(2, ctxs):
            if j % 2 == 0:
                own = own + got[j - 1]
            else:
                opposite = opposite + got[j - 1]
        return jnp.where(lo == 0, own, opposite), jnp.where(lo == 0, opposite, own)

    def decoded(got, counts=()):
        return [unpacked(sent, counts)[0] for sent in got]

    def ridden(got, counts):
        return [unpacked(sent, counts)[2][0] for sent in got]

    taps_x = jnp.concatenate([mine(conv_main, 1, inner), conv_state], axis=1)
    bias_x = jnp.concatenate([mine(bias_main, 0, inner), bias_state])[None]
    rate_own = -jnp.exp(mine(log_rate, 0, heads))

    def in_heads(value):
        return jnp.pad(value, (HEAD0, 128 - HEAD0 - heads))[None]

    rate_row = in_heads(rate_own)
    dbias_row = in_heads(mine(delta_bias, 0, heads))
    skip_row = jnp.repeat(mine(skip_gain, 0, heads), inner // heads)[None]
    ggain_row = mine(gate_gain, 0, inner)[None]
    gain_row = norm_gain[None]
    edge, scalars, taps_x, bias_x, rate_row, dbias_row, _ = lax.optimization_barrier(
        (hidden[steps - 16 :], scalars, taps_x, bias_x, rate_row, dbias_row, first)
    )
    route = [
        ((z0 - 1) * tps + c, (z0 + c) * tps + c) for z0 in range(2, ctxs, 2) for c in range(2)
    ]
    edge = lax.ppermute(edge, ("ctx", "tp"), route)
    halo = jnp.where(core == lo, edge, swap(edge))

    ws1, near, main_gate, out_later, cot_later = lax.optimization_barrier(
        (ws1, near, main_part[:, 0], proj_out, cotangent)
    )
    second = jnp.concatenate([main_gate, mine(out_later, 1, inner)], axis=1)
    ws2 = gathered(second)
    cot_near = across(piece(cot_later, core, halfway), 1)

    own_spec = pl.BlockSpec(
        (BLOCK, model), lambda b, s: (jnp.clip(b - s[LO] * 2 * quarter, 0, 2 * quarter - 1), 0)
    )
    part_spec = pl.BlockSpec((BLOCK, model), lambda b, s: (b % quarter, 0))
    subs = BLOCK // SUB
    last = count * subs
    state_block = pl.BlockSpec((subs, states, inner), lambda b, s: (b, 0, 0))
    pre_block = pl.BlockSpec((subs, 8, inner), lambda b, s: (b, 0, 0))

    normed, u, uh, conv, per_head, hloc, pre, own_end = grid_call(
        functools.partial(front_body, parts, inner, states, quarter),
        (count,),
        [own_spec, part_spec, part_spec, whole((16, model)), whole((1, model)), whole((4, wide)),
         whole((1, wide)), whole((1, 128)), whole((1, 128))] + [whole((shard, wide + 128))] * parts,
        [rows_spec(model), rows_spec(wide), whole((8, wide)), rows_spec(wide), rows_spec(128),
         whole((last + 1, states, inner)), whole((last + 1, 8, inner)), whole((states, inner))],
        [shaped((tokens, model), BF16), shaped((tokens, wide)), shaped((8, wide)), shaped((tokens, wide)),
         shaped((tokens, 128)), shaped((last + 1, states, inner)), shaped((last + 1, 8, inner)),
         shaped((states, inner))],
        [pltpu.VMEM((16, model), BF16), pltpu.VMEM((8 + BLOCK, wide), F32), pltpu.VMEM((states, inner), F32),
         pltpu.VMEM((8, inner), F32), pltpu.VMEM((384, inner), BF16)],
        name="front",
    )(scalars, hidden, near, far, halo, gain_row, taps_x, bias_x, dbias_row, rate_row, *ws1)

    cot_near, own_end = lax.optimization_barrier((cot_near, own_end))
    cot_far = swap(cot_near)
    growth = jnp.exp(pre[last][0:1])
    carried = jnp.zeros_like(own_end)
    sending = own_end
    for hop in range(pairs - 1):
        carried = along(sending, 2)
        if hop < pairs - 2:
            sending = own_end + growth * carried

    (inside,) = grid_call(
        functools.partial(within_body, inner, states),
        (count,),
        [rows_spec(wide), rows_spec(128)],
        [rows_spec(inner)],
        [shaped((tokens, inner))],
        [pltpu.VMEM((384, inner), BF16)] * 2,
        name="within",
        limit=20 << 20,
    )(scalars, *streamed(conv, per_head))

    gate, gated_grad, branch_grad = grid_call(
        functools.partial(gates_body, parts, quarter),
        (count,),
        [rows_spec(model), own_spec, part_spec, part_spec] + [whole((shard, 2 * inner))] * parts,
        [rows_spec(inner), rows_spec(inner), rows_spec(model)],
        [shaped((tokens, inner)), shaped((tokens, inner)), shaped((tokens, model), BF16)],
        name="gates",
        limit=20 << 20,
    )(scalars, *streamed(normed, cotangent, cot_near, cot_far, *ws2))

    y, sums = grid_call(
        functools.partial(output_body, inner, states),
        (count,),
        [rows_spec(wide), rows_spec(128), rows_spec(inner), rows_spec(inner), rows_spec(inner), state_block,
         pre_block, whole((states, inner)), whole((1, inner)), whole((1, inner))],
        [rows_spec(inner), pl.BlockSpec((16, BLOCK), lambda b, s: (0, b))],
        [shaped((tokens, inner)), shaped((16, tokens))],
        [pltpu.VMEM((384, inner), BF16)],
        name="output",
        limit=20 << 20,
    )(scalars, *streamed(conv, per_head), inside, gate, gated_grad, *streamed(hloc), pre, carried, skip_row, ggain_row)

    corner = [(n, ((n // tps) ^ 1) * tps + (n % tps + 1) % tps) for n in range(ctxs * tps)]
    all_sums = [sums, swap(sums), across(sums, 1), lax.ppermute(sums, ("ctx", "tp"), corner)]

    def back(width, rows=BLOCK):
        return pl.BlockSpec((rows, width), lambda b, s: (count - 1 - b, 0))

    back_sums = pl.BlockSpec((16, BLOCK), lambda b, s: (0, count - 1 - b))
    gated, gate_grad, out_grad, gloc, own_start, turn_cols = grid_call(
        functools.partial(turn_body, inner, states, 2 * tps * inner),
        (count,),
        [back(wide), back(128), back(inner), back(inner), back(inner),
         back_sums, back_sums, back_sums, back_sums, whole((1, inner)), whole((1, inner))],
        [back(inner), back(inner), back(inner), whole((last + 1, states, inner)), whole((states, inner)),
         whole((8, inner))],
        [kept((tokens, inner), BF16), kept((tokens, inner), BF16), kept((tokens, inner)),
         kept((last + 1, states, inner)), shaped((states, inner)), shaped((8, inner))],
        [pltpu.VMEM((states, inner), F32), pltpu.VMEM((384, inner), BF16)],
        name="turn",
        limit=20 << 20,
    )(scalars, *streamed(conv, per_head), y, gate, gated_grad, *all_sums, skip_row, ggain_row)

    returned = jnp.zeros_like(own_start)
    sending = own_start
    for hop in range(pairs - 1):
        returned = along(sending, -2)
        if hop < pairs - 2:
            sending = own_start + growth * returned

    turned = pl.BlockSpec((tokens, shard), lambda j, s: (0, s[SLOT0 + j]))
    dealt_specs = [whole((halfway, model))] * 4
    dealt_shapes = [shaped((halfway, model))] * 4
    def grads(lefts, rights, name):
        sources = []
        for left, right in zip(lefts, rights):
            sources += [left, right]
        width = sum(right.shape[1] for right in rights)
        specs = [turned if n % 2 == 0 else whole(source.shape) for n, source in enumerate(sources)]
        *pieces, powers, inverse = grid_call(
            functools.partial(grads_body, parts, [(n, n + 1) for n in range(0, len(sources), 2)]),
            (parts,),
            specs,
            [whole((shard, width))] * parts + [whole((16, width)), whole((1, width))],
            [shaped((shard, width))] * parts + [shaped((16, width)), shaped((1, width))],
            [pltpu.VMEM((8, width), F32)],
            name=name,
        )(scalars, *sources)
        return pieces, (powers, inverse)

    early, early_scale = grads([normed, branch_grad], [gate_grad, gated], "grad_early")
    early_got = over_sequences(payloads(early, early_scale))
    early, out_grad = lax.optimization_barrier((early, out_grad))

    zed, dbc = grid_call(
        functools.partial(back_body, inner, states),
        (count,),
        [rows_spec(wide), rows_spec(128), rows_spec(inner), state_block, pre_block, whole((states, inner))],
        [rows_spec(inner), rows_spec(2 * states)],
        [shaped((tokens, inner)), shaped((tokens, 2 * states))],
        [pltpu.VMEM((384, inner), BF16)] * 2,
        name="back",
    )(scalars, conv, per_head, out_grad, hloc, pre, carried)

    gated_later, zed = lax.optimization_barrier((gated, zed))
    branch = grid_call(
        functools.partial(branch_body, parts, quarter),
        (count,),
        [rows_spec(inner)] + [whole((shard, 2 * inner))] * parts,
        dealt_specs,
        dealt_shapes,
        [pltpu.VMEM((BLOCK, model), F32)],
        name="branch",
    )(scalars, gated_later, *ws2)

    returned, early_got, branch = lax.optimization_barrier((returned, early_got, branch))
    front_rows = halfway // 4
    branch_give = swap(branch[3])
    branch_theirs = [branch[1][:front_rows] + branch_give[:front_rows], branch[1][front_rows:] + branch_give[front_rows:]]
    returned, branch_theirs = lax.optimization_barrier((returned, branch_theirs))
    branch_back = [across(branch_theirs[0], 1)]
    all_states = whole((last + 1, states, inner))
    all_pre = whole((last + 1, 8, inner))
    per = BLOCK // 8
    half_rows = tokens // 2

    def back_lanes(width, lanes):
        return [
            pl.BlockSpec((BLOCK, width), lambda b, s: (count - 1 - b, lanes(s))),
            pl.BlockSpec((8, width), lambda b, s: (jnp.maximum((count - 1 - b) * per - 1, 0), lanes(s))),
            pl.BlockSpec((8, width), lambda b, s: (0, lanes(s))),
        ]

    def table(rows, width, lanes):
        return pl.BlockSpec((rows, width), lambda b, s: (0, lanes(s)))

    zed, ends, dbc_keep, dbc_give = grid_call(
        functools.partial(meet_body, inner, states),
        (count,),
        [rows_spec(wide), rows_spec(128), rows_spec(inner), rows_spec(2 * states), all_states,
         all_pre, all_states, whole((states, inner)), whole((states, inner))],
        [rows_spec(inner), rows_spec(inner, 8), whole((half_rows, 2 * states)), whole((half_rows, 2 * states))],
        [shaped((tokens, inner)), shaped((8 * count, inner)), shaped((half_rows, 2 * states)),
         shaped((half_rows, 2 * states))],
        [pltpu.VMEM((384, inner), BF16)] * 2,
        name="meet",
        limit=20 << 20,
    )(scalars, *streamed(conv, per_head, zed, dbc, hloc, pre, gloc), returned, carried)

    zed, ends, dbc_keep, dbc_give, branch_back = lax.optimization_barrier((zed, ends, dbc_keep, dbc_give, branch_back))
    early_total, early_power, _ = totalled(early, early_scale, early_got)
    early_cut = chunks([early_total], early_power)
    early_far = over_positions(early_cut)
    signal_pre, tail, head, raw_grad, head_cols, signal_cols = grid_call(
        functools.partial(join_body, inner),
        (count,),
        [back(inner), back(128), back(inner), back(inner), back(inner), back(inner, 8)]
        + back_lanes(inner, lambda s: 0)
        + [table(4, inner, lambda s: 0), whole((1, 128)), whole((1, inner))],
        [back(inner), whole((8, inner)), whole((8, inner)), back(128), whole((8, 128)), whole((8, inner))],
        [shaped((tokens, inner), BF16), shaped((8, inner)), shaped((8, inner)), shaped((tokens, 128)),
         shaped((8, 128)), shaped((8, inner))],
        [pltpu.VMEM((3 * inner, 128), BF16), pltpu.VMEM((BLOCK + 8, inner), F32),
         pltpu.VMEM((BLOCK + 8, inner), F32), pltpu.VMEM((384, inner), BF16)],
        name="join",
        limit=20 << 20,
    )(scalars, *streamed(conv, per_head, out_grad, y), zed, ends, *streamed(u, u), uh, taps_x, rate_row, skip_row)

    head, early_far = lax.optimization_barrier((head, early_far))
    early_sum = settled(early_cut[0], decoded(early_far))
    out_sum = jnp.concatenate([part[:, inner:] for part in early_sum], axis=1)
    gate_sum = jnp.concatenate([part[:, :inner] for part in early_sum], axis=1)

    ahead, out_sum, gate_sum = lax.optimization_barrier((along(head, -2), out_sum, gate_sum))
    ahead = jnp.where(hi < pairs - 1, ahead, 0.0)
    for k in range(3):
        tail = tail + taps_x[k, :inner] * jnp.concatenate([jnp.zeros((5 + k, inner), F32), ahead[: 3 - k]])
    signal_pre = lax.dynamic_update_slice_in_dim(signal_pre, tail.astype(BF16), tokens - 8, 0)

    dbc = dbc_keep + swap(dbc_give)
    signal_pre, dbc = lax.optimization_barrier((signal_pre, dbc))
    dbc_back = across(lax.dynamic_slice_in_dim(dbc, (1 - lo) * states, states, 1), 1)
    signal_small = jnp.concatenate([signal_cols, turn_cols])
    signal, signal_scale = grads([normed], [signal_pre], "grad_signal")
    signal, dbc_back = lax.optimization_barrier((signal, dbc_back))
    signal_payload = payloads(signal, signal_scale, [signal_small])

    dbc = mine(dbc, 1, states) + dbc_back
    dbc_other = swap(dbc)
    head_rows = jnp.where(core == 0, dbc[:8], dbc_other[:8])
    head_conv = lax.dynamic_slice(conv, (0, inner + lo * states), (8, states))
    state_ahead = along(head_rows * slope(head_conv, jax.nn.sigmoid(head_conv)), -2)
    branch_later, state_ahead, signal_payload = lax.optimization_barrier((branch_theirs[1], state_ahead, signal_payload))
    signal_got = over_sequences(signal_payload)
    def back_own(b, s):
        return jnp.clip(count - 1 - b - s[LO] * 2 * quarter, 0, 2 * quarter - 1), 0

    def state_lanes(s):
        return inner // states + s[LO]

    back_part = pl.BlockSpec((BLOCK, model), lambda b, s: ((count - 1 - b) % quarter, 0))
    back_half = pl.BlockSpec((BLOCK, states), lambda b, s: ((count - 1 - b) % (count // 2), 0))
    state_side = back_lanes(states, state_lanes)
    *feature, extra_pre, feature_cols, state_cols = grid_call(
        functools.partial(feature_body, parts, quarter),
        (count,),
        [pl.BlockSpec((BLOCK, model), back_own), back_part, back_part, back(inner), back(inner), back(128),
         back_half, back_half, state_side[0]] + state_side
        + [whole((8, states)), table(4, states, state_lanes)]
        + [whole((shard, wide + 128))] * parts + [whole((shard, 2 * inner))] * parts,
        dealt_specs + [back(128), whole((8, model)), whole((8, states))],
        dealt_shapes + [shaped((tokens, 128), BF16), shaped((8, model)), shaped((8, states))],
        [pltpu.VMEM((BLOCK, model), F32), pltpu.VMEM((BLOCK + 8, states), F32),
         pltpu.VMEM((BLOCK + 8, states), F32)],
        name="feature",
    )(scalars, hidden, near, far, gate_grad, signal_pre, raw_grad, dbc, dbc_other, conv, u, u, uh, state_ahead,
      taps_x, *ws1, *ws2)
    feature, branch_rest, signal_got = lax.optimization_barrier((feature, across(branch_later, 1), signal_got))
    branch_back = jnp.concatenate(branch_back + [branch_rest])
    feature_theirs = feature[1] + swap(feature[3])
    feature_mine = feature[0] + swap(feature[2])

    folds = model // 128
    extra_small = jnp.concatenate(
        [state_cols[:5], head_cols[:2], jnp.zeros((1, 128), F32), feature_cols[0].reshape(folds, 128)]
    )
    extra, extra_scale = grads([normed], [extra_pre], "grad_extra")
    extra, feature_theirs = lax.optimization_barrier((extra, feature_theirs))
    feature_power = exponents(jnp.max(jnp.abs(feature_theirs), axis=0, keepdims=True))
    feature_back = across(packed(feature_theirs, feature_power, jnp.exp2(-feature_power)), 1)
    signal_total, signal_power, (signal_here,) = totalled(signal, signal_scale, signal_got, [signal_small])
    extra_got = over_sequences(payloads(extra, extra_scale, [extra_small]))
    extra_got, feature_back = lax.optimization_barrier((extra_got, feature_back))
    extra_total, extra_power, (extra_here,) = totalled(extra, extra_scale, extra_got, [extra_small])
    late_power = jnp.concatenate([signal_power, extra_power], axis=1)
    small_here = jnp.concatenate([signal_here, extra_here], axis=1)
    late_cut = chunks([signal_total, extra_total], late_power, [small_here])
    late_far = over_positions(late_cut)
    feature_back = unpacked(feature_back)[0]

    def both_halves(value):
        other = swap(value)
        return jnp.where(core == 0, jnp.concatenate([value, other]), jnp.concatenate([other, value]))

    residual = piece(hidden, core, halfway).astype(F32)
    place = z * steps + core * halfway + lax.broadcasted_iota(jnp.int32, (halfway, 1), 0)
    valid = (place < lengths[0]).astype(F32)
    mixed = both_halves((residual + valid * (branch[0] + swap(branch[2]) + branch_back)).astype(BF16))

    feature_grad = feature_mine + feature_back
    inverse = lax.rsqrt(jnp.mean(residual * residual, axis=1, keepdims=True) + EPSILON)
    scaled_own = residual * inverse
    scaled_grad = feature_grad * norm_gain
    upstream = piece(cotangent, core, halfway).astype(F32)
    grad_hidden = both_halves(
        upstream + inverse * (scaled_grad - scaled_own * jnp.mean(scaled_grad * scaled_own, axis=1, keepdims=True))
    )

    mixed, grad_hidden, late_far = lax.optimization_barrier((mixed, grad_hidden, late_far))
    late_sum = settled(late_cut[0], decoded(late_far, [16]))
    small_sum = settled(small_here, ridden(late_far, [16]))

    def side_by_side(pair):
        return jnp.concatenate(pair, axis=-1)

    signal_small = side_by_side([part[:, :inner] for part in small_sum])
    state_small = side_by_side([part[:8, inner:] for part in small_sum])
    heads_small = [part[5:7, inner + HEAD0 : inner + HEAD0 + heads] for part in small_sum]
    rate_all = -jnp.exp(log_rate)
    skip_sum = signal_small[9].reshape(2 * heads, inner // heads).sum(axis=1)
    gain_here = (small_sum[0] + small_sum[1])[8 : 8 + folds, inner:].reshape(model)
    state_here = jnp.stack([part[:, inner : inner + HEAD0] for part in late_sum])
    gain_there, state_there = swap(gain_here), swap(state_here)
    gain_size = model // (dps * ctxs)
    gain_sum = piece(gain_here + gain_there, dp * ctxs + z, gain_size)
    in_order = jnp.where(
        core == 0, jnp.stack([state_here, state_there], 1), jnp.stack([state_there, state_here], 1)
    )
    state_sum = jnp.transpose(in_order, (2, 0, 1, 3)).reshape(-1, 2 * states)
    main_sum = jnp.stack([gate_sum, side_by_side([part[:, :inner] for part in late_sum])], axis=1)
    delta_sum = side_by_side([part[:, inner + HEAD0 : inner + HEAD0 + heads] for part in late_sum])

    return (
        mixed[None],
        grad_hidden[None],
        gain_sum,
        main_sum,
        state_sum,
        delta_sum,
        signal_small[:4],
        state_small[:4],
        signal_small[4],
        state_small[4],
        side_by_side([part[0] for part in heads_small]),
        side_by_side([part[1] for part in heads_small]) * rate_all,
        skip_sum,
        signal_small[8],
        out_sum,
    )


def solution(mesh):
    in_specs = (
        P("dp", "ctx", None), P("dp"), P("dp", "ctx", None), P(), P("dp", None, "tp"), P("dp", None),
        P("dp", "tp"), P(None, "tp"), P(), P("tp"), P(), P("tp"), P("tp"), P("tp"), P("tp"), P("dp", "tp"),
    )
    out_specs = (
        P("dp", "ctx", None), P("dp", "ctx", None), P(("dp", "ctx")), P(("dp", "ctx"), None, "tp"),
        P(("dp", "ctx"), None), P(("dp", "ctx"), "tp"), P(None, "tp"), P(), P("tp"), P(), P("tp"), P("tp"),
        P("tp"), P("tp"), P(("dp", "ctx"), "tp"),
    )
    return jax.shard_map(
        per_device, mesh=mesh, in_specs=in_specs, out_specs=out_specs, check_vma=False
    )
```

```python
import functools

import jax
import jax.numpy as jnp
from jax import lax
from jax.experimental import pallas as pl
from jax.experimental.pallas import tpu as pltpu
from jax.sharding import PartitionSpec as P

BLOCK = 256
SUB = 128
EPSILON = 1e-05
HIGH = lax.Precision.HIGH
HIGHEST = lax.Precision.HIGHEST
F32 = jnp.float32
BF16 = jnp.bfloat16
F16 = jnp.float16
NN = (((1,), (0,)), ((), ()))
NT = (((1,), (1,)), ((), ()))
TN = (((0,), (0,)), ((), ()))
HEAD0 = 64
STEP = 16
LO, CORE, BASE, LENGTH, HASPREV, HASNEXT, SLOT0 = range(7)


def mm(a, b, dims=NN, precision=None):
    return lax.dot_general(a, b, dims, precision=precision, preferred_element_type=F32)


def grid_call(body, grid, in_specs, out_specs, out_shape, scratch=(), name=None, limit=None):
    return pl.pallas_call(
        body,
        grid_spec=pltpu.PrefetchScalarGridSpec(
            num_scalar_prefetch=1,
            grid=grid,
            in_specs=in_specs,
            out_specs=out_specs,
            scratch_shapes=list(scratch),
        ),
        out_shape=out_shape,
        compiler_params=pltpu.CompilerParams(
            dimension_semantics=("arbitrary",) * len(grid), vmem_limit_bytes=limit
        ),
        name=name,
    )


def streamed(*arrays):
    return [pltpu.with_memory_space_constraint(array, pltpu.HBM) for array in arrays]


def rows_spec(width, rows=BLOCK, lane=0):
    return pl.BlockSpec((rows, width), lambda b, s: (b, lane))


def whole(shape):
    return pl.BlockSpec(shape, lambda b, s: (0,) * len(shape))


def shaped(shape, dtype=F32):
    return jax.ShapeDtypeStruct(shape, dtype)


def kept(shape, dtype=F32):
    return pltpu.HBM(shape, dtype)


def slope(v, sig):
    return sig * (1.0 + v * (1.0 - sig))


def lanes_of(s_ref, slot, width):
    return pl.ds(pl.multiple_of(s_ref[SLOT0 + slot] * width, width), width)


def normalize(x, gain):
    value = x.astype(F32)
    inverse = lax.rsqrt(jnp.mean(value * value, axis=1, keepdims=True) + EPSILON)
    scaled = value * inverse
    return scaled, (scaled * gain).astype(BF16)


def pick(s_ref, b, quarter, own, near, far):
    lo, core = s_ref[LO], s_ref[CORE]
    place = b // quarter
    mine = (place // 2) == lo
    from_near = (place % 2) == core
    return jnp.where(mine, own, jnp.where(from_near, near, far))


def valid_rows(s_ref, b):
    position = s_ref[BASE] + b * BLOCK + lax.broadcasted_iota(jnp.int32, (BLOCK, 1), 0)
    return (position < s_ref[LENGTH]).astype(F32)


def expander(inner, shift=0):
    lane = lax.broadcasted_iota(jnp.int32, (384, inner), 0) % 128 - HEAD0 - shift
    head = lax.broadcasted_iota(jnp.int32, (384, inner), 1) // 64
    return (lane == head).astype(F32).astype(BF16)


def collector(inner):
    head = lax.broadcasted_iota(jnp.int32, (3 * inner, 128), 0) % inner // 64
    lane = lax.broadcasted_iota(jnp.int32, (3 * inner, 128), 1) - HEAD0
    return (lane == head).astype(F32).astype(BF16)


def two(x):
    high = x.astype(BF16)
    return high, (x - high.astype(F32)).astype(BF16)


def three(x, axis=1):
    high = x.astype(BF16)
    rest = x - high.astype(F32)
    middle = rest.astype(BF16)
    return jnp.concatenate([high, middle, (rest - middle.astype(F32)).astype(BF16)], axis=axis)


def running(tri, x):
    width = x.shape[1]
    wide = mm(tri, three(x))
    return wide[:, :width] + wide[:, width : 2 * width] + wide[:, 2 * width :]


def triangle(forward):
    row = lax.broadcasted_iota(jnp.int32, (BLOCK, BLOCK), 0)
    col = lax.broadcasted_iota(jnp.int32, (BLOCK, BLOCK), 1)
    same = (row // SUB) == (col // SUB)
    keep = (row >= col) if forward else (col >= row)
    return (same & keep).astype(F32).astype(BF16)


def stacked_heads(x):
    half = lax.broadcasted_iota(jnp.int32, (1, 128), 1) < 64
    return two(jnp.concatenate([jnp.where(half, x, 0.0), jnp.where(half, 0.0, x)], axis=0))


def faded(keep, level, level_t, level_x, pair, forward):
    out = []
    for side in range(2):
        h = HEAD0 + 2 * pair + side
        at = pair * 128 + side * 64
        column, row = level_x[:, at : at + 1], level_t[h : h + 1, :]
        diff = column - row if forward else row - column
        out.append(jnp.exp(jnp.where(keep, diff, -1e30)))
    return jnp.concatenate(out, axis=1)


def mixed_heads(mix, high, low):
    mh, ml = two(mix)
    wide = mm(mh, jnp.concatenate([high, low], axis=1))
    return wide[:, :128] + wide[:, 128:] + mm(ml, high)


def head_lanes(inner):
    lane = lax.broadcasted_iota(jnp.int32, (1, 128), 1)
    return (lane >= HEAD0) & (lane < HEAD0 + inner // 64)


def front_body(parts, inner, states, quarter, s_ref, own, near, far, halo, gain, taps, bias, dbias, rate,
               *rest):
    ws = rest[:parts]
    normed_ref, u_ref, uh_ref, co_ref, hd_ref, hloc_ref, pre_ref, end_ref = rest[parts : parts + 8]
    hsc, usc, state, pre, esc, wsc = rest[parts + 8 :]
    b = pl.program_id(0)
    wide = inner + 2 * states
    shard = ws[0].shape[0]
    normed_ref[...] = normalize(pick(s_ref, b, quarter, own[...], near[...], far[...]), gain[...])[1]

    @pl.when(b == 0)
    def _():
        hsc[...] = normalize(halo[...], gain[...])[1]
        for j in range(parts):
            wsc[lanes_of(s_ref, j, shard)] = ws[j][...]
        edge = mm(hsc[...], wsc[:, :wide])
        edge = jnp.where(s_ref[HASPREV] > 0, edge[8:], 0.0)
        usc[0:8] = edge
        uh_ref[...] = edge
        state[...] = jnp.zeros_like(state)
        pre[...] = jnp.zeros_like(pre)
        esc[...] = expander(inner)

    @pl.when(b > 0)
    def _():
        usc[0:8] = usc[BLOCK : BLOCK + 8]

    u = mm(normed_ref[...], wsc[...])
    usc[8 : 8 + BLOCK] = u[:, :wide]
    u_ref[...] = u[:, :wide]
    conv = bias[...] + taps[0:1] * usc[5 : 5 + BLOCK]
    for k in range(1, 4):
        conv = conv + taps[k : k + 1] * usc[5 + k : 5 + k + BLOCK]
    co_ref[...] = conv
    raw = u[:, wide:] + dbias[...]
    delta = jnp.where(head_lanes(inner), jnp.maximum(raw, 0.0) + jnp.log1p(jnp.exp(-jnp.abs(raw))), 0.0)
    delta = delta * valid_rows(s_ref, b)
    level = running(triangle(True), delta * rate[...])
    raw = jnp.where(head_lanes(inner), raw, 0.0)
    hd_ref[...] = level + pltpu.roll(delta, STEP, 1) + pltpu.roll(raw, 2 * STEP, 1)
    both = mm(jnp.concatenate([three(level), three(delta)], axis=0), esc[...])
    level_x, delta_x = both[:BLOCK], both[BLOCK:]
    act = conv * jax.nn.sigmoid(conv)
    source = delta_x * act[:, :inner]
    inject_t = act[:, inner : inner + states].T
    for i in range(BLOCK // SUB):
        at = slice(i * SUB, (i + 1) * SUB)
        last = level_x[(i + 1) * SUB - 1 : (i + 1) * SUB]
        fresh = mm(inject_t[:, at], jnp.exp(last - level_x[at]) * source[at], precision=HIGH)
        before = state[...]
        n = b * (BLOCK // SUB) + i
        hloc_ref[i] = before
        pre_ref[n] = pre[...]
        state[...] = jnp.exp(last) * before + fresh
        pre[...] = pre[...] + last

    @pl.when(b == pl.num_programs(0) - 1)
    def _():
        end_ref[...] = state[...]
        pre_ref[n + 1] = pre[...]


def start_expanders(inner, *scs):
    @pl.when(pl.program_id(0) == 0)
    def _():
        for shift, sc in scs:
            sc[...] = expander(inner, shift)


def within_body(inner, states, s_ref, co, hd, yw_ref, lsc, dsc):
    start_expanders(inner, (0, lsc), (STEP, dsc))
    conv = co[...]
    act = conv * jax.nn.sigmoid(conv)
    level = hd[...]
    exact = three(level)
    lx = mm(exact, lsc[...])
    xs = mm(exact, dsc[...]) * act[:, :inner]
    keep = lax.broadcasted_iota(jnp.int32, (SUB, SUB), 0) >= lax.broadcasted_iota(jnp.int32, (SUB, SUB), 1)
    for i in range(BLOCK // SUB):
        at = slice(i * SUB, (i + 1) * SUB)
        affinity = mm(act[at, inner + states :], act[at, inner : inner + states], NT, HIGH)
        affinity = jnp.concatenate([affinity, affinity], axis=1)
        level_t = level[at].T
        level_x = lx[at]
        for pair in range(inner // 128):
            lanes = slice(pair * 128, pair * 128 + 128)
            mix = faded(keep, level, level_t, level_x, pair, True) * affinity
            yw_ref[at, lanes] = mixed_heads(mix, *stacked_heads(xs[at, lanes]))


def gates_body(parts, quarter, s_ref, normed, own, near, far, *rest):
    ws = rest[:parts]
    gate_ref, gg_ref, bg_ref, wsc = rest[parts:]
    b = pl.program_id(0)
    shard = ws[0].shape[0]
    inner = gate_ref.shape[1]
    up = pick(s_ref, b, quarter, own[...], near[...], far[...])
    bg_ref[...] = (up.astype(F32) * valid_rows(s_ref, b)).astype(BF16)

    @pl.when(b == 0)
    def _():
        for j in range(parts):
            wsc[lanes_of(s_ref, j, shard)] = ws[j][...]

    gate_ref[...] = mm(normed[...], wsc[:, :inner])
    gg_ref[...] = mm(bg_ref[...], wsc[:, inner:])


def entering(hloc, pre, hin):
    return hloc + jnp.exp(pre[0:1]) * hin


def output_body(inner, states, s_ref, co, hd, yw, gate, gg, hloc, pre, hin, skip, ggain, y_ref, sum_ref, lsc):
    start_expanders(inner, (0, lsc))
    lx = mm(three(hd[...]), lsc[...])
    conv = co[...]
    act = conv * jax.nn.sigmoid(conv)
    for i in range(BLOCK // SUB):
        at = slice(i * SUB, (i + 1) * SUB)
        held = entering(hloc[i], pre[i], hin[...])
        y_ref[at] = yw[at] + jnp.exp(lx[at]) * mm(act[at, inner + states :], held, precision=HIGH)
    out = y_ref[...] + skip[...] * act[:, :inner]
    g = gate[...]
    product = out * (g * jax.nn.sigmoid(g))
    ones = jnp.ones((8, 3 * inner), BF16)
    sum_ref[0:8] = mm(ones, three(product * product), NT)
    sum_ref[8:16] = mm(ones, three(gg[...] * ggain[...] * product), NT)


def turn_body(inner, states, total, s_ref, co, hd, y, gate, gg, sums, sums1, sums2, sums3, skip, ggain,
              gated_ref, ggrad_ref, og_ref, gloc_ref, start_ref, cols_ref, chain, lsc):
    start_expanders(inner, (0, lsc))
    lx = mm(three(hd[...]), lsc[...])
    step = pl.program_id(0)
    conv = co[...]
    act = conv * jax.nn.sigmoid(conv)
    x = act[:, :inner]
    readout_t = act[:, inner + states :].T
    both = (sums[...] + sums1[...] + sums2[...] + sums3[...]).T
    ginv = lax.rsqrt(both[:, 0:1] / total + EPSILON)
    dot = ginv * both[:, 8:9] / total
    g = gate[...]
    sig = jax.nn.sigmoid(g)
    ga = g * sig
    out = y[...] + skip[...] * x
    unit = out * ga * ginv
    gated_ref[...] = (unit * ggain[...]).astype(BF16)
    grad = gg[...]
    pg = ginv * (grad * ggain[...] - unit * dot)
    og = pg * ga
    og_ref[...] = og
    ggrad_ref[...] = (pg * out * slope(g, sig)).astype(BF16)

    @pl.when(step == 0)
    def _():
        chain[...] = jnp.zeros_like(chain)
        cols_ref[...] = jnp.zeros_like(cols_ref)

    cols_ref[0:1] += jnp.sum(grad * unit, axis=0, keepdims=True)
    cols_ref[1:2] += jnp.sum(og * x, axis=0, keepdims=True)
    b = pl.num_programs(0) - 1 - step
    for i in reversed(range(BLOCK // SUB)):
        at = slice(i * SUB, (i + 1) * SUB)
        held = chain[...]
        gloc_ref[i] = held
        level_x = lx[at]
        chain[...] = jnp.exp(level_x[SUB - 1 : SUB]) * held + mm(
            readout_t[:, at], jnp.exp(level_x) * og[at], precision=HIGH
        )

    @pl.when(b == 0)
    def _():
        start_ref[...] = chain[...]


def back_body(inner, states, s_ref, co, hd, og, hloc, pre, hin, z_ref, dbc_ref, lsc, dsc):
    start_expanders(inner, (0, lsc), (STEP, dsc))
    conv = co[...]
    act = conv * jax.nn.sigmoid(conv)
    level = hd[...]
    exact = three(level)
    lx = mm(exact, lsc[...])
    xs = mm(exact, dsc[...]) * act[:, :inner]
    keep = lax.broadcasted_iota(jnp.int32, (SUB, SUB), 1) >= lax.broadcasted_iota(jnp.int32, (SUB, SUB), 0)
    for i in range(BLOCK // SUB):
        at = slice(i * SUB, (i + 1) * SUB)
        inject, readout = act[at, inner : inner + states], act[at, inner + states :]
        affinity = mm(inject, readout, NT, HIGH)
        affinity = jnp.concatenate([affinity, affinity], axis=1)
        level_t = level[at].T
        level_x = lx[at]
        grad = jnp.zeros((SUB, SUB), F32)
        for pair in range(inner // 128):
            lanes = slice(pair * 128, pair * 128 + 128)
            fade = faded(keep, level, level_t, level_x, pair, False)
            g = og[at, lanes]
            z_ref[at, lanes] = mixed_heads(fade * affinity, *stacked_heads(g))
            xh, xl = stacked_heads(xs[at, lanes])
            gh, gl = two(g)
            outer = mm(
                jnp.concatenate([xh, xl], axis=1), jnp.concatenate([gh, gh], axis=1), NT
            ) + mm(xh, gl, NT)
            grad += fade[:, :SUB] * outer[:SUB] + fade[:, SUB:] * outer[SUB:]
        held = entering(hloc[i], pre[i], hin[...])
        dbc_ref[at, :states] = mm(grad, readout, precision=HIGH)
        dbc_ref[at, states:] = mm(grad.T, inject, precision=HIGH) + mm(
            jnp.exp(level_x) * og[at], held, NT, HIGH
        )


def conv_back(grad, csc, usc, taps, cols_ref):
    csc[0:BLOCK] = grad
    pre = taps[0:1] * csc[3 : 3 + BLOCK]
    for k in range(1, 4):
        pre = pre + taps[k : k + 1] * csc[3 - k : 3 - k + BLOCK]
    for k in range(4):
        cols_ref[k : k + 1] += jnp.sum(grad * usc[5 + k : 5 + k + BLOCK], axis=0, keepdims=True)
    cols_ref[4:5] += jnp.sum(grad, axis=0, keepdims=True)
    csc[BLOCK : BLOCK + 8] = grad[0:8]
    return pre


def meet_body(inner, states, s_ref, co, hd, z, dbc, hloc, hnext, hend, pre, gloc, gin, hin, zed_ref, ends_ref, keep_ref,
              give_ref, lsc, dsc):
    start_expanders(inner, (0, lsc), (STEP, dsc))
    exact = three(hd[...])
    lx = mm(exact, lsc[...])
    subs = BLOCK // SUB
    count = pl.num_programs(0)
    b = pl.program_id(0)
    conv = co[...]
    act = conv * jax.nn.sigmoid(conv)
    source = mm(exact, dsc[...]) * act[:, :inner]
    ends = []
    inject_grads = []
    for i in range(subs):
        at = slice(i * SUB, (i + 1) * SUB)
        n = b * subs + i + 1
        level_x = lx[at]
        later = gloc[i] + jnp.exp(pre[subs * count][0:1] - pre[n][0:1]) * gin[...]
        after = hloc[i + 1] if i < subs - 1 else jnp.where(b == count - 1, hend[...], hnext[0])
        fade = jnp.exp(level_x[SUB - 1 : SUB] - level_x)
        zed_ref[at] = z[at] + fade * mm(act[at, inner : inner + states], later, precision=HIGH)
        inject_grads.append(dbc[at, :states] + mm(fade * source[at], later, NT, HIGH))
        ends.append(jnp.sum(later * entering(after, pre[n], hin[...]), axis=0, keepdims=True))
    ends_ref[...] = jnp.concatenate(ends + [jnp.zeros((8 - subs, inner), F32)], axis=0)
    inject_grad = jnp.concatenate(inject_grads, axis=0)
    half = count // 2
    rows = pl.ds(pl.multiple_of((b % half) * BLOCK, BLOCK), BLOCK)

    @pl.when(b // half == s_ref[CORE])
    def _():
        keep_ref[rows, :states] = inject_grad
        keep_ref[rows, states:] = dbc[:, states:]

    @pl.when(b // half != s_ref[CORE])
    def _():
        give_ref[rows, :states] = inject_grad
        give_ref[rows, states:] = dbc[:, states:]


def join_body(inner, s_ref, co, hd, og, y, zed_in, ends_in, u, prior, uh, taps, rate, skip, mg_ref,
              tail_ref, head_ref, rg_ref, cols_ref, sig_ref, col_sc, csc, usc, dsc):
    start_expanders(inner, (STEP, dsc))
    step = pl.program_id(0)
    subs = BLOCK // SUB
    count = pl.num_programs(0)
    b = count - 1 - step

    @pl.when(step == 0)
    def _():
        cols_ref[...] = jnp.zeros_like(cols_ref)
        sig_ref[...] = jnp.zeros_like(sig_ref)
        col_sc[...] = collector(inner)
        csc[BLOCK : BLOCK + 8] = jnp.zeros((8, inner), F32)

    conv = co[...]
    sig = jax.nn.sigmoid(conv)
    x = conv * sig
    packed_heads = hd[...]
    delta_x = mm(three(packed_heads), dsc[...])
    zed = zed_in[...]
    ends = ends_in[...]
    g = og[...]
    sums = mm(three(jnp.concatenate([x * zed, g * y[...], ends], axis=0)), col_sc[...])
    direct, read, ends = sums[:BLOCK], sums[BLOCK : 2 * BLOCK], sums[2 * BLOCK :]
    dlt = jnp.where(head_lanes(inner), pltpu.roll(packed_heads, 128 - STEP, 1), 0.0)
    draw = pltpu.roll(packed_heads, 128 - 2 * STEP, 1)
    q = running(triangle(False), read - dlt * direct)
    q = jnp.concatenate([q[i * SUB : (i + 1) * SUB] + ends[i : i + 1] for i in range(subs)], axis=0)
    rg = (direct + rate[...] * q) * valid_rows(s_ref, b) * jax.nn.sigmoid(draw)
    rg = jnp.where(head_lanes(inner), rg, 0.0)
    rg_ref[...] = rg
    cols_ref[0:1] += jnp.sum(rg, axis=0, keepdims=True)
    cols_ref[1:2] += jnp.sum(dlt * q, axis=0, keepdims=True)

    usc[0:8] = jnp.where(b == 0, uh[...], prior[...])
    usc[8 : 8 + BLOCK] = u[...]
    grad = (delta_x * zed + skip[...] * g) * slope(conv, sig)
    pre_grad = conv_back(grad, csc, usc, taps, sig_ref)
    mg_ref[...] = pre_grad.astype(BF16)
    head_ref[...] = grad[0:8]

    @pl.when(step == 0)
    def _():
        tail_ref[...] = pre_grad[BLOCK - 8 :]


def exponents(peak):
    return jnp.clip(jnp.ceil(jnp.log(jnp.maximum(peak, 1e-36)) * 1.4426950408889634) - 14.0, -100.0, 100.0)


def packed(value, power, inverse, riders=()):
    rows = [(value * inverse).astype(F16), jnp.broadcast_to(power, (16, value.shape[1])).astype(F16)]
    for more in riders:
        each = exponents(jnp.abs(more))
        rows += [(more * jnp.exp2(-each)).astype(F16), each.astype(F16)]
    return jnp.concatenate(rows)


def unpacked(sent, counts=()):
    rows = sent.shape[0] - 16 - 2 * sum(counts)
    power = sent[rows : rows + 1].astype(F32)
    more = []
    at = rows + 16
    for size in counts:
        more.append(sent[at : at + size].astype(F32) * jnp.exp2(sent[at + size : at + 2 * size].astype(F32)))
        at += 2 * size
    return sent[:rows].astype(F32) * jnp.exp2(power), power, more


def grads_body(parts, pairs, s_ref, *refs):
    inputs = 1 + max(max(pair) for pair in pairs)
    outs = refs[inputs : inputs + parts]
    powers, inverse, peak = refs[inputs + parts :]
    j = pl.program_id(0)

    @pl.when(j == 0)
    def _():
        peak[...] = jnp.zeros_like(peak)

    at = 0
    for left, right in pairs:
        value = mm(refs[left][...], refs[right][...], TN)
        lanes = slice(at, at + value.shape[1])
        at += value.shape[1]
        peak[0:1, lanes] = jnp.maximum(peak[0:1, lanes], jnp.max(jnp.abs(value), axis=0, keepdims=True))
        for k in range(parts):

            @pl.when(j == k)
            def _():
                outs[k][:, lanes] = value

    @pl.when(j == parts - 1)
    def _():
        power = exponents(peak[...])
        powers[...] = jnp.broadcast_to(power[0:1], (16, at))
        inverse[...] = jnp.exp2(-power[0:1])


def deal(s_ref, b, quarter, value, outs):
    place = b // quarter
    rows = pl.ds(pl.multiple_of((b % quarter) * BLOCK, BLOCK), BLOCK)
    at = (place % 2 != s_ref[CORE]).astype(jnp.int32) * 2 + (place // 2 != s_ref[LO]).astype(jnp.int32)
    for k in range(4):

        @pl.when(at == k)
        def _():
            outs[k][rows] = value


def feature_body(parts, quarter, s_ref, own, near, far, ggrad, mg, rg, dbc, dbc_other, co, u, prior, uh, ahead,
                 taps, *rest):
    ws1 = rest[:parts]
    ws2 = rest[parts : 2 * parts]
    outs = rest[2 * parts : 2 * parts + 4]
    xg_ref, cols_ref, state_ref, whole_sc, csc, usc = rest[2 * parts + 4 :]
    step = pl.program_id(0)
    count = pl.num_programs(0)
    b = count - 1 - step
    inner = ggrad.shape[1]
    shard = ws1[0].shape[0]

    @pl.when(step == 0)
    def _():
        cols_ref[...] = jnp.zeros_like(cols_ref)
        state_ref[...] = jnp.zeros_like(state_ref)
        csc[BLOCK : BLOCK + 8] = jnp.where(s_ref[HASNEXT] > 0, ahead[...], 0.0)

    usc[0:8] = jnp.where(b == 0, uh[...], prior[...])
    usc[8 : 8 + BLOCK] = u[...]
    conv = co[...]
    grad = jnp.where(b // (count // 2) == s_ref[CORE], dbc[...], dbc_other[...])
    grad = grad * slope(conv, jax.nn.sigmoid(conv))
    pre = conv_back(grad, csc, usc, taps, state_ref)
    pre = jnp.where(s_ref[CORE] > 0, pltpu.roll(pre, 64, 1), pre)
    lane = lax.broadcasted_iota(jnp.int32, (BLOCK, 128), 1)
    xg = jnp.where(lane < HEAD0, pre, rg[...]).astype(BF16)
    xg_ref[...] = xg
    for j in range(parts):
        at = lanes_of(s_ref, j, shard)
        whole_sc[:, at] = (
            mm(ggrad[...], ws2[j][:, :inner], NT)
            + mm(mg[...], ws1[j][:, :inner], NT)
            + mm(xg, ws1[j][:, -128:], NT)
        )
    value = whole_sc[...]
    scaled = normalize(pick(s_ref, b, quarter, own[...], near[...], far[...]), 1.0)[0]
    cols_ref[0:1] += jnp.sum(value * scaled, axis=0, keepdims=True)
    deal(s_ref, b, quarter, value, outs)


def branch_body(parts, quarter, s_ref, gated, *rest):
    ws2 = rest[:parts]
    outs = rest[parts : parts + 4]
    whole_sc = rest[parts + 4]
    inner = gated.shape[1]
    shard = ws2[0].shape[0]
    for j in range(parts):
        whole_sc[:, lanes_of(s_ref, j, shard)] = mm(gated[...], ws2[j][:, inner:], NT)
    deal(s_ref, pl.program_id(0), quarter, whole_sc[...], outs)


def finish_body(inner, s_ref, first, second, rate, taps_ref, bias_ref, gain_ref, staps_ref, sbias_ref, raw_ref,
                rate_ref, skip_ref, norm_ref):
    both = (first, second)
    heads = inner // 64
    lane = lax.broadcasted_iota(jnp.int32, (8, 128), 1)
    pairs, skips = [], []
    for n, part in enumerate(both):
        at = slice(n * inner, (n + 1) * inner)
        taps_ref[:, at] = part[0:4, :inner]
        bias_ref[:, at] = part[4:5, :inner]
        gain_ref[:, at] = part[8:9, :inner]
        here = slice(n * 128, (n + 1) * 128)
        staps_ref[:, here] = part[0:4, inner:]
        sbias_ref[:, here] = part[4:5, inner:]
        turn = (128 - HEAD0 + n * heads) % 128
        pairs.append(pltpu.roll(part[0:8, inner:], turn, 1))
        skips.append(pltpu.roll(mm(three(part[8:16, :inner]), collector(inner)), turn, 1))
    values = jnp.where(lane < heads, pairs[0], pairs[1])
    skip = jnp.where(lane < heads, skips[0], skips[1])
    raw_ref[...] = values[5:6, : 2 * heads]
    rate_ref[...] = values[6:7, : 2 * heads] * rate[...]
    skip_ref[...] = skip[1:2, : 2 * heads]
    norm_ref[...] = first[8:16, inner:] + second[8:16, inner:]


def per_device(
    hidden, lengths, cotangent, norm_gain, proj_main, proj_state, proj_delta, conv_main, conv_state,
    bias_main, bias_state, delta_bias, log_rate, skip_gain, gate_gain, proj_out,
):
    _, steps, model = hidden.shape
    hidden, cotangent = hidden[0], cotangent[0]
    dps, ctxs, tps = lax.axis_size("dp"), lax.axis_size("ctx"), lax.axis_size("tp")
    dp, z, core = lax.axis_index("dp"), lax.axis_index("ctx"), lax.axis_index("tp")
    lo, hi = z % 2, z // 2
    pairs = ctxs // 2
    tokens = 2 * steps
    count = tokens // BLOCK
    quarter = count // 4
    inner = bias_main.shape[0] // 2
    heads = delta_bias.shape[0] // 2
    states = bias_state.shape[0] // 2
    wide = inner + 2 * states

    def swap(value):
        return lax.ppermute(value, "tp", [(0, 1), (1, 0)])

    def across(value, j):
        return lax.ppermute(value, "ctx", [(i, i ^ j) for i in range(ctxs)])

    def along(value, step):
        return lax.ppermute(
            value, "ctx", [(i, i + step) for i in range(ctxs) if 0 <= i + step < ctxs]
        )

    def spread(value, j):
        return lax.ppermute(value, "dp", [(i, i ^ j) for i in range(dps)])

    def mine(value, axis, size):
        return lax.dynamic_slice_in_dim(value, lo * size, size, axis)

    def piece(value, at, size):
        return lax.dynamic_slice_in_dim(value, at * size, size, 0)

    apart = proj_main.shape[0] % 128 == 0
    parts = dps if apart else 1
    shard = proj_main.shape[0] * (dps // parts)

    def gathered(value):
        if not apart:
            return [lax.all_gather(value, "dp", axis=0, tiled=True)]
        return [value] + [spread(value, j) for j in range(1, dps)]

    scalars = jnp.stack(
        [lo, core, hi * tokens, lengths[0], (hi > 0).astype(jnp.int32), (hi < pairs - 1).astype(jnp.int32)]
        + [dp ^ j if apart else 0 * dp for j in range(parts)]
    ).astype(jnp.int32)

    state_own = lax.dynamic_slice_in_dim(proj_state, lo * states + core * (states // 2), states // 2, 1)
    delta_own = mine(proj_delta, 1, heads)
    main_part = mine(proj_main, 2, inner)
    first = jnp.concatenate(
        [main_part[:, 1], proj_state, state_own, delta_own,
         jnp.zeros((proj_main.shape[0], 64 - heads), BF16)], axis=1
    )
    halfway = steps // 2
    near = across(piece(hidden, core, halfway), 1)
    far = swap(near)
    ws1 = gathered(first)

    def payloads(pieces, scale, riders=()):
        return [packed(pieces[j], scale[0], scale[1], riders) for j in range(1, parts)]

    def over_sequences(payload):
        return [spread(payload[j - 1], j) for j in range(1, parts)]

    def totalled(pieces, scale, got, riders=()):
        total, power = pieces[0], scale[0][0:1]
        if not apart:
            total = lax.psum_scatter(total, "dp", scatter_dimension=0, tiled=True)
            power = exponents(jnp.max(jnp.abs(total), axis=0, keepdims=True))
            riders = [lax.psum(value, "dp") for value in riders]
        for sent in got:
            value, other, more = unpacked(sent, [rider.shape[0] for rider in riders])
            total, power = total + value, jnp.maximum(power, other)
            riders = [one + two for one, two in zip(riders, more)]
        return total, power + (parts - 1).bit_length(), riders

    def chunks(totals, power, riders=()):
        size = totals[0].shape[0] // ctxs
        rows = [jnp.concatenate([piece(total, z ^ j, size) for total in totals], axis=1) for j in range(ctxs)]
        return rows[:1] + [packed(value, power, jnp.exp2(-power), riders) for value in rows[1:]]

    def over_positions(cut):
        return [across(cut[j], j) for j in range(1, ctxs)]

    def settled(own, got):
        opposite = got[0]
        for j in range(2, ctxs):
            if j % 2 == 0:
                own = own + got[j - 1]
            else:
                opposite = opposite + got[j - 1]
        return jnp.where(lo == 0, own, opposite), jnp.where(lo == 0, opposite, own)

    def decoded(got, counts=()):
        return [unpacked(sent, counts)[0] for sent in got]

    def ridden(got, counts):
        return [unpacked(sent, counts)[2][0] for sent in got]

    taps_x = jnp.concatenate([mine(conv_main, 1, inner), conv_state], axis=1)
    bias_x = jnp.concatenate([mine(bias_main, 0, inner), bias_state])[None]
    rate_own = -jnp.exp(mine(log_rate, 0, heads))

    def in_heads(value):
        return jnp.pad(value, (HEAD0, 128 - HEAD0 - heads))[None]

    rate_row = in_heads(rate_own)
    dbias_row = in_heads(mine(delta_bias, 0, heads))
    skip_row = jnp.repeat(mine(skip_gain, 0, heads), inner // heads)[None]
    ggain_row = mine(gate_gain, 0, inner)[None]
    gain_row = norm_gain[None]
    edge, scalars, taps_x, bias_x, rate_row, dbias_row, _ = lax.optimization_barrier(
        (hidden[steps - 16 :], scalars, taps_x, bias_x, rate_row, dbias_row, first)
    )
    route = [
        ((z0 - 1) * tps + c, (z0 + c) * tps + c) for z0 in range(2, ctxs, 2) for c in range(2)
    ]
    edge = lax.ppermute(edge, ("ctx", "tp"), route)
    halo = jnp.where(core == lo, edge, swap(edge))

    near, cot_later = lax.optimization_barrier((near, cotangent))
    ws1, near, main_gate, out_later = lax.optimization_barrier((ws1, near, main_part[:, 0], proj_out))
    second = jnp.concatenate([main_gate, mine(out_later, 1, inner)], axis=1)
    ws2 = gathered(second)
    cot_near = across(piece(cot_later, core, halfway), 1)

    own_spec = pl.BlockSpec(
        (BLOCK, model), lambda b, s: (jnp.clip(b - s[LO] * 2 * quarter, 0, 2 * quarter - 1), 0)
    )
    part_spec = pl.BlockSpec((BLOCK, model), lambda b, s: (b % quarter, 0))
    subs = BLOCK // SUB
    last = count * subs
    state_block = pl.BlockSpec((subs, states, inner), lambda b, s: (b, 0, 0))
    pre_block = pl.BlockSpec((subs, 8, inner), lambda b, s: (b, 0, 0))

    normed, u, uh, conv, per_head, hloc, pre, own_end = grid_call(
        functools.partial(front_body, parts, inner, states, quarter),
        (count,),
        [own_spec, part_spec, part_spec, whole((16, model)), whole((1, model)), whole((4, wide)),
         whole((1, wide)), whole((1, 128)), whole((1, 128))] + [whole((shard, wide + 128))] * parts,
        [rows_spec(model), rows_spec(wide), whole((8, wide)), rows_spec(wide), rows_spec(128),
         state_block, whole((last + 1, 8, inner)), whole((states, inner))],
        [shaped((tokens, model), BF16), shaped((tokens, wide)), shaped((8, wide)), shaped((tokens, wide)),
         shaped((tokens, 128)), shaped((last, states, inner)), shaped((last + 1, 8, inner)),
         shaped((states, inner))],
        [pltpu.VMEM((16, model), BF16), pltpu.VMEM((8 + BLOCK, wide), F32), pltpu.VMEM((states, inner), F32),
         pltpu.VMEM((8, inner), F32), pltpu.VMEM((384, inner), BF16), pltpu.VMEM((model, wide + 128), BF16)],
        name="front",
    )(scalars, hidden, near, far, halo, gain_row, taps_x, bias_x, dbias_row, rate_row, *ws1)

    cot_near, own_end = lax.optimization_barrier((cot_near, own_end))
    cot_far = swap(cot_near)
    growth = jnp.exp(pre[last][0:1])
    carried = jnp.zeros_like(own_end)
    sending = own_end
    for hop in range(pairs - 1):
        carried = along(sending, 2)
        if hop < pairs - 2:
            sending = own_end + growth * carried

    (inside,) = grid_call(
        functools.partial(within_body, inner, states),
        (count,),
        [rows_spec(wide), rows_spec(128)],
        [rows_spec(inner)],
        [shaped((tokens, inner))],
        [pltpu.VMEM((384, inner), BF16)] * 2,
        name="within",
        limit=20 << 20,
    )(scalars, *streamed(conv, per_head))

    gate, gated_grad, branch_grad = grid_call(
        functools.partial(gates_body, parts, quarter),
        (count,),
        [rows_spec(model), own_spec, part_spec, part_spec] + [whole((shard, 2 * inner))] * parts,
        [rows_spec(inner), rows_spec(inner), rows_spec(model)],
        [shaped((tokens, inner)), shaped((tokens, inner)), shaped((tokens, model), BF16)],
        [pltpu.VMEM((model, 2 * inner), BF16)],
        name="gates",
        limit=20 << 20,
    )(scalars, *streamed(normed, cotangent, cot_near, cot_far, *ws2))

    y, sums = grid_call(
        functools.partial(output_body, inner, states),
        (count,),
        [rows_spec(wide), rows_spec(128), rows_spec(inner), rows_spec(inner), rows_spec(inner), state_block,
         pre_block, whole((states, inner)), whole((1, inner)), whole((1, inner))],
        [rows_spec(inner), pl.BlockSpec((16, BLOCK), lambda b, s: (0, b))],
        [shaped((tokens, inner)), shaped((16, tokens))],
        [pltpu.VMEM((384, inner), BF16)],
        name="output",
        limit=20 << 20,
    )(scalars, *streamed(conv, per_head), inside, gate, gated_grad, *streamed(hloc), pre, carried, skip_row, ggain_row)

    corner = [(n, ((n // tps) ^ 1) * tps + (n % tps + 1) % tps) for n in range(ctxs * tps)]
    all_sums = [sums, swap(sums), across(sums, 1), lax.ppermute(sums, ("ctx", "tp"), corner)]

    def back(width, rows=BLOCK):
        return pl.BlockSpec((rows, width), lambda b, s: (count - 1 - b, 0))

    back_sums = pl.BlockSpec((16, BLOCK), lambda b, s: (0, count - 1 - b))
    gated, gate_grad, out_grad, gloc, own_start, turn_cols = grid_call(
        functools.partial(turn_body, inner, states, 2 * tps * inner),
        (count,),
        [back(wide), back(128), back(inner), back(inner), back(inner),
         back_sums, back_sums, back_sums, back_sums, whole((1, inner)), whole((1, inner))],
        [back(inner), back(inner), back(inner),
         pl.BlockSpec((subs, states, inner), lambda b, s: (count - 1 - b, 0, 0)), whole((states, inner)),
         whole((8, inner))],
        [shaped((tokens, inner), BF16), shaped((tokens, inner), BF16), kept((tokens, inner)),
         kept((last, states, inner)), shaped((states, inner)), shaped((8, inner))],
        [pltpu.VMEM((states, inner), F32), pltpu.VMEM((384, inner), BF16)],
        name="turn",
        limit=20 << 20,
    )(scalars, *streamed(conv, per_head), y, gate, gated_grad, *all_sums, skip_row, ggain_row)

    returned = jnp.zeros_like(own_start)
    sending = own_start
    for hop in range(pairs - 1):
        returned = along(sending, -2)
        if hop < pairs - 2:
            sending = own_start + growth * returned

    turned = pl.BlockSpec((tokens, shard), lambda j, s: (0, s[SLOT0 + j]))
    dealt_specs = [whole((halfway, model))] * 4
    dealt_shapes = [shaped((halfway, model))] * 4
    def grads(lefts, rights, name, limit=None):
        sources = []
        for left, right in zip(lefts, rights):
            sources += [left, right]
        width = sum(right.shape[1] for right in rights)
        specs = [turned if n % 2 == 0 else whole(source.shape) for n, source in enumerate(sources)]
        *pieces, powers, inverse = grid_call(
            functools.partial(grads_body, parts, [(n, n + 1) for n in range(0, len(sources), 2)]),
            (parts,),
            specs,
            [whole((shard, width))] * parts + [whole((16, width)), whole((1, width))],
            [shaped((shard, width))] * parts + [shaped((16, width)), shaped((1, width))],
            [pltpu.VMEM((8, width), F32)],
            name=name,
            limit=limit,
        )(scalars, *sources)
        return pieces, (powers, inverse)

    early, early_scale = grads(streamed(normed, branch_grad), [gate_grad, gated], "grad_early", 20 << 20)
    early_got = over_sequences(payloads(early, early_scale))
    early, out_grad = lax.optimization_barrier((early, out_grad))

    zed, dbc = grid_call(
        functools.partial(back_body, inner, states),
        (count,),
        [rows_spec(wide), rows_spec(128), rows_spec(inner), state_block, pre_block, whole((states, inner))],
        [rows_spec(inner), rows_spec(2 * states)],
        [shaped((tokens, inner)), shaped((tokens, 2 * states))],
        [pltpu.VMEM((384, inner), BF16)] * 2,
        name="back",
    )(scalars, conv, per_head, out_grad, hloc, pre, carried)

    gated_later, zed = lax.optimization_barrier((gated, zed))
    branch = grid_call(
        functools.partial(branch_body, parts, quarter),
        (count,),
        [rows_spec(inner)] + [whole((shard, 2 * inner))] * parts,
        dealt_specs,
        dealt_shapes,
        [pltpu.VMEM((BLOCK, model), F32)],
        name="branch",
    )(scalars, gated_later, *ws2)

    returned, early_got, branch = lax.optimization_barrier((returned, early_got, branch))
    front_rows = halfway // 4
    branch_give = swap(branch[3])
    branch_theirs = [branch[1][:front_rows] + branch_give[:front_rows], branch[1][front_rows:] + branch_give[front_rows:]]
    returned, branch_theirs = lax.optimization_barrier((returned, branch_theirs))
    branch_back = [across(branch_theirs[0], 1)]
    all_pre = whole((last + 1, 8, inner))
    per = BLOCK // 8
    half_rows = tokens // 2

    def back_lanes(width, lanes):
        return [
            pl.BlockSpec((BLOCK, width), lambda b, s: (count - 1 - b, lanes(s))),
            pl.BlockSpec((8, width), lambda b, s: (jnp.maximum((count - 1 - b) * per - 1, 0), lanes(s))),
            pl.BlockSpec((8, width), lambda b, s: (0, lanes(s))),
        ]

    def table(rows, width, lanes):
        return pl.BlockSpec((rows, width), lambda b, s: (0, lanes(s)))

    zed, ends, dbc_keep, dbc_give = grid_call(
        functools.partial(meet_body, inner, states),
        (count,),
        [rows_spec(wide), rows_spec(128), rows_spec(inner), rows_spec(2 * states), state_block,
         pl.BlockSpec((1, states, inner), lambda b, s: (jnp.minimum((b + 1) * subs, last - 1), 0, 0)),
         whole((states, inner)), all_pre, state_block, whole((states, inner)), whole((states, inner))],
        [rows_spec(inner), rows_spec(inner, 8), whole((half_rows, 2 * states)), whole((half_rows, 2 * states))],
        [shaped((tokens, inner)), shaped((8 * count, inner)), shaped((half_rows, 2 * states)),
         shaped((half_rows, 2 * states))],
        [pltpu.VMEM((384, inner), BF16)] * 2,
        name="meet",
        limit=20 << 20,
    )(scalars, *streamed(conv, per_head, zed, dbc, hloc, hloc), own_end, *streamed(pre, gloc), returned, carried)

    zed, ends, dbc_keep, dbc_give, branch_back = lax.optimization_barrier((zed, ends, dbc_keep, dbc_give, branch_back))
    early_total, early_power, _ = totalled(early, early_scale, early_got)
    early_cut = chunks([early_total], early_power)
    early_far = over_positions(early_cut)
    signal_pre, tail, head, raw_grad, head_cols, signal_cols = grid_call(
        functools.partial(join_body, inner),
        (count,),
        [back(inner), back(128), back(inner), back(inner), back(inner), back(inner, 8)]
        + back_lanes(inner, lambda s: 0)
        + [table(4, inner, lambda s: 0), whole((1, 128)), whole((1, inner))],
        [back(inner), whole((8, inner)), whole((8, inner)), back(128), whole((8, 128)), whole((8, inner))],
        [shaped((tokens, inner), BF16), shaped((8, inner)), shaped((8, inner)), shaped((tokens, 128)),
         shaped((8, 128)), shaped((8, inner))],
        [pltpu.VMEM((3 * inner, 128), BF16), pltpu.VMEM((BLOCK + 8, inner), F32),
         pltpu.VMEM((BLOCK + 8, inner), F32), pltpu.VMEM((384, inner), BF16)],
        name="join",
        limit=20 << 20,
    )(scalars, *streamed(conv, per_head, out_grad, y), zed, ends, *streamed(u, u), uh, taps_x, rate_row, skip_row)

    head, early_far = lax.optimization_barrier((head, early_far))
    early_sum = settled(early_cut[0], decoded(early_far))
    out_sum = jnp.concatenate([part[:, inner:] for part in early_sum], axis=1)
    gate_sum = jnp.concatenate([part[:, :inner] for part in early_sum], axis=1)

    ahead, out_sum, gate_sum = lax.optimization_barrier((along(head, -2), out_sum, gate_sum))
    ahead = jnp.where(hi < pairs - 1, ahead, 0.0)
    for k in range(3):
        tail = tail + taps_x[k, :inner] * jnp.concatenate([jnp.zeros((5 + k, inner), F32), ahead[: 3 - k]])
    signal_pre = lax.dynamic_update_slice_in_dim(signal_pre, tail.astype(BF16), tokens - 8, 0)

    dbc = dbc_keep + swap(dbc_give)
    signal_pre, dbc = lax.optimization_barrier((signal_pre, dbc))
    dbc_back = across(lax.dynamic_slice_in_dim(dbc, (1 - lo) * states, states, 1), 1)
    signal_small = jnp.concatenate([signal_cols, turn_cols])
    signal, signal_scale = grads(streamed(normed), streamed(signal_pre), "grad_signal", 20 << 20)
    signal, dbc_back = lax.optimization_barrier((signal, dbc_back))
    signal_payload = payloads(signal, signal_scale, [signal_small])

    dbc = mine(dbc, 1, states) + dbc_back
    dbc_other = swap(dbc)
    head_rows = jnp.where(core == 0, dbc[:8], dbc_other[:8])
    head_conv = lax.dynamic_slice(conv, (0, inner + lo * states), (8, states))
    state_ahead = along(head_rows * slope(head_conv, jax.nn.sigmoid(head_conv)), -2)
    branch_later, state_ahead, signal_payload = lax.optimization_barrier((branch_theirs[1], state_ahead, signal_payload))
    signal_got = over_sequences(signal_payload)
    def back_own(b, s):
        return jnp.clip(count - 1 - b - s[LO] * 2 * quarter, 0, 2 * quarter - 1), 0

    def state_lanes(s):
        return inner // states + s[LO]

    back_part = pl.BlockSpec((BLOCK, model), lambda b, s: ((count - 1 - b) % quarter, 0))
    back_half = pl.BlockSpec((BLOCK, states), lambda b, s: ((count - 1 - b) % (count // 2), 0))
    state_side = back_lanes(states, state_lanes)
    *feature, extra_pre, feature_cols, state_cols = grid_call(
        functools.partial(feature_body, parts, quarter),
        (count,),
        [pl.BlockSpec((BLOCK, model), back_own), back_part, back_part, back(inner), back(inner), back(128),
         back_half, back_half, state_side[0]] + state_side
        + [whole((8, states)), table(4, states, state_lanes)]
        + [whole((shard, wide + 128))] * parts + [whole((shard, 2 * inner))] * parts,
        dealt_specs + [back(128), whole((8, model)), whole((8, states))],
        dealt_shapes + [shaped((tokens, 128), BF16), shaped((8, model)), shaped((8, states))],
        [pltpu.VMEM((BLOCK, model), F32), pltpu.VMEM((BLOCK + 8, states), F32),
         pltpu.VMEM((BLOCK + 8, states), F32)],
        name="feature",
        limit=24 << 20,
    )(scalars, *streamed(hidden, near, far, gate_grad, signal_pre, raw_grad), dbc, dbc_other, *streamed(conv, u, u), uh,
      state_ahead, taps_x, *streamed(*ws1, *ws2))
    feature, branch_rest, signal_got = lax.optimization_barrier((feature, across(branch_later, 1), signal_got))
    branch_back = jnp.concatenate(branch_back + [branch_rest])
    feature_theirs = feature[1] + swap(feature[3])
    feature_mine = feature[0] + swap(feature[2])

    folds = model // 128
    extra_small = jnp.concatenate(
        [state_cols[:5], head_cols[:2], jnp.zeros((1, 128), F32), feature_cols[0].reshape(folds, 128)]
    )
    feature_power = exponents(jnp.max(jnp.abs(feature_theirs), axis=0, keepdims=True))
    feature_payload = packed(feature_theirs, feature_power, jnp.exp2(-feature_power))
    extra_pre, feature_payload = lax.optimization_barrier((extra_pre, feature_payload))
    extra, extra_scale = grads(streamed(normed), [extra_pre], "grad_extra", 20 << 20)
    feature_back = across(feature_payload, 1)
    signal_total, signal_power, (signal_here,) = totalled(signal, signal_scale, signal_got, [signal_small])
    extra_got = over_sequences(payloads(extra, extra_scale, [extra_small]))
    extra_got, feature_back = lax.optimization_barrier((extra_got, feature_back))
    extra_total, extra_power, (extra_here,) = totalled(extra, extra_scale, extra_got, [extra_small])
    late_power = jnp.concatenate([signal_power, extra_power], axis=1)
    small_here = jnp.concatenate([signal_here, extra_here], axis=1)
    late_cut = chunks([signal_total, extra_total], late_power, [small_here])
    feature_back, late_cut = lax.optimization_barrier((feature_back, late_cut))
    late_far = over_positions(late_cut)
    feature_back = unpacked(feature_back)[0]

    def both_halves(value):
        other = swap(value)
        return jnp.where(core == 0, jnp.concatenate([value, other]), jnp.concatenate([other, value]))

    residual = piece(hidden, core, halfway).astype(F32)
    place = z * steps + core * halfway + lax.broadcasted_iota(jnp.int32, (halfway, 1), 0)
    valid = (place < lengths[0]).astype(F32)
    mixed = both_halves((residual + valid * (branch[0] + swap(branch[2]) + branch_back)).astype(BF16))

    feature_grad = feature_mine + feature_back
    inverse = lax.rsqrt(jnp.mean(residual * residual, axis=1, keepdims=True) + EPSILON)
    scaled_own = residual * inverse
    scaled_grad = feature_grad * norm_gain
    upstream = piece(cotangent, core, halfway).astype(F32)
    grad_hidden = both_halves(
        upstream + inverse * (scaled_grad - scaled_own * jnp.mean(scaled_grad * scaled_own, axis=1, keepdims=True))
    )

    mixed, grad_hidden, late_far = lax.optimization_barrier((mixed, grad_hidden, late_far))
    late_sum = settled(late_cut[0], decoded(late_far, [16]))
    small_sum = settled(small_here, ridden(late_far, [16]))

    def side_by_side(pair):
        return jnp.concatenate(pair, axis=-1)

    taps_sum, bias_sum, ggain_sum, state_taps, state_bias, raw_sum, rate_sum, skip_sum, gain_here = grid_call(
        functools.partial(finish_body, inner),
        (1,),
        [whole((16, inner + 128)), whole((16, inner + 128)), whole((1, 2 * heads))],
        [whole((4, 2 * inner)), whole((1, 2 * inner)), whole((1, 2 * inner)), whole((4, 2 * states)),
         whole((1, 2 * states)), whole((1, 2 * heads)), whole((1, 2 * heads)), whole((1, 2 * heads)),
         whole((8, 128))],
        [shaped((4, 2 * inner)), shaped((1, 2 * inner)), shaped((1, 2 * inner)), shaped((4, 2 * states)),
         shaped((1, 2 * states)), shaped((1, 2 * heads)), shaped((1, 2 * heads)), shaped((1, 2 * heads)),
         shaped((8, 128))],
        name="finish",
    )(scalars, *small_sum, -jnp.exp(log_rate)[None])
    gain_here = gain_here.reshape(model)
    state_here = jnp.stack([part[:, inner : inner + HEAD0] for part in late_sum])
    gain_there, state_there = swap(gain_here), swap(state_here)
    gain_size = model // (dps * ctxs)
    gain_sum = piece(gain_here + gain_there, dp * ctxs + z, gain_size)
    in_order = jnp.where(
        core == 0, jnp.stack([state_here, state_there], 1), jnp.stack([state_there, state_here], 1)
    )
    state_sum = jnp.transpose(in_order, (2, 0, 1, 3)).reshape(-1, 2 * states)
    main_sum = jnp.stack([gate_sum, side_by_side([part[:, :inner] for part in late_sum])], axis=1)
    delta_sum = side_by_side([part[:, inner + HEAD0 : inner + HEAD0 + heads] for part in late_sum])

    return (
        mixed[None],
        grad_hidden[None],
        gain_sum,
        main_sum,
        state_sum,
        delta_sum,
        taps_sum,
        state_taps,
        bias_sum[0],
        state_bias[0],
        raw_sum[0],
        rate_sum[0],
        skip_sum[0],
        ggain_sum[0],
        out_sum,
    )


def solution(mesh):
    in_specs = (
        P("dp", "ctx", None), P("dp"), P("dp", "ctx", None), P(), P("dp", None, "tp"), P("dp", None),
        P("dp", "tp"), P(None, "tp"), P(), P("tp"), P(), P("tp"), P("tp"), P("tp"), P("tp"), P("dp", "tp"),
    )
    out_specs = (
        P("dp", "ctx", None), P("dp", "ctx", None), P(("dp", "ctx")), P(("dp", "ctx"), None, "tp"),
        P(("dp", "ctx"), None), P(("dp", "ctx"), "tp"), P(None, "tp"), P(), P("tp"), P(), P("tp"), P("tp"),
        P("tp"), P("tp"), P(("dp", "ctx"), "tp"),
    )
    return jax.shard_map(
        per_device, mesh=mesh, in_specs=in_specs, out_specs=out_specs, check_vma=False
    )
```

```python
import functools

import jax
import jax.numpy as jnp
from jax import lax
from jax.experimental import pallas as pl
from jax.experimental.pallas import tpu as pltpu
from jax.sharding import PartitionSpec as P

BLOCK = 256
SUB = 128
EPSILON = 1e-05
HIGH = lax.Precision.HIGH
HIGHEST = lax.Precision.HIGHEST
F32 = jnp.float32
BF16 = jnp.bfloat16
F16 = jnp.float16
NN = (((1,), (0,)), ((), ()))
NT = (((1,), (1,)), ((), ()))
TN = (((0,), (0,)), ((), ()))
HEAD0 = 64
STEP = 16
LO, CORE, BASE, LENGTH, HASPREV, HASNEXT, SLOT0 = range(7)


def mm(a, b, dims=NN, precision=None):
    return lax.dot_general(a, b, dims, precision=precision, preferred_element_type=F32)


def grid_call(body, grid, in_specs, out_specs, out_shape, scratch=(), name=None, limit=None):
    return pl.pallas_call(
        body,
        grid_spec=pltpu.PrefetchScalarGridSpec(
            num_scalar_prefetch=1,
            grid=grid,
            in_specs=in_specs,
            out_specs=out_specs,
            scratch_shapes=list(scratch),
        ),
        out_shape=out_shape,
        compiler_params=pltpu.CompilerParams(
            dimension_semantics=("arbitrary",) * len(grid), vmem_limit_bytes=limit
        ),
        name=name,
    )


def streamed(*arrays):
    return [pltpu.with_memory_space_constraint(array, pltpu.HBM) for array in arrays]


def rows_spec(width, rows=BLOCK, lane=0):
    return pl.BlockSpec((rows, width), lambda b, s: (b, lane))


def whole(shape):
    return pl.BlockSpec(shape, lambda b, s: (0,) * len(shape))


def shaped(shape, dtype=F32):
    return jax.ShapeDtypeStruct(shape, dtype)


def kept(shape, dtype=F32):
    return pltpu.HBM(shape, dtype)


def slope(v, sig):
    return sig * (1.0 + v * (1.0 - sig))


def lanes_of(s_ref, slot, width):
    return pl.ds(pl.multiple_of(s_ref[SLOT0 + slot] * width, width), width)


def normalize(x, gain):
    value = x.astype(F32)
    inverse = lax.rsqrt(jnp.mean(value * value, axis=1, keepdims=True) + EPSILON)
    scaled = value * inverse
    return scaled, (scaled * gain).astype(BF16)


def pick(s_ref, b, quarter, own, near, far):
    lo, core = s_ref[LO], s_ref[CORE]
    place = b // quarter
    mine = (place // 2) == lo
    from_near = (place % 2) == core
    return jnp.where(mine, own, jnp.where(from_near, near, far))


def valid_rows(s_ref, b):
    position = s_ref[BASE] + b * BLOCK + lax.broadcasted_iota(jnp.int32, (BLOCK, 1), 0)
    return (position < s_ref[LENGTH]).astype(F32)


def expander(inner, shift=0):
    lane = lax.broadcasted_iota(jnp.int32, (384, inner), 0) % 128 - HEAD0 - shift
    head = lax.broadcasted_iota(jnp.int32, (384, inner), 1) // 64
    return (lane == head).astype(F32).astype(BF16)


def collector(inner):
    head = lax.broadcasted_iota(jnp.int32, (3 * inner, 128), 0) % inner // 64
    lane = lax.broadcasted_iota(jnp.int32, (3 * inner, 128), 1) - HEAD0
    return (lane == head).astype(F32).astype(BF16)


def two(x):
    high = x.astype(BF16)
    return high, (x - high.astype(F32)).astype(BF16)


def three(x, axis=1):
    high = x.astype(BF16)
    rest = x - high.astype(F32)
    middle = rest.astype(BF16)
    return jnp.concatenate([high, middle, (rest - middle.astype(F32)).astype(BF16)], axis=axis)


def running(tri, x):
    width = x.shape[1]
    wide = mm(tri, three(x))
    return wide[:, :width] + wide[:, width : 2 * width] + wide[:, 2 * width :]


def triangle(forward):
    row = lax.broadcasted_iota(jnp.int32, (BLOCK, BLOCK), 0)
    col = lax.broadcasted_iota(jnp.int32, (BLOCK, BLOCK), 1)
    same = (row // SUB) == (col // SUB)
    keep = (row >= col) if forward else (col >= row)
    return (same & keep).astype(F32).astype(BF16)


def stacked_heads(x):
    half = lax.broadcasted_iota(jnp.int32, (1, 128), 1) < 64
    return two(jnp.concatenate([jnp.where(half, x, 0.0), jnp.where(half, 0.0, x)], axis=0))


def faded(keep, level, level_t, level_x, pair, forward):
    out = []
    for side in range(2):
        h = HEAD0 + 2 * pair + side
        at = pair * 128 + side * 64
        column, row = level_x[:, at : at + 1], level_t[h : h + 1, :]
        diff = column - row if forward else row - column
        out.append(jnp.exp(jnp.where(keep, diff, -1e30)))
    return jnp.concatenate(out, axis=1)


def mixed_heads(mix, high, low):
    mh, ml = two(mix)
    wide = mm(mh, jnp.concatenate([high, low], axis=1))
    return wide[:, :128] + wide[:, 128:] + mm(ml, high)


def head_lanes(inner):
    lane = lax.broadcasted_iota(jnp.int32, (1, 128), 1)
    return (lane >= HEAD0) & (lane < HEAD0 + inner // 64)


def front_body(parts, inner, states, quarter, s_ref, own, near, far, halo, gain, taps, bias, dbias, rate,
               *rest):
    ws = rest[:parts]
    normed_ref, u_ref, uh_ref, co_ref, hd_ref, hloc_ref, pre_ref, end_ref = rest[parts : parts + 8]
    hsc, usc, state, pre, esc, wsc = rest[parts + 8 :]
    b = pl.program_id(0)
    wide = inner + 2 * states
    shard = ws[0].shape[0]
    normed_ref[...] = normalize(pick(s_ref, b, quarter, own[...], near[...], far[...]), gain[...])[1]

    @pl.when(b == 0)
    def _():
        hsc[...] = normalize(halo[...], gain[...])[1]
        for j in range(parts):
            wsc[lanes_of(s_ref, j, shard)] = ws[j][...]
        edge = mm(hsc[...], wsc[:, :wide])
        edge = jnp.where(s_ref[HASPREV] > 0, edge[8:], 0.0)
        usc[0:8] = edge
        uh_ref[...] = edge
        state[...] = jnp.zeros_like(state)
        pre[...] = jnp.zeros_like(pre)
        esc[...] = expander(inner)

    @pl.when(b > 0)
    def _():
        usc[0:8] = usc[BLOCK : BLOCK + 8]

    u = mm(normed_ref[...], wsc[...])
    usc[8 : 8 + BLOCK] = u[:, :wide]
    u_ref[...] = u[:, :wide]
    conv = bias[...] + taps[0:1] * usc[5 : 5 + BLOCK]
    for k in range(1, 4):
        conv = conv + taps[k : k + 1] * usc[5 + k : 5 + k + BLOCK]
    co_ref[...] = conv
    raw = u[:, wide:] + dbias[...]
    delta = jnp.where(head_lanes(inner), jnp.maximum(raw, 0.0) + jnp.log1p(jnp.exp(-jnp.abs(raw))), 0.0)
    delta = delta * valid_rows(s_ref, b)
    level = running(triangle(True), delta * rate[...])
    raw = jnp.where(head_lanes(inner), raw, 0.0)
    hd_ref[...] = level + pltpu.roll(delta, STEP, 1) + pltpu.roll(raw, 2 * STEP, 1)
    both = mm(jnp.concatenate([three(level), three(delta)], axis=0), esc[...])
    level_x, delta_x = both[:BLOCK], both[BLOCK:]
    act = conv * jax.nn.sigmoid(conv)
    source = delta_x * act[:, :inner]
    inject_t = act[:, inner : inner + states].T
    for i in range(BLOCK // SUB):
        at = slice(i * SUB, (i + 1) * SUB)
        last = level_x[(i + 1) * SUB - 1 : (i + 1) * SUB]
        fresh = mm(inject_t[:, at], jnp.exp(last - level_x[at]) * source[at], precision=HIGH)
        before = state[...]
        n = b * (BLOCK // SUB) + i
        hloc_ref[i] = before
        pre_ref[n] = pre[...]
        state[...] = jnp.exp(last) * before + fresh
        pre[...] = pre[...] + last

    @pl.when(b == pl.num_programs(0) - 1)
    def _():
        end_ref[...] = state[...]
        pre_ref[n + 1] = pre[...]


def start_expanders(inner, *scs):
    @pl.when(pl.program_id(0) == 0)
    def _():
        for shift, sc in scs:
            sc[...] = expander(inner, shift)


def within_body(inner, states, s_ref, co, hd, yw_ref, lsc, dsc):
    start_expanders(inner, (0, lsc), (STEP, dsc))
    conv = co[...]
    act = conv * jax.nn.sigmoid(conv)
    level = hd[...]
    exact = three(level)
    lx = mm(exact, lsc[...])
    xs = mm(exact, dsc[...]) * act[:, :inner]
    keep = lax.broadcasted_iota(jnp.int32, (SUB, SUB), 0) >= lax.broadcasted_iota(jnp.int32, (SUB, SUB), 1)
    for i in range(BLOCK // SUB):
        at = slice(i * SUB, (i + 1) * SUB)
        affinity = mm(act[at, inner + states :], act[at, inner : inner + states], NT, HIGH)
        affinity = jnp.concatenate([affinity, affinity], axis=1)
        level_t = level[at].T
        level_x = lx[at]
        for pair in range(inner // 128):
            lanes = slice(pair * 128, pair * 128 + 128)
            mix = faded(keep, level, level_t, level_x, pair, True) * affinity
            yw_ref[at, lanes] = mixed_heads(mix, *stacked_heads(xs[at, lanes]))


def gates_body(parts, quarter, s_ref, normed, own, near, far, *rest):
    ws = rest[:parts]
    gate_ref, gg_ref, bg_ref, wsc = rest[parts:]
    b = pl.program_id(0)
    shard = ws[0].shape[0]
    inner = gate_ref.shape[1]
    up = pick(s_ref, b, quarter, own[...], near[...], far[...])
    bg_ref[...] = (up.astype(F32) * valid_rows(s_ref, b)).astype(BF16)

    @pl.when(b == 0)
    def _():
        for j in range(parts):
            wsc[lanes_of(s_ref, j, shard)] = ws[j][...]

    gate_ref[...] = mm(normed[...], wsc[:, :inner])
    gg_ref[...] = mm(bg_ref[...], wsc[:, inner:])


def entering(hloc, pre, hin):
    return hloc + jnp.exp(pre[0:1]) * hin


def output_body(inner, states, s_ref, co, hd, yw, gate, gg, hloc, pre, hin, skip, ggain, y_ref, sum_ref, lsc):
    start_expanders(inner, (0, lsc))
    lx = mm(three(hd[...]), lsc[...])
    conv = co[...]
    act = conv * jax.nn.sigmoid(conv)
    for i in range(BLOCK // SUB):
        at = slice(i * SUB, (i + 1) * SUB)
        held = entering(hloc[i], pre[i], hin[...])
        y_ref[at] = yw[at] + jnp.exp(lx[at]) * mm(act[at, inner + states :], held, precision=HIGH)
    out = y_ref[...] + skip[...] * act[:, :inner]
    g = gate[...]
    product = out * (g * jax.nn.sigmoid(g))
    ones = jnp.ones((8, 3 * inner), BF16)
    sum_ref[0:8] = mm(ones, three(product * product), NT)
    sum_ref[8:16] = mm(ones, three(gg[...] * ggain[...] * product), NT)


def turn_body(inner, states, total, s_ref, co, hd, y, gate, gg, sums, sums1, sums2, sums3, skip, ggain,
              gated_ref, ggrad_ref, og_ref, gloc_ref, start_ref, cols_ref, chain, lsc):
    start_expanders(inner, (0, lsc))
    lx = mm(three(hd[...]), lsc[...])
    step = pl.program_id(0)
    conv = co[...]
    act = conv * jax.nn.sigmoid(conv)
    x = act[:, :inner]
    readout_t = act[:, inner + states :].T
    both = (sums[...] + sums1[...] + sums2[...] + sums3[...]).T
    ginv = lax.rsqrt(both[:, 0:1] / total + EPSILON)
    dot = ginv * both[:, 8:9] / total
    g = gate[...]
    sig = jax.nn.sigmoid(g)
    ga = g * sig
    out = y[...] + skip[...] * x
    unit = out * ga * ginv
    gated_ref[...] = (unit * ggain[...]).astype(BF16)
    grad = gg[...]
    pg = ginv * (grad * ggain[...] - unit * dot)
    og = pg * ga
    og_ref[...] = og
    ggrad_ref[...] = (pg * out * slope(g, sig)).astype(BF16)

    @pl.when(step == 0)
    def _():
        chain[...] = jnp.zeros_like(chain)
        cols_ref[...] = jnp.zeros_like(cols_ref)

    cols_ref[0:1] += jnp.sum(grad * unit, axis=0, keepdims=True)
    cols_ref[1:2] += jnp.sum(og * x, axis=0, keepdims=True)
    b = pl.num_programs(0) - 1 - step
    for i in reversed(range(BLOCK // SUB)):
        at = slice(i * SUB, (i + 1) * SUB)
        held = chain[...]
        gloc_ref[i] = held
        level_x = lx[at]
        chain[...] = jnp.exp(level_x[SUB - 1 : SUB]) * held + mm(
            readout_t[:, at], jnp.exp(level_x) * og[at], precision=HIGH
        )

    @pl.when(b == 0)
    def _():
        start_ref[...] = chain[...]


def back_body(inner, states, s_ref, co, hd, og, hloc, pre, hin, z_ref, dbc_ref, lsc, dsc):
    start_expanders(inner, (0, lsc), (STEP, dsc))
    conv = co[...]
    act = conv * jax.nn.sigmoid(conv)
    level = hd[...]
    exact = three(level)
    lx = mm(exact, lsc[...])
    xs = mm(exact, dsc[...]) * act[:, :inner]
    keep = lax.broadcasted_iota(jnp.int32, (SUB, SUB), 1) >= lax.broadcasted_iota(jnp.int32, (SUB, SUB), 0)
    for i in range(BLOCK // SUB):
        at = slice(i * SUB, (i + 1) * SUB)
        inject, readout = act[at, inner : inner + states], act[at, inner + states :]
        affinity = mm(inject, readout, NT, HIGH)
        affinity = jnp.concatenate([affinity, affinity], axis=1)
        level_t = level[at].T
        level_x = lx[at]
        grad = jnp.zeros((SUB, SUB), F32)
        for pair in range(inner // 128):
            lanes = slice(pair * 128, pair * 128 + 128)
            fade = faded(keep, level, level_t, level_x, pair, False)
            g = og[at, lanes]
            z_ref[at, lanes] = mixed_heads(fade * affinity, *stacked_heads(g))
            xh, xl = stacked_heads(xs[at, lanes])
            gh, gl = two(g)
            outer = mm(
                jnp.concatenate([xh, xl], axis=1), jnp.concatenate([gh, gh], axis=1), NT
            ) + mm(xh, gl, NT)
            grad += fade[:, :SUB] * outer[:SUB] + fade[:, SUB:] * outer[SUB:]
        held = entering(hloc[i], pre[i], hin[...])
        dbc_ref[at, :states] = mm(grad, readout, precision=HIGH)
        dbc_ref[at, states:] = mm(grad.T, inject, precision=HIGH) + mm(
            jnp.exp(level_x) * og[at], held, NT, HIGH
        )


def conv_back(grad, csc, usc, taps, cols_ref):
    csc[0:BLOCK] = grad
    pre = taps[0:1] * csc[3 : 3 + BLOCK]
    for k in range(1, 4):
        pre = pre + taps[k : k + 1] * csc[3 - k : 3 - k + BLOCK]
    for k in range(4):
        cols_ref[k : k + 1] += jnp.sum(grad * usc[5 + k : 5 + k + BLOCK], axis=0, keepdims=True)
    cols_ref[4:5] += jnp.sum(grad, axis=0, keepdims=True)
    csc[BLOCK : BLOCK + 8] = grad[0:8]
    return pre


def meet_body(inner, states, s_ref, co, hd, z, dbc, hloc, hnext, hend, pre, gloc, gin, hin, zed_ref, ends_ref, keep_ref,
              give_ref, lsc, dsc):
    start_expanders(inner, (0, lsc), (STEP, dsc))
    exact = three(hd[...])
    lx = mm(exact, lsc[...])
    subs = BLOCK // SUB
    count = pl.num_programs(0)
    b = pl.program_id(0)
    conv = co[...]
    act = conv * jax.nn.sigmoid(conv)
    source = mm(exact, dsc[...]) * act[:, :inner]
    ends = []
    inject_grads = []
    for i in range(subs):
        at = slice(i * SUB, (i + 1) * SUB)
        n = b * subs + i + 1
        level_x = lx[at]
        later = gloc[i] + jnp.exp(pre[subs * count][0:1] - pre[n][0:1]) * gin[...]
        after = hloc[i + 1] if i < subs - 1 else jnp.where(b == count - 1, hend[...], hnext[0])
        fade = jnp.exp(level_x[SUB - 1 : SUB] - level_x)
        zed_ref[at] = z[at] + fade * mm(act[at, inner : inner + states], later, precision=HIGH)
        inject_grads.append(dbc[at, :states] + mm(fade * source[at], later, NT, HIGH))
        ends.append(jnp.sum(later * entering(after, pre[n], hin[...]), axis=0, keepdims=True))
    ends_ref[...] = jnp.concatenate(ends + [jnp.zeros((8 - subs, inner), F32)], axis=0)
    inject_grad = jnp.concatenate(inject_grads, axis=0)
    half = count // 2
    rows = pl.ds(pl.multiple_of((b % half) * BLOCK, BLOCK), BLOCK)

    @pl.when(b // half == s_ref[CORE])
    def _():
        keep_ref[rows, :states] = inject_grad
        keep_ref[rows, states:] = dbc[:, states:]

    @pl.when(b // half != s_ref[CORE])
    def _():
        give_ref[rows, :states] = inject_grad
        give_ref[rows, states:] = dbc[:, states:]


def join_body(inner, s_ref, co, hd, og, y, zed_in, ends_in, u, prior, uh, taps, rate, skip, mg_ref,
              tail_ref, head_ref, rg_ref, cols_ref, sig_ref, col_sc, csc, usc, dsc):
    start_expanders(inner, (STEP, dsc))
    step = pl.program_id(0)
    subs = BLOCK // SUB
    count = pl.num_programs(0)
    b = count - 1 - step

    @pl.when(step == 0)
    def _():
        cols_ref[...] = jnp.zeros_like(cols_ref)
        sig_ref[...] = jnp.zeros_like(sig_ref)
        col_sc[...] = collector(inner)
        csc[BLOCK : BLOCK + 8] = jnp.zeros((8, inner), F32)

    conv = co[...]
    sig = jax.nn.sigmoid(conv)
    x = conv * sig
    packed_heads = hd[...]
    delta_x = mm(three(packed_heads), dsc[...])
    zed = zed_in[...]
    ends = ends_in[...]
    g = og[...]
    sums = mm(three(jnp.concatenate([x * zed, g * y[...], ends], axis=0)), col_sc[...])
    direct, read, ends = sums[:BLOCK], sums[BLOCK : 2 * BLOCK], sums[2 * BLOCK :]
    dlt = jnp.where(head_lanes(inner), pltpu.roll(packed_heads, 128 - STEP, 1), 0.0)
    draw = pltpu.roll(packed_heads, 128 - 2 * STEP, 1)
    q = running(triangle(False), read - dlt * direct)
    q = jnp.concatenate([q[i * SUB : (i + 1) * SUB] + ends[i : i + 1] for i in range(subs)], axis=0)
    rg = (direct + rate[...] * q) * valid_rows(s_ref, b) * jax.nn.sigmoid(draw)
    rg = jnp.where(head_lanes(inner), rg, 0.0)
    rg_ref[...] = rg
    cols_ref[0:1] += jnp.sum(rg, axis=0, keepdims=True)
    cols_ref[1:2] += jnp.sum(dlt * q, axis=0, keepdims=True)

    usc[0:8] = jnp.where(b == 0, uh[...], prior[...])
    usc[8 : 8 + BLOCK] = u[...]
    grad = (delta_x * zed + skip[...] * g) * slope(conv, sig)
    pre_grad = conv_back(grad, csc, usc, taps, sig_ref)
    mg_ref[...] = pre_grad.astype(BF16)
    head_ref[...] = grad[0:8]

    @pl.when(step == 0)
    def _():
        tail_ref[...] = pre_grad[BLOCK - 8 :]


def exponents(peak):
    return jnp.clip(jnp.ceil(jnp.log(jnp.maximum(peak, 1e-36)) * 1.4426950408889634) - 14.0, -100.0, 100.0)


def packed(value, power, inverse, riders=()):
    rows = [(value * inverse).astype(F16), jnp.broadcast_to(power, (16, value.shape[1])).astype(F16)]
    for more in riders:
        each = exponents(jnp.abs(more))
        rows += [(more * jnp.exp2(-each)).astype(F16), each.astype(F16)]
    return jnp.concatenate(rows)


def unpacked(sent, counts=()):
    rows = sent.shape[0] - 16 - 2 * sum(counts)
    power = sent[rows : rows + 1].astype(F32)
    more = []
    at = rows + 16
    for size in counts:
        more.append(sent[at : at + size].astype(F32) * jnp.exp2(sent[at + size : at + 2 * size].astype(F32)))
        at += 2 * size
    return sent[:rows].astype(F32) * jnp.exp2(power), power, more


def grads_body(parts, pairs, s_ref, *refs):
    inputs = 1 + max(max(pair) for pair in pairs)
    outs = refs[inputs : inputs + parts]
    powers, inverse, peak = refs[inputs + parts :]
    j = pl.program_id(0)

    @pl.when(j == 0)
    def _():
        peak[...] = jnp.zeros_like(peak)

    at = 0
    for left, right in pairs:
        value = mm(refs[left][...], refs[right][...], TN)
        lanes = slice(at, at + value.shape[1])
        at += value.shape[1]
        peak[0:1, lanes] = jnp.maximum(peak[0:1, lanes], jnp.max(jnp.abs(value), axis=0, keepdims=True))
        for k in range(parts):

            @pl.when(j == k)
            def _():
                outs[k][:, lanes] = value

    @pl.when(j == parts - 1)
    def _():
        power = exponents(peak[...])
        powers[...] = jnp.broadcast_to(power[0:1], (16, at))
        inverse[...] = jnp.exp2(-power[0:1])


def deal(s_ref, b, quarter, value, outs):
    place = b // quarter
    rows = pl.ds(pl.multiple_of((b % quarter) * BLOCK, BLOCK), BLOCK)
    at = (place % 2 != s_ref[CORE]).astype(jnp.int32) * 2 + (place // 2 != s_ref[LO]).astype(jnp.int32)
    for k in range(4):

        @pl.when(at == k)
        def _():
            outs[k][rows] = value


def feature_body(parts, quarter, s_ref, own, near, far, ggrad, mg, rg, dbc, dbc_other, co, u, prior, uh, ahead,
                 taps, *rest):
    ws1 = rest[:parts]
    ws2 = rest[parts : 2 * parts]
    outs = rest[2 * parts : 2 * parts + 4]
    xg_ref, cols_ref, state_ref, whole_sc, csc, usc = rest[2 * parts + 4 :]
    step = pl.program_id(0)
    count = pl.num_programs(0)
    b = count - 1 - step
    inner = ggrad.shape[1]
    shard = ws1[0].shape[0]

    @pl.when(step == 0)
    def _():
        cols_ref[...] = jnp.zeros_like(cols_ref)
        state_ref[...] = jnp.zeros_like(state_ref)
        csc[BLOCK : BLOCK + 8] = jnp.where(s_ref[HASNEXT] > 0, ahead[...], 0.0)

    usc[0:8] = jnp.where(b == 0, uh[...], prior[...])
    usc[8 : 8 + BLOCK] = u[...]
    conv = co[...]
    grad = jnp.where(b // (count // 2) == s_ref[CORE], dbc[...], dbc_other[...])
    grad = grad * slope(conv, jax.nn.sigmoid(conv))
    pre = conv_back(grad, csc, usc, taps, state_ref)
    pre = jnp.where(s_ref[CORE] > 0, pltpu.roll(pre, 64, 1), pre)
    lane = lax.broadcasted_iota(jnp.int32, (BLOCK, 128), 1)
    xg = jnp.where(lane < HEAD0, pre, rg[...]).astype(BF16)
    xg_ref[...] = xg
    for j in range(parts):
        at = lanes_of(s_ref, j, shard)
        whole_sc[:, at] = (
            mm(ggrad[...], ws2[j][:, :inner], NT)
            + mm(mg[...], ws1[j][:, :inner], NT)
            + mm(xg, ws1[j][:, -128:], NT)
        )
    value = whole_sc[...]
    scaled = normalize(pick(s_ref, b, quarter, own[...], near[...], far[...]), 1.0)[0]
    cols_ref[0:1] += jnp.sum(value * scaled, axis=0, keepdims=True)
    deal(s_ref, b, quarter, value, outs)


def branch_body(parts, quarter, s_ref, gated, *rest):
    ws2 = rest[:parts]
    outs = rest[parts : parts + 4]
    whole_sc = rest[parts + 4]
    inner = gated.shape[1]
    shard = ws2[0].shape[0]
    for j in range(parts):
        whole_sc[:, lanes_of(s_ref, j, shard)] = mm(gated[...], ws2[j][:, inner:], NT)
    deal(s_ref, pl.program_id(0), quarter, whole_sc[...], outs)


def finish_body(inner, s_ref, first, second, rate, taps_ref, bias_ref, gain_ref, staps_ref, sbias_ref, raw_ref,
                rate_ref, skip_ref, norm_ref):
    both = (first, second)
    heads = inner // 64
    lane = lax.broadcasted_iota(jnp.int32, (8, 128), 1)
    pairs, skips = [], []
    for n, part in enumerate(both):
        at = slice(n * inner, (n + 1) * inner)
        taps_ref[:, at] = part[0:4, :inner]
        bias_ref[:, at] = part[4:5, :inner]
        gain_ref[:, at] = part[8:9, :inner]
        here = slice(n * 128, (n + 1) * 128)
        staps_ref[:, here] = part[0:4, inner:]
        sbias_ref[:, here] = part[4:5, inner:]
        turn = (128 - HEAD0 + n * heads) % 128
        pairs.append(pltpu.roll(part[0:8, inner:], turn, 1))
        skips.append(pltpu.roll(mm(three(part[8:16, :inner]), collector(inner)), turn, 1))
    values = jnp.where(lane < heads, pairs[0], pairs[1])
    skip = jnp.where(lane < heads, skips[0], skips[1])
    raw_ref[...] = values[5:6, : 2 * heads]
    rate_ref[...] = values[6:7, : 2 * heads] * rate[...]
    skip_ref[...] = skip[1:2, : 2 * heads]
    norm_ref[...] = first[8:16, inner:] + second[8:16, inner:]


def per_device(
    hidden, lengths, cotangent, norm_gain, proj_main, proj_state, proj_delta, conv_main, conv_state,
    bias_main, bias_state, delta_bias, log_rate, skip_gain, gate_gain, proj_out,
):
    _, steps, model = hidden.shape
    hidden, cotangent = hidden[0], cotangent[0]
    dps, ctxs, tps = lax.axis_size("dp"), lax.axis_size("ctx"), lax.axis_size("tp")
    dp, z, core = lax.axis_index("dp"), lax.axis_index("ctx"), lax.axis_index("tp")
    lo, hi = z % 2, z // 2
    pairs = ctxs // 2
    tokens = 2 * steps
    count = tokens // BLOCK
    quarter = count // 4
    inner = bias_main.shape[0] // 2
    heads = delta_bias.shape[0] // 2
    states = bias_state.shape[0] // 2
    wide = inner + 2 * states

    def swap(value):
        return lax.ppermute(value, "tp", [(0, 1), (1, 0)])

    def across(value, j):
        return lax.ppermute(value, "ctx", [(i, i ^ j) for i in range(ctxs)])

    def along(value, step):
        return lax.ppermute(
            value, "ctx", [(i, i + step) for i in range(ctxs) if 0 <= i + step < ctxs]
        )

    def spread(value, j):
        return lax.ppermute(value, "dp", [(i, i ^ j) for i in range(dps)])

    def mine(value, axis, size):
        return lax.dynamic_slice_in_dim(value, lo * size, size, axis)

    def piece(value, at, size):
        return lax.dynamic_slice_in_dim(value, at * size, size, 0)

    apart = proj_main.shape[0] % 128 == 0
    parts = dps if apart else 1
    shard = proj_main.shape[0] * (dps // parts)

    def gathered(value):
        if not apart:
            return [lax.all_gather(value, "dp", axis=0, tiled=True)]
        return [value] + [spread(value, j) for j in range(1, dps)]

    scalars = jnp.stack(
        [lo, core, hi * tokens, lengths[0], (hi > 0).astype(jnp.int32), (hi < pairs - 1).astype(jnp.int32)]
        + [dp ^ j if apart else 0 * dp for j in range(parts)]
    ).astype(jnp.int32)

    state_own = lax.dynamic_slice_in_dim(proj_state, lo * states + core * (states // 2), states // 2, 1)
    delta_own = mine(proj_delta, 1, heads)
    main_part = mine(proj_main, 2, inner)
    first = jnp.concatenate(
        [main_part[:, 1], proj_state, state_own, delta_own,
         jnp.zeros((proj_main.shape[0], 64 - heads), BF16)], axis=1
    )
    halfway = steps // 2
    near = across(piece(hidden, core, halfway), 1)
    far = swap(near)
    ws1 = gathered(first)

    def payloads(pieces, scale, riders=()):
        return [packed(pieces[j], scale[0], scale[1], riders) for j in range(1, parts)]

    def over_sequences(payload):
        return [spread(payload[j - 1], j) for j in range(1, parts)]

    def totalled(pieces, scale, got, riders=()):
        total, power = pieces[0], scale[0][0:1]
        if not apart:
            total = lax.psum_scatter(total, "dp", scatter_dimension=0, tiled=True)
            power = exponents(jnp.max(jnp.abs(total), axis=0, keepdims=True))
            riders = [lax.psum(value, "dp") for value in riders]
        for sent in got:
            value, other, more = unpacked(sent, [rider.shape[0] for rider in riders])
            total, power = total + value, jnp.maximum(power, other)
            riders = [one + two for one, two in zip(riders, more)]
        return total, power + (parts - 1).bit_length(), riders

    def chunks(totals, power, riders=()):
        size = totals[0].shape[0] // ctxs
        rows = [jnp.concatenate([piece(total, z ^ j, size) for total in totals], axis=1) for j in range(ctxs)]
        return rows[:1] + [packed(value, power, jnp.exp2(-power), riders) for value in rows[1:]]

    def over_positions(cut):
        return [across(cut[j], j) for j in range(1, ctxs)]

    def settled(own, got):
        opposite = got[0]
        for j in range(2, ctxs):
            if j % 2 == 0:
                own = own + got[j - 1]
            else:
                opposite = opposite + got[j - 1]
        return jnp.where(lo == 0, own, opposite), jnp.where(lo == 0, opposite, own)

    def decoded(got, counts=()):
        return [unpacked(sent, counts)[0] for sent in got]

    def ridden(got, counts):
        return [unpacked(sent, counts)[2][0] for sent in got]

    taps_x = jnp.concatenate([mine(conv_main, 1, inner), conv_state], axis=1)
    bias_x = jnp.concatenate([mine(bias_main, 0, inner), bias_state])[None]
    rate_own = -jnp.exp(mine(log_rate, 0, heads))

    def in_heads(value):
        return jnp.pad(value, (HEAD0, 128 - HEAD0 - heads))[None]

    rate_row = in_heads(rate_own)
    dbias_row = in_heads(mine(delta_bias, 0, heads))
    skip_row = jnp.repeat(mine(skip_gain, 0, heads), inner // heads)[None]
    ggain_row = mine(gate_gain, 0, inner)[None]
    gain_row = norm_gain[None]
    edge, scalars, taps_x, bias_x, rate_row, dbias_row, _ = lax.optimization_barrier(
        (hidden[steps - 16 :], scalars, taps_x, bias_x, rate_row, dbias_row, first)
    )
    route = [
        ((z0 - 1) * tps + c, (z0 + c) * tps + c) for z0 in range(2, ctxs, 2) for c in range(2)
    ]
    edge = lax.ppermute(edge, ("ctx", "tp"), route)
    halo = jnp.where(core == lo, edge, swap(edge))

    near, cot_later = lax.optimization_barrier((near, cotangent))
    ws1, near, main_gate, out_later = lax.optimization_barrier((ws1, near, main_part[:, 0], proj_out))
    second = jnp.concatenate([main_gate, mine(out_later, 1, inner)], axis=1)
    ws2 = gathered(second)
    cot_near = across(piece(cot_later, core, halfway), 1)

    own_spec = pl.BlockSpec(
        (BLOCK, model), lambda b, s: (jnp.clip(b - s[LO] * 2 * quarter, 0, 2 * quarter - 1), 0)
    )
    part_spec = pl.BlockSpec((BLOCK, model), lambda b, s: (b % quarter, 0))
    subs = BLOCK // SUB
    last = count * subs
    state_block = pl.BlockSpec((subs, states, inner), lambda b, s: (b, 0, 0))
    pre_block = pl.BlockSpec((subs, 8, inner), lambda b, s: (b, 0, 0))

    normed, u, uh, conv, per_head, hloc, pre, own_end = grid_call(
        functools.partial(front_body, parts, inner, states, quarter),
        (count,),
        [own_spec, part_spec, part_spec, whole((16, model)), whole((1, model)), whole((4, wide)),
         whole((1, wide)), whole((1, 128)), whole((1, 128))] + [whole((shard, wide + 128))] * parts,
        [rows_spec(model), rows_spec(wide), whole((8, wide)), rows_spec(wide), rows_spec(128),
         state_block, whole((last + 1, 8, inner)), whole((states, inner))],
        [shaped((tokens, model), BF16), shaped((tokens, wide)), shaped((8, wide)), shaped((tokens, wide)),
         shaped((tokens, 128)), shaped((last, states, inner)), shaped((last + 1, 8, inner)),
         shaped((states, inner))],
        [pltpu.VMEM((16, model), BF16), pltpu.VMEM((8 + BLOCK, wide), F32), pltpu.VMEM((states, inner), F32),
         pltpu.VMEM((8, inner), F32), pltpu.VMEM((384, inner), BF16), pltpu.VMEM((model, wide + 128), BF16)],
        name="front",
    )(scalars, hidden, near, far, halo, gain_row, taps_x, bias_x, dbias_row, rate_row, *ws1)

    cot_near, own_end = lax.optimization_barrier((cot_near, own_end))
    cot_far = swap(cot_near)
    growth = jnp.exp(pre[last][0:1])
    carried = jnp.zeros_like(own_end)
    sending = own_end
    for hop in range(pairs - 1):
        carried = along(sending, 2)
        if hop < pairs - 2:
            sending = own_end + growth * carried

    (inside,) = grid_call(
        functools.partial(within_body, inner, states),
        (count,),
        [rows_spec(wide), rows_spec(128)],
        [rows_spec(inner)],
        [shaped((tokens, inner))],
        [pltpu.VMEM((384, inner), BF16)] * 2,
        name="within",
        limit=20 << 20,
    )(scalars, *streamed(conv, per_head))

    gate, gated_grad, branch_grad = grid_call(
        functools.partial(gates_body, parts, quarter),
        (count,),
        [rows_spec(model), own_spec, part_spec, part_spec] + [whole((shard, 2 * inner))] * parts,
        [rows_spec(inner), rows_spec(inner), rows_spec(model)],
        [shaped((tokens, inner)), shaped((tokens, inner)), kept((tokens, model), BF16)],
        [pltpu.VMEM((model, 2 * inner), BF16)],
        name="gates",
        limit=20 << 20,
    )(scalars, *streamed(normed, cotangent, cot_near, cot_far, *ws2))

    y, sums = grid_call(
        functools.partial(output_body, inner, states),
        (count,),
        [rows_spec(wide), rows_spec(128), rows_spec(inner), rows_spec(inner), rows_spec(inner), state_block,
         pre_block, whole((states, inner)), whole((1, inner)), whole((1, inner))],
        [rows_spec(inner), pl.BlockSpec((16, BLOCK), lambda b, s: (0, b))],
        [shaped((tokens, inner)), shaped((16, tokens))],
        [pltpu.VMEM((384, inner), BF16)],
        name="output",
        limit=20 << 20,
    )(scalars, *streamed(conv, per_head), inside, gate, gated_grad, *streamed(hloc), pre, carried, skip_row, ggain_row)

    corner = [(n, ((n // tps) ^ 1) * tps + (n % tps + 1) % tps) for n in range(ctxs * tps)]
    all_sums = [sums, swap(sums), across(sums, 1), lax.ppermute(sums, ("ctx", "tp"), corner)]

    def back(width, rows=BLOCK):
        return pl.BlockSpec((rows, width), lambda b, s: (count - 1 - b, 0))

    back_sums = pl.BlockSpec((16, BLOCK), lambda b, s: (0, count - 1 - b))
    gated, gate_grad, out_grad, gloc, own_start, turn_cols = grid_call(
        functools.partial(turn_body, inner, states, 2 * tps * inner),
        (count,),
        [back(wide), back(128), back(inner), back(inner), back(inner),
         back_sums, back_sums, back_sums, back_sums, whole((1, inner)), whole((1, inner))],
        [back(inner), back(inner), back(inner),
         pl.BlockSpec((subs, states, inner), lambda b, s: (count - 1 - b, 0, 0)), whole((states, inner)),
         whole((8, inner))],
        [shaped((tokens, inner), BF16), shaped((tokens, inner), BF16), kept((tokens, inner)),
         kept((last, states, inner)), shaped((states, inner)), shaped((8, inner))],
        [pltpu.VMEM((states, inner), F32), pltpu.VMEM((384, inner), BF16)],
        name="turn",
        limit=20 << 20,
    )(scalars, *streamed(conv, per_head), y, gate, gated_grad, *all_sums, skip_row, ggain_row)

    returned = jnp.zeros_like(own_start)
    sending = own_start
    for hop in range(pairs - 1):
        returned = along(sending, -2)
        if hop < pairs - 2:
            sending = own_start + growth * returned

    turned = pl.BlockSpec((tokens, shard), lambda j, s: (0, s[SLOT0 + j]))
    dealt_specs = [whole((halfway, model))] * 4
    dealt_shapes = [shaped((halfway, model))] * 4
    def grads(lefts, rights, name, limit=None):
        sources = []
        for left, right in zip(lefts, rights):
            sources += [left, right]
        width = sum(right.shape[1] for right in rights)
        specs = [turned if n % 2 == 0 else whole(source.shape) for n, source in enumerate(sources)]
        *pieces, powers, inverse = grid_call(
            functools.partial(grads_body, parts, [(n, n + 1) for n in range(0, len(sources), 2)]),
            (parts,),
            specs,
            [whole((shard, width))] * parts + [whole((16, width)), whole((1, width))],
            [shaped((shard, width))] * parts + [shaped((16, width)), shaped((1, width))],
            [pltpu.VMEM((8, width), F32)],
            name=name,
            limit=limit,
        )(scalars, *sources)
        return pieces, (powers, inverse)

    early, early_scale = grads(streamed(normed, branch_grad), [gate_grad, gated], "grad_early", 20 << 20)
    early_got = over_sequences(payloads(early, early_scale))
    early, out_grad = lax.optimization_barrier((early, out_grad))

    zed, dbc = grid_call(
        functools.partial(back_body, inner, states),
        (count,),
        [rows_spec(wide), rows_spec(128), rows_spec(inner), state_block, pre_block, whole((states, inner))],
        [rows_spec(inner), rows_spec(2 * states)],
        [shaped((tokens, inner)), shaped((tokens, 2 * states))],
        [pltpu.VMEM((384, inner), BF16)] * 2,
        name="back",
    )(scalars, conv, per_head, out_grad, hloc, pre, carried)

    gated_later, zed = lax.optimization_barrier((gated, zed))
    branch = grid_call(
        functools.partial(branch_body, parts, quarter),
        (count,),
        [rows_spec(inner)] + [whole((shard, 2 * inner))] * parts,
        dealt_specs,
        dealt_shapes,
        [pltpu.VMEM((BLOCK, model), F32)],
        name="branch",
    )(scalars, gated_later, *ws2)

    returned, early_got, branch = lax.optimization_barrier((returned, early_got, branch))
    front_rows = halfway // 4
    branch_give = swap(branch[3])
    branch_theirs = [branch[1][:front_rows] + branch_give[:front_rows], branch[1][front_rows:] + branch_give[front_rows:]]
    returned, branch_theirs = lax.optimization_barrier((returned, branch_theirs))
    branch_back = [across(branch_theirs[0], 1)]
    all_pre = whole((last + 1, 8, inner))
    per = BLOCK // 8
    half_rows = tokens // 2

    def back_lanes(width, lanes):
        return [
            pl.BlockSpec((BLOCK, width), lambda b, s: (count - 1 - b, lanes(s))),
            pl.BlockSpec((8, width), lambda b, s: (jnp.maximum((count - 1 - b) * per - 1, 0), lanes(s))),
            pl.BlockSpec((8, width), lambda b, s: (0, lanes(s))),
        ]

    def table(rows, width, lanes):
        return pl.BlockSpec((rows, width), lambda b, s: (0, lanes(s)))

    zed, ends, dbc_keep, dbc_give = grid_call(
        functools.partial(meet_body, inner, states),
        (count,),
        [rows_spec(wide), rows_spec(128), rows_spec(inner), rows_spec(2 * states), state_block,
         pl.BlockSpec((1, states, inner), lambda b, s: (jnp.minimum((b + 1) * subs, last - 1), 0, 0)),
         whole((states, inner)), all_pre, state_block, whole((states, inner)), whole((states, inner))],
        [rows_spec(inner), rows_spec(inner, 8), whole((half_rows, 2 * states)), whole((half_rows, 2 * states))],
        [shaped((tokens, inner)), shaped((8 * count, inner)), shaped((half_rows, 2 * states)),
         shaped((half_rows, 2 * states))],
        [pltpu.VMEM((384, inner), BF16)] * 2,
        name="meet",
        limit=20 << 20,
    )(scalars, *streamed(conv, per_head, zed, dbc, hloc, hloc), own_end, *streamed(pre, gloc), returned, carried)

    zed, ends, dbc_keep, dbc_give, branch_back = lax.optimization_barrier((zed, ends, dbc_keep, dbc_give, branch_back))
    early_total, early_power, _ = totalled(early, early_scale, early_got)
    early_cut = chunks([early_total], early_power)
    early_far = over_positions(early_cut)
    signal_pre, tail, head, raw_grad, head_cols, signal_cols = grid_call(
        functools.partial(join_body, inner),
        (count,),
        [back(inner), back(128), back(inner), back(inner), back(inner), back(inner, 8)]
        + back_lanes(inner, lambda s: 0)
        + [table(4, inner, lambda s: 0), whole((1, 128)), whole((1, inner))],
        [back(inner), whole((8, inner)), whole((8, inner)), back(128), whole((8, 128)), whole((8, inner))],
        [shaped((tokens, inner), BF16), shaped((8, inner)), shaped((8, inner)), shaped((tokens, 128)),
         shaped((8, 128)), shaped((8, inner))],
        [pltpu.VMEM((3 * inner, 128), BF16), pltpu.VMEM((BLOCK + 8, inner), F32),
         pltpu.VMEM((BLOCK + 8, inner), F32), pltpu.VMEM((384, inner), BF16)],
        name="join",
        limit=20 << 20,
    )(scalars, *streamed(conv, per_head, out_grad, y), zed, ends, *streamed(u, u), uh, taps_x, rate_row, skip_row)

    head, early_far = lax.optimization_barrier((head, early_far))
    early_sum = settled(early_cut[0], decoded(early_far))
    out_sum = jnp.concatenate([part[:, inner:] for part in early_sum], axis=1)
    gate_sum = jnp.concatenate([part[:, :inner] for part in early_sum], axis=1)

    ahead, out_sum, gate_sum = lax.optimization_barrier((along(head, -2), out_sum, gate_sum))
    ahead = jnp.where(hi < pairs - 1, ahead, 0.0)
    for k in range(3):
        tail = tail + taps_x[k, :inner] * jnp.concatenate([jnp.zeros((5 + k, inner), F32), ahead[: 3 - k]])
    signal_pre = lax.dynamic_update_slice_in_dim(signal_pre, tail.astype(BF16), tokens - 8, 0)

    dbc = dbc_keep + swap(dbc_give)
    signal_pre, dbc = lax.optimization_barrier((signal_pre, dbc))
    dbc_back = across(lax.dynamic_slice_in_dim(dbc, (1 - lo) * states, states, 1), 1)
    signal_small = jnp.concatenate([signal_cols, turn_cols])
    signal, signal_scale = grads(streamed(normed), streamed(signal_pre), "grad_signal", 20 << 20)
    signal, dbc_back = lax.optimization_barrier((signal, dbc_back))
    signal_payload = payloads(signal, signal_scale, [signal_small])

    dbc = mine(dbc, 1, states) + dbc_back
    dbc_other = swap(dbc)
    head_rows = jnp.where(core == 0, dbc[:8], dbc_other[:8])
    head_conv = lax.dynamic_slice(conv, (0, inner + lo * states), (8, states))
    state_ahead = along(head_rows * slope(head_conv, jax.nn.sigmoid(head_conv)), -2)
    branch_later, state_ahead, signal_payload = lax.optimization_barrier((branch_theirs[1], state_ahead, signal_payload))
    signal_got = over_sequences(signal_payload)
    def back_own(b, s):
        return jnp.clip(count - 1 - b - s[LO] * 2 * quarter, 0, 2 * quarter - 1), 0

    def state_lanes(s):
        return inner // states + s[LO]

    back_part = pl.BlockSpec((BLOCK, model), lambda b, s: ((count - 1 - b) % quarter, 0))
    back_half = pl.BlockSpec((BLOCK, states), lambda b, s: ((count - 1 - b) % (count // 2), 0))
    state_side = back_lanes(states, state_lanes)
    *feature, extra_pre, feature_cols, state_cols = grid_call(
        functools.partial(feature_body, parts, quarter),
        (count,),
        [pl.BlockSpec((BLOCK, model), back_own), back_part, back_part, back(inner), back(inner), back(128),
         back_half, back_half, state_side[0]] + state_side
        + [whole((8, states)), table(4, states, state_lanes)]
        + [whole((shard, wide + 128))] * parts + [whole((shard, 2 * inner))] * parts,
        dealt_specs + [back(128), whole((8, model)), whole((8, states))],
        dealt_shapes + [shaped((tokens, 128), BF16), shaped((8, model)), shaped((8, states))],
        [pltpu.VMEM((BLOCK, model), F32), pltpu.VMEM((BLOCK + 8, states), F32),
         pltpu.VMEM((BLOCK + 8, states), F32)],
        name="feature",
        limit=24 << 20,
    )(scalars, *streamed(hidden, near, far, gate_grad, signal_pre, raw_grad), dbc, dbc_other, *streamed(conv, u, u), uh,
      state_ahead, taps_x, *streamed(*ws1, *ws2))
    feature, branch_rest, signal_got = lax.optimization_barrier((feature, across(branch_later, 1), signal_got))
    branch_back = jnp.concatenate(branch_back + [branch_rest])
    feature_theirs = feature[1] + swap(feature[3])
    feature_mine = feature[0] + swap(feature[2])

    folds = model // 128
    extra_small = jnp.concatenate(
        [state_cols[:5], head_cols[:2], jnp.zeros((1, 128), F32), feature_cols[0].reshape(folds, 128)]
    )
    feature_power = exponents(jnp.max(jnp.abs(feature_theirs), axis=0, keepdims=True))
    feature_payload = packed(feature_theirs, feature_power, jnp.exp2(-feature_power))
    extra_pre, feature_payload = lax.optimization_barrier((extra_pre, feature_payload))
    extra, extra_scale = grads(streamed(normed), [extra_pre], "grad_extra", 20 << 20)
    feature_back = across(feature_payload, 1)
    signal_total, signal_power, (signal_here,) = totalled(signal, signal_scale, signal_got, [signal_small])
    extra_got = over_sequences(payloads(extra, extra_scale, [extra_small]))
    extra_got, feature_back = lax.optimization_barrier((extra_got, feature_back))
    extra_total, extra_power, (extra_here,) = totalled(extra, extra_scale, extra_got, [extra_small])
    late_power = jnp.concatenate([signal_power, extra_power], axis=1)
    small_here = jnp.concatenate([signal_here, extra_here], axis=1)
    late_cut = chunks([signal_total, extra_total], late_power, [small_here])
    feature_back, late_cut = lax.optimization_barrier((feature_back, late_cut))
    late_far = over_positions(late_cut)
    feature_back = unpacked(feature_back)[0]

    def both_halves(value):
        other = swap(value)
        return jnp.where(core == 0, jnp.concatenate([value, other]), jnp.concatenate([other, value]))

    residual = piece(hidden, core, halfway).astype(F32)
    place = z * steps + core * halfway + lax.broadcasted_iota(jnp.int32, (halfway, 1), 0)
    valid = (place < lengths[0]).astype(F32)
    mixed = both_halves((residual + valid * (branch[0] + swap(branch[2]) + branch_back)).astype(BF16))

    feature_grad = feature_mine + feature_back
    inverse = lax.rsqrt(jnp.mean(residual * residual, axis=1, keepdims=True) + EPSILON)
    scaled_own = residual * inverse
    scaled_grad = feature_grad * norm_gain
    upstream = piece(cotangent, core, halfway).astype(F32)
    grad_hidden = both_halves(
        upstream + inverse * (scaled_grad - scaled_own * jnp.mean(scaled_grad * scaled_own, axis=1, keepdims=True))
    )

    mixed, grad_hidden, late_far = lax.optimization_barrier((mixed, grad_hidden, late_far))
    late_sum = settled(late_cut[0], decoded(late_far, [16]))
    small_sum = settled(small_here, ridden(late_far, [16]))

    def side_by_side(pair):
        return jnp.concatenate(pair, axis=-1)

    taps_sum, bias_sum, ggain_sum, state_taps, state_bias, raw_sum, rate_sum, skip_sum, gain_here = grid_call(
        functools.partial(finish_body, inner),
        (1,),
        [whole((16, inner + 128)), whole((16, inner + 128)), whole((1, 2 * heads))],
        [whole((4, 2 * inner)), whole((1, 2 * inner)), whole((1, 2 * inner)), whole((4, 2 * states)),
         whole((1, 2 * states)), whole((1, 2 * heads)), whole((1, 2 * heads)), whole((1, 2 * heads)),
         whole((8, 128))],
        [shaped((4, 2 * inner)), shaped((1, 2 * inner)), shaped((1, 2 * inner)), shaped((4, 2 * states)),
         shaped((1, 2 * states)), shaped((1, 2 * heads)), shaped((1, 2 * heads)), shaped((1, 2 * heads)),
         shaped((8, 128))],
        name="finish",
    )(scalars, *small_sum, -jnp.exp(log_rate)[None])
    gain_here = gain_here.reshape(model)
    state_here = jnp.stack([part[:, inner : inner + HEAD0] for part in late_sum])
    gain_there, state_there = swap(gain_here), swap(state_here)
    gain_size = model // (dps * ctxs)
    gain_sum = piece(gain_here + gain_there, dp * ctxs + z, gain_size)
    in_order = jnp.where(
        core == 0, jnp.stack([state_here, state_there], 1), jnp.stack([state_there, state_here], 1)
    )
    state_sum = jnp.transpose(in_order, (2, 0, 1, 3)).reshape(-1, 2 * states)
    main_sum = jnp.stack([gate_sum, side_by_side([part[:, :inner] for part in late_sum])], axis=1)
    delta_sum = side_by_side([part[:, inner + HEAD0 : inner + HEAD0 + heads] for part in late_sum])

    return (
        mixed[None],
        grad_hidden[None],
        gain_sum,
        main_sum,
        state_sum,
        delta_sum,
        taps_sum,
        state_taps,
        bias_sum[0],
        state_bias[0],
        raw_sum[0],
        rate_sum[0],
        skip_sum[0],
        ggain_sum[0],
        out_sum,
    )


def solution(mesh):
    in_specs = (
        P("dp", "ctx", None), P("dp"), P("dp", "ctx", None), P(), P("dp", None, "tp"), P("dp", None),
        P("dp", "tp"), P(None, "tp"), P(), P("tp"), P(), P("tp"), P("tp"), P("tp"), P("tp"), P("dp", "tp"),
    )
    out_specs = (
        P("dp", "ctx", None), P("dp", "ctx", None), P(("dp", "ctx")), P(("dp", "ctx"), None, "tp"),
        P(("dp", "ctx"), None), P(("dp", "ctx"), "tp"), P(None, "tp"), P(), P("tp"), P(), P("tp"), P("tp"),
        P("tp"), P("tp"), P(("dp", "ctx"), "tp"),
    )
    return jax.shard_map(
        per_device, mesh=mesh, in_specs=in_specs, out_specs=out_specs, check_vma=False
    )
```

```python
import functools

import jax
import jax.numpy as jnp
from jax import lax
from jax.experimental import pallas as pl
from jax.experimental.pallas import tpu as pltpu
from jax.sharding import PartitionSpec as P

BLOCK = 256
SUB = 128
EPSILON = 1e-05
HIGH = lax.Precision.HIGH
HIGHEST = lax.Precision.HIGHEST
F32 = jnp.float32
BF16 = jnp.bfloat16
F16 = jnp.float16
NN = (((1,), (0,)), ((), ()))
NT = (((1,), (1,)), ((), ()))
TN = (((0,), (0,)), ((), ()))
HEAD0 = 64
STEP = 16
LO, CORE, BASE, LENGTH, HASPREV, HASNEXT, SLOT0 = range(7)


def mm(a, b, dims=NN, precision=None):
    return lax.dot_general(a, b, dims, precision=precision, preferred_element_type=F32)


def grid_call(body, grid, in_specs, out_specs, out_shape, scratch=(), name=None, limit=None):
    return pl.pallas_call(
        body,
        grid_spec=pltpu.PrefetchScalarGridSpec(
            num_scalar_prefetch=1,
            grid=grid,
            in_specs=in_specs,
            out_specs=out_specs,
            scratch_shapes=list(scratch),
        ),
        out_shape=out_shape,
        compiler_params=pltpu.CompilerParams(
            dimension_semantics=("arbitrary",) * len(grid), vmem_limit_bytes=limit
        ),
        name=name,
    )


def streamed(*arrays):
    return [pltpu.with_memory_space_constraint(array, pltpu.HBM) for array in arrays]


def rows_spec(width, rows=BLOCK, lane=0):
    return pl.BlockSpec((rows, width), lambda b, s: (b, lane))


def whole(shape):
    return pl.BlockSpec(shape, lambda b, s: (0,) * len(shape))


def shaped(shape, dtype=F32):
    return jax.ShapeDtypeStruct(shape, dtype)


def kept(shape, dtype=F32):
    return pltpu.HBM(shape, dtype)


def slope(v, sig):
    return sig * (1.0 + v * (1.0 - sig))


def lanes_of(s_ref, slot, width):
    return pl.ds(pl.multiple_of(s_ref[SLOT0 + slot] * width, width), width)


def normalize(x, gain):
    value = x.astype(F32)
    inverse = lax.rsqrt(jnp.mean(value * value, axis=1, keepdims=True) + EPSILON)
    scaled = value * inverse
    return scaled, (scaled * gain).astype(BF16)


def pick(s_ref, b, quarter, own, near, far):
    lo, core = s_ref[LO], s_ref[CORE]
    place = b // quarter
    mine = (place // 2) == lo
    from_near = (place % 2) == core
    return jnp.where(mine, own, jnp.where(from_near, near, far))


def valid_rows(s_ref, b):
    position = s_ref[BASE] + b * BLOCK + lax.broadcasted_iota(jnp.int32, (BLOCK, 1), 0)
    return (position < s_ref[LENGTH]).astype(F32)


def expander(inner, shift=0):
    lane = lax.broadcasted_iota(jnp.int32, (384, inner), 0) % 128 - HEAD0 - shift
    head = lax.broadcasted_iota(jnp.int32, (384, inner), 1) // 64
    return (lane == head).astype(F32).astype(BF16)


def collector(inner):
    head = lax.broadcasted_iota(jnp.int32, (3 * inner, 128), 0) % inner // 64
    lane = lax.broadcasted_iota(jnp.int32, (3 * inner, 128), 1) - HEAD0
    return (lane == head).astype(F32).astype(BF16)


def two(x):
    high = x.astype(BF16)
    return high, (x - high.astype(F32)).astype(BF16)


def three(x, axis=1):
    high = x.astype(BF16)
    rest = x - high.astype(F32)
    middle = rest.astype(BF16)
    return jnp.concatenate([high, middle, (rest - middle.astype(F32)).astype(BF16)], axis=axis)


def running(tri, x):
    width = x.shape[1]
    wide = mm(tri, three(x))
    return wide[:, :width] + wide[:, width : 2 * width] + wide[:, 2 * width :]


def triangle(forward):
    row = lax.broadcasted_iota(jnp.int32, (BLOCK, BLOCK), 0)
    col = lax.broadcasted_iota(jnp.int32, (BLOCK, BLOCK), 1)
    same = (row // SUB) == (col // SUB)
    keep = (row >= col) if forward else (col >= row)
    return (same & keep).astype(F32).astype(BF16)


def stacked_heads(x):
    half = lax.broadcasted_iota(jnp.int32, (1, 128), 1) < 64
    return two(jnp.concatenate([jnp.where(half, x, 0.0), jnp.where(half, 0.0, x)], axis=0))


def faded(keep, level, level_t, level_x, pair, forward):
    out = []
    for side in range(2):
        h = HEAD0 + 2 * pair + side
        at = pair * 128 + side * 64
        column, row = level_x[:, at : at + 1], level_t[h : h + 1, :]
        diff = column - row if forward else row - column
        out.append(jnp.exp(jnp.where(keep, diff, -1e30)))
    return jnp.concatenate(out, axis=1)


def mixed_heads(mix, high, low):
    mh, ml = two(mix)
    wide = mm(mh, jnp.concatenate([high, low], axis=1))
    return wide[:, :128] + wide[:, 128:] + mm(ml, high)


def head_lanes(inner):
    lane = lax.broadcasted_iota(jnp.int32, (1, 128), 1)
    return (lane >= HEAD0) & (lane < HEAD0 + inner // 64)


def front_body(parts, inner, states, quarter, s_ref, own, near, far, halo, gain, taps, bias, dbias, rate,
               *rest):
    ws = rest[:parts]
    normed_ref, u_ref, uh_ref, co_ref, hd_ref, hloc_ref, pre_ref, end_ref = rest[parts : parts + 8]
    hsc, usc, state, pre, esc, wsc = rest[parts + 8 :]
    b = pl.program_id(0)
    wide = inner + 2 * states
    shard = ws[0].shape[0]
    normed_ref[...] = normalize(pick(s_ref, b, quarter, own[...], near[...], far[...]), gain[...])[1]

    @pl.when(b == 0)
    def _():
        hsc[...] = normalize(halo[...], gain[...])[1]
        for j in range(parts):
            wsc[lanes_of(s_ref, j, shard)] = ws[j][...]
        edge = mm(hsc[...], wsc[:, :wide])
        edge = jnp.where(s_ref[HASPREV] > 0, edge[8:], 0.0)
        usc[0:8] = edge
        uh_ref[...] = edge
        state[...] = jnp.zeros_like(state)
        pre[...] = jnp.zeros_like(pre)
        esc[...] = expander(inner)

    @pl.when(b > 0)
    def _():
        usc[0:8] = usc[BLOCK : BLOCK + 8]

    u = mm(normed_ref[...], wsc[...])
    usc[8 : 8 + BLOCK] = u[:, :wide]
    u_ref[...] = u[:, :wide]
    conv = bias[...] + taps[0:1] * usc[5 : 5 + BLOCK]
    for k in range(1, 4):
        conv = conv + taps[k : k + 1] * usc[5 + k : 5 + k + BLOCK]
    co_ref[...] = conv
    raw = u[:, wide:] + dbias[...]
    delta = jnp.where(head_lanes(inner), jnp.maximum(raw, 0.0) + jnp.log1p(jnp.exp(-jnp.abs(raw))), 0.0)
    delta = delta * valid_rows(s_ref, b)
    level = running(triangle(True), delta * rate[...])
    raw = jnp.where(head_lanes(inner), raw, 0.0)
    hd_ref[...] = level + pltpu.roll(delta, STEP, 1) + pltpu.roll(raw, 2 * STEP, 1)
    both = mm(jnp.concatenate([three(level), three(delta)], axis=0), esc[...])
    level_x, delta_x = both[:BLOCK], both[BLOCK:]
    act = conv * jax.nn.sigmoid(conv)
    source = delta_x * act[:, :inner]
    inject_t = act[:, inner : inner + states].T
    for i in range(BLOCK // SUB):
        at = slice(i * SUB, (i + 1) * SUB)
        last = level_x[(i + 1) * SUB - 1 : (i + 1) * SUB]
        fresh = mm(inject_t[:, at], jnp.exp(last - level_x[at]) * source[at], precision=HIGH)
        before = state[...]
        n = b * (BLOCK // SUB) + i
        hloc_ref[i] = before
        pre_ref[n] = pre[...]
        state[...] = jnp.exp(last) * before + fresh
        pre[...] = pre[...] + last

    @pl.when(b == pl.num_programs(0) - 1)
    def _():
        end_ref[...] = state[...]
        pre_ref[n + 1] = pre[...]


def start_expanders(inner, *scs):
    @pl.when(pl.program_id(0) == 0)
    def _():
        for shift, sc in scs:
            sc[...] = expander(inner, shift)


def within_body(inner, states, s_ref, co, hd, yw_ref, lsc, dsc):
    start_expanders(inner, (0, lsc), (STEP, dsc))
    conv = co[...]
    act = conv * jax.nn.sigmoid(conv)
    level = hd[...]
    exact = three(level)
    lx = mm(exact, lsc[...])
    xs = mm(exact, dsc[...]) * act[:, :inner]
    keep = lax.broadcasted_iota(jnp.int32, (SUB, SUB), 0) >= lax.broadcasted_iota(jnp.int32, (SUB, SUB), 1)
    for i in range(BLOCK // SUB):
        at = slice(i * SUB, (i + 1) * SUB)
        affinity = mm(act[at, inner + states :], act[at, inner : inner + states], NT, HIGH)
        affinity = jnp.concatenate([affinity, affinity], axis=1)
        level_t = level[at].T
        level_x = lx[at]
        for pair in range(inner // 128):
            lanes = slice(pair * 128, pair * 128 + 128)
            mix = faded(keep, level, level_t, level_x, pair, True) * affinity
            yw_ref[at, lanes] = mixed_heads(mix, *stacked_heads(xs[at, lanes]))


def gates_body(parts, quarter, s_ref, normed, own, near, far, *rest):
    ws = rest[:parts]
    gate_ref, gg_ref, bg_ref, wsc = rest[parts:]
    b = pl.program_id(0)
    shard = ws[0].shape[0]
    inner = gate_ref.shape[1]
    up = pick(s_ref, b, quarter, own[...], near[...], far[...])
    bg_ref[...] = (up.astype(F32) * valid_rows(s_ref, b)).astype(BF16)

    @pl.when(b == 0)
    def _():
        for j in range(parts):
            wsc[lanes_of(s_ref, j, shard)] = ws[j][...]

    gate_ref[...] = mm(normed[...], wsc[:, :inner])
    gg_ref[...] = mm(bg_ref[...], wsc[:, inner:])


def entering(hloc, pre, hin):
    return hloc + jnp.exp(pre[0:1]) * hin


def output_body(inner, states, s_ref, co, hd, yw, gate, gg, hloc, pre, hin, skip, ggain, y_ref, sum_ref, lsc):
    start_expanders(inner, (0, lsc))
    lx = mm(three(hd[...]), lsc[...])
    conv = co[...]
    act = conv * jax.nn.sigmoid(conv)
    for i in range(BLOCK // SUB):
        at = slice(i * SUB, (i + 1) * SUB)
        held = entering(hloc[i], pre[i], hin[...])
        y_ref[at] = yw[at] + jnp.exp(lx[at]) * mm(act[at, inner + states :], held, precision=HIGH)
    out = y_ref[...] + skip[...] * act[:, :inner]
    g = gate[...]
    product = out * (g * jax.nn.sigmoid(g))
    ones = jnp.ones((8, 3 * inner), BF16)
    sum_ref[0:8] = mm(ones, three(product * product), NT)
    sum_ref[8:16] = mm(ones, three(gg[...] * ggain[...] * product), NT)


def turn_body(inner, states, total, s_ref, co, hd, y, gate, gg, sums, sums1, sums2, sums3, skip, ggain,
              gated_ref, ggrad_ref, og_ref, gloc_ref, start_ref, cols_ref, chain, lsc):
    start_expanders(inner, (0, lsc))
    lx = mm(three(hd[...]), lsc[...])
    step = pl.program_id(0)
    conv = co[...]
    act = conv * jax.nn.sigmoid(conv)
    x = act[:, :inner]
    readout_t = act[:, inner + states :].T
    both = (sums[...] + sums1[...] + sums2[...] + sums3[...]).T
    ginv = lax.rsqrt(both[:, 0:1] / total + EPSILON)
    dot = ginv * both[:, 8:9] / total
    g = gate[...]
    sig = jax.nn.sigmoid(g)
    ga = g * sig
    out = y[...] + skip[...] * x
    unit = out * ga * ginv
    gated_ref[...] = (unit * ggain[...]).astype(BF16)
    grad = gg[...]
    pg = ginv * (grad * ggain[...] - unit * dot)
    og = pg * ga
    og_ref[...] = og
    ggrad_ref[...] = (pg * out * slope(g, sig)).astype(BF16)

    @pl.when(step == 0)
    def _():
        chain[...] = jnp.zeros_like(chain)
        cols_ref[...] = jnp.zeros_like(cols_ref)

    cols_ref[0:1] += jnp.sum(grad * unit, axis=0, keepdims=True)
    cols_ref[1:2] += jnp.sum(og * x, axis=0, keepdims=True)
    b = pl.num_programs(0) - 1 - step
    for i in reversed(range(BLOCK // SUB)):
        at = slice(i * SUB, (i + 1) * SUB)
        held = chain[...]
        gloc_ref[i] = held
        level_x = lx[at]
        chain[...] = jnp.exp(level_x[SUB - 1 : SUB]) * held + mm(
            readout_t[:, at], jnp.exp(level_x) * og[at], precision=HIGH
        )

    @pl.when(b == 0)
    def _():
        start_ref[...] = chain[...]


def back_body(inner, states, s_ref, co, hd, og, hloc, pre, hin, z_ref, dbc_ref, lsc, dsc):
    start_expanders(inner, (0, lsc), (STEP, dsc))
    conv = co[...]
    act = conv * jax.nn.sigmoid(conv)
    level = hd[...]
    exact = three(level)
    lx = mm(exact, lsc[...])
    xs = mm(exact, dsc[...]) * act[:, :inner]
    keep = lax.broadcasted_iota(jnp.int32, (SUB, SUB), 1) >= lax.broadcasted_iota(jnp.int32, (SUB, SUB), 0)
    for i in range(BLOCK // SUB):
        at = slice(i * SUB, (i + 1) * SUB)
        inject, readout = act[at, inner : inner + states], act[at, inner + states :]
        affinity = mm(inject, readout, NT, HIGH)
        affinity = jnp.concatenate([affinity, affinity], axis=1)
        level_t = level[at].T
        level_x = lx[at]
        grad = jnp.zeros((SUB, SUB), F32)
        for pair in range(inner // 128):
            lanes = slice(pair * 128, pair * 128 + 128)
            fade = faded(keep, level, level_t, level_x, pair, False)
            g = og[at, lanes]
            z_ref[at, lanes] = mixed_heads(fade * affinity, *stacked_heads(g))
            xh, xl = stacked_heads(xs[at, lanes])
            gh, gl = two(g)
            outer = mm(
                jnp.concatenate([xh, xl], axis=1), jnp.concatenate([gh, gh], axis=1), NT
            ) + mm(xh, gl, NT)
            grad += fade[:, :SUB] * outer[:SUB] + fade[:, SUB:] * outer[SUB:]
        held = entering(hloc[i], pre[i], hin[...])
        dbc_ref[at, :states] = mm(grad, readout, precision=HIGH)
        dbc_ref[at, states:] = mm(grad.T, inject, precision=HIGH) + mm(
            jnp.exp(level_x) * og[at], held, NT, HIGH
        )


def conv_back(grad, csc, usc, taps, cols_ref):
    csc[0:BLOCK] = grad
    pre = taps[0:1] * csc[3 : 3 + BLOCK]
    for k in range(1, 4):
        pre = pre + taps[k : k + 1] * csc[3 - k : 3 - k + BLOCK]
    for k in range(4):
        cols_ref[k : k + 1] += jnp.sum(grad * usc[5 + k : 5 + k + BLOCK], axis=0, keepdims=True)
    cols_ref[4:5] += jnp.sum(grad, axis=0, keepdims=True)
    csc[BLOCK : BLOCK + 8] = grad[0:8]
    return pre


def meet_body(inner, states, s_ref, co, hd, z, dbc, hloc, hnext, hend, pre, gloc, gin, hin, og, skip, zed_ref, ends_ref, keep_ref,
              give_ref, head_ref, lsc, dsc):
    start_expanders(inner, (0, lsc), (STEP, dsc))
    exact = three(hd[...])
    lx = mm(exact, lsc[...])
    subs = BLOCK // SUB
    count = pl.num_programs(0)
    b = pl.program_id(0)
    conv = co[...]
    act = conv * jax.nn.sigmoid(conv)
    delta_x = mm(exact, dsc[...])
    source = delta_x * act[:, :inner]
    ends = []
    inject_grads = []
    for i in range(subs):
        at = slice(i * SUB, (i + 1) * SUB)
        n = b * subs + i + 1
        level_x = lx[at]
        later = gloc[i] + jnp.exp(pre[subs * count][0:1] - pre[n][0:1]) * gin[...]
        after = hloc[i + 1] if i < subs - 1 else jnp.where(b == count - 1, hend[...], hnext[0])
        fade = jnp.exp(level_x[SUB - 1 : SUB] - level_x)
        zed_ref[at] = z[at] + fade * mm(act[at, inner : inner + states], later, precision=HIGH)
        inject_grads.append(dbc[at, :states] + mm(fade * source[at], later, NT, HIGH))
        ends.append(jnp.sum(later * entering(after, pre[n], hin[...]), axis=0, keepdims=True))

    @pl.when(b == 0)
    def _():
        first = conv[0:8, :inner]
        grad = delta_x[0:8] * zed_ref[0:8] + skip[...] * og[...]
        head_ref[...] = grad * slope(first, jax.nn.sigmoid(first))

    ends_ref[...] = jnp.concatenate(ends + [jnp.zeros((8 - subs, inner), F32)], axis=0)
    inject_grad = jnp.concatenate(inject_grads, axis=0)
    half = count // 2
    rows = pl.ds(pl.multiple_of((b % half) * BLOCK, BLOCK), BLOCK)

    @pl.when(b // half == s_ref[CORE])
    def _():
        keep_ref[rows, :states] = inject_grad
        keep_ref[rows, states:] = dbc[:, states:]

    @pl.when(b // half != s_ref[CORE])
    def _():
        give_ref[rows, :states] = inject_grad
        give_ref[rows, states:] = dbc[:, states:]


def join_body(inner, s_ref, co, hd, og, y, zed_in, ends_in, u, prior, uh, taps, rate, skip, mg_ref,
              tail_ref, rg_ref, cols_ref, sig_ref, col_sc, csc, usc, dsc):
    start_expanders(inner, (STEP, dsc))
    step = pl.program_id(0)
    subs = BLOCK // SUB
    count = pl.num_programs(0)
    b = count - 1 - step

    @pl.when(step == 0)
    def _():
        cols_ref[...] = jnp.zeros_like(cols_ref)
        sig_ref[...] = jnp.zeros_like(sig_ref)
        col_sc[...] = collector(inner)
        csc[BLOCK : BLOCK + 8] = jnp.zeros((8, inner), F32)

    conv = co[...]
    sig = jax.nn.sigmoid(conv)
    x = conv * sig
    packed_heads = hd[...]
    delta_x = mm(three(packed_heads), dsc[...])
    zed = zed_in[...]
    ends = ends_in[...]
    g = og[...]
    sums = mm(three(jnp.concatenate([x * zed, g * y[...], ends], axis=0)), col_sc[...])
    direct, read, ends = sums[:BLOCK], sums[BLOCK : 2 * BLOCK], sums[2 * BLOCK :]
    dlt = jnp.where(head_lanes(inner), pltpu.roll(packed_heads, 128 - STEP, 1), 0.0)
    draw = pltpu.roll(packed_heads, 128 - 2 * STEP, 1)
    q = running(triangle(False), read - dlt * direct)
    q = jnp.concatenate([q[i * SUB : (i + 1) * SUB] + ends[i : i + 1] for i in range(subs)], axis=0)
    rg = (direct + rate[...] * q) * valid_rows(s_ref, b) * jax.nn.sigmoid(draw)
    rg = jnp.where(head_lanes(inner), rg, 0.0)
    rg_ref[...] = rg
    cols_ref[0:1] += jnp.sum(rg, axis=0, keepdims=True)
    cols_ref[1:2] += jnp.sum(dlt * q, axis=0, keepdims=True)

    usc[0:8] = jnp.where(b == 0, uh[...], prior[...])
    usc[8 : 8 + BLOCK] = u[...]
    grad = (delta_x * zed + skip[...] * g) * slope(conv, sig)
    pre_grad = conv_back(grad, csc, usc, taps, sig_ref)
    mg_ref[...] = pre_grad.astype(BF16)

    @pl.when(step == 0)
    def _():
        tail_ref[...] = pre_grad[BLOCK - 8 :]


def exponents(peak):
    return jnp.clip(jnp.ceil(jnp.log(jnp.maximum(peak, 1e-36)) * 1.4426950408889634) - 14.0, -100.0, 100.0)


def packed(value, power, inverse, riders=()):
    rows = [(value * inverse).astype(F16), jnp.broadcast_to(power, (16, value.shape[1])).astype(F16)]
    for more in riders:
        each = exponents(jnp.abs(more))
        rows += [(more * jnp.exp2(-each)).astype(F16), each.astype(F16)]
    return jnp.concatenate(rows)


def unpacked(sent, counts=()):
    rows = sent.shape[0] - 16 - 2 * sum(counts)
    power = sent[rows : rows + 1].astype(F32)
    more = []
    at = rows + 16
    for size in counts:
        more.append(sent[at : at + size].astype(F32) * jnp.exp2(sent[at + size : at + 2 * size].astype(F32)))
        at += 2 * size
    return sent[:rows].astype(F32) * jnp.exp2(power), power, more


def grads_body(parts, pairs, s_ref, *refs):
    inputs = 1 + max(max(pair) for pair in pairs)
    outs = refs[inputs : inputs + parts]
    powers, inverse, peak = refs[inputs + parts :]
    j = pl.program_id(0)

    @pl.when(j == 0)
    def _():
        peak[...] = jnp.zeros_like(peak)

    at = 0
    for left, right in pairs:
        value = mm(refs[left][...], refs[right][...], TN)
        lanes = slice(at, at + value.shape[1])
        at += value.shape[1]
        peak[0:1, lanes] = jnp.maximum(peak[0:1, lanes], jnp.max(jnp.abs(value), axis=0, keepdims=True))
        for k in range(parts):

            @pl.when(j == k)
            def _():
                outs[k][:, lanes] = value

    @pl.when(j == parts - 1)
    def _():
        power = exponents(peak[...])
        powers[...] = jnp.broadcast_to(power[0:1], (16, at))
        inverse[...] = jnp.exp2(-power[0:1])


def deal(s_ref, b, quarter, value, outs):
    place = b // quarter
    rows = pl.ds(pl.multiple_of((b % quarter) * BLOCK, BLOCK), BLOCK)
    at = (place % 2 != s_ref[CORE]).astype(jnp.int32) * 2 + (place // 2 != s_ref[LO]).astype(jnp.int32)
    for k in range(4):

        @pl.when(at == k)
        def _():
            outs[k][rows] = value


def feature_body(parts, quarter, s_ref, own, near, far, ggrad, mg, rg, dbc, dbc_other, co, u, prior, uh, ahead,
                 taps, *rest):
    ws1 = rest[:parts]
    ws2 = rest[parts : 2 * parts]
    outs = rest[2 * parts : 2 * parts + 4]
    xg_ref, cols_ref, state_ref, whole_sc, csc, usc = rest[2 * parts + 4 :]
    step = pl.program_id(0)
    count = pl.num_programs(0)
    b = count - 1 - step
    inner = ggrad.shape[1]
    shard = ws1[0].shape[0]

    @pl.when(step == 0)
    def _():
        cols_ref[...] = jnp.zeros_like(cols_ref)
        state_ref[...] = jnp.zeros_like(state_ref)
        csc[BLOCK : BLOCK + 8] = jnp.where(s_ref[HASNEXT] > 0, ahead[...], 0.0)

    usc[0:8] = jnp.where(b == 0, uh[...], prior[...])
    usc[8 : 8 + BLOCK] = u[...]
    conv = co[...]
    grad = jnp.where(b // (count // 2) == s_ref[CORE], dbc[...], dbc_other[...])
    grad = grad * slope(conv, jax.nn.sigmoid(conv))
    pre = conv_back(grad, csc, usc, taps, state_ref)
    pre = jnp.where(s_ref[CORE] > 0, pltpu.roll(pre, 64, 1), pre)
    lane = lax.broadcasted_iota(jnp.int32, (BLOCK, 128), 1)
    xg = jnp.where(lane < HEAD0, pre, rg[...]).astype(BF16)
    xg_ref[...] = xg
    for j in range(parts):
        at = lanes_of(s_ref, j, shard)
        whole_sc[:, at] = (
            mm(ggrad[...], ws2[j][:, :inner], NT)
            + mm(mg[...], ws1[j][:, :inner], NT)
            + mm(xg, ws1[j][:, -128:], NT)
        )
    value = whole_sc[...]
    scaled = normalize(pick(s_ref, b, quarter, own[...], near[...], far[...]), 1.0)[0]
    cols_ref[0:1] += jnp.sum(value * scaled, axis=0, keepdims=True)
    deal(s_ref, b, quarter, value, outs)


def branch_body(parts, quarter, s_ref, gated, *rest):
    ws2 = rest[:parts]
    outs = rest[parts : parts + 4]
    whole_sc = rest[parts + 4]
    inner = gated.shape[1]
    shard = ws2[0].shape[0]
    for j in range(parts):
        whole_sc[:, lanes_of(s_ref, j, shard)] = mm(gated[...], ws2[j][:, inner:], NT)
    deal(s_ref, pl.program_id(0), quarter, whole_sc[...], outs)


def finish_body(inner, s_ref, first, second, rate, taps_ref, bias_ref, gain_ref, staps_ref, sbias_ref, raw_ref,
                rate_ref, skip_ref, norm_ref):
    both = (first, second)
    heads = inner // 64
    lane = lax.broadcasted_iota(jnp.int32, (8, 128), 1)
    pairs, skips = [], []
    for n, part in enumerate(both):
        at = slice(n * inner, (n + 1) * inner)
        taps_ref[:, at] = part[0:4, :inner]
        bias_ref[:, at] = part[4:5, :inner]
        gain_ref[:, at] = part[8:9, :inner]
        here = slice(n * 128, (n + 1) * 128)
        staps_ref[:, here] = part[0:4, inner:]
        sbias_ref[:, here] = part[4:5, inner:]
        turn = (128 - HEAD0 + n * heads) % 128
        pairs.append(pltpu.roll(part[0:8, inner:], turn, 1))
        skips.append(pltpu.roll(mm(three(part[8:16, :inner]), collector(inner)), turn, 1))
    values = jnp.where(lane < heads, pairs[0], pairs[1])
    skip = jnp.where(lane < heads, skips[0], skips[1])
    raw_ref[...] = values[5:6, : 2 * heads]
    rate_ref[...] = values[6:7, : 2 * heads] * rate[...]
    skip_ref[...] = skip[1:2, : 2 * heads]
    norm_ref[...] = first[8:16, inner:] + second[8:16, inner:]


def per_device(
    hidden, lengths, cotangent, norm_gain, proj_main, proj_state, proj_delta, conv_main, conv_state,
    bias_main, bias_state, delta_bias, log_rate, skip_gain, gate_gain, proj_out,
):
    _, steps, model = hidden.shape
    hidden, cotangent = hidden[0], cotangent[0]
    dps, ctxs, tps = lax.axis_size("dp"), lax.axis_size("ctx"), lax.axis_size("tp")
    dp, z, core = lax.axis_index("dp"), lax.axis_index("ctx"), lax.axis_index("tp")
    lo, hi = z % 2, z // 2
    pairs = ctxs // 2
    tokens = 2 * steps
    count = tokens // BLOCK
    quarter = count // 4
    inner = bias_main.shape[0] // 2
    heads = delta_bias.shape[0] // 2
    states = bias_state.shape[0] // 2
    wide = inner + 2 * states

    def swap(value):
        return lax.ppermute(value, "tp", [(0, 1), (1, 0)])

    def across(value, j):
        return lax.ppermute(value, "ctx", [(i, i ^ j) for i in range(ctxs)])

    def along(value, step):
        return lax.ppermute(
            value, "ctx", [(i, i + step) for i in range(ctxs) if 0 <= i + step < ctxs]
        )

    def spread(value, j):
        return lax.ppermute(value, "dp", [(i, i ^ j) for i in range(dps)])

    def mine(value, axis, size):
        return lax.dynamic_slice_in_dim(value, lo * size, size, axis)

    def piece(value, at, size):
        return lax.dynamic_slice_in_dim(value, at * size, size, 0)

    apart = proj_main.shape[0] % 128 == 0
    parts = dps if apart else 1
    shard = proj_main.shape[0] * (dps // parts)

    def gathered(value):
        if not apart:
            return [lax.all_gather(value, "dp", axis=0, tiled=True)]
        return [value] + [spread(value, j) for j in range(1, dps)]

    scalars = jnp.stack(
        [lo, core, hi * tokens, lengths[0], (hi > 0).astype(jnp.int32), (hi < pairs - 1).astype(jnp.int32)]
        + [dp ^ j if apart else 0 * dp for j in range(parts)]
    ).astype(jnp.int32)

    state_own = lax.dynamic_slice_in_dim(proj_state, lo * states + core * (states // 2), states // 2, 1)
    delta_own = mine(proj_delta, 1, heads)
    main_part = mine(proj_main, 2, inner)
    first = jnp.concatenate(
        [main_part[:, 1], proj_state, state_own, delta_own,
         jnp.zeros((proj_main.shape[0], 64 - heads), BF16)], axis=1
    )
    halfway = steps // 2
    near = across(piece(hidden, core, halfway), 1)
    far = swap(near)
    ws1 = gathered(first)

    def payloads(pieces, scale, riders=()):
        return [packed(pieces[j], scale[0], scale[1], riders) for j in range(1, parts)]

    def over_sequences(payload):
        return [spread(payload[j - 1], j) for j in range(1, parts)]

    def totalled(pieces, scale, got, riders=()):
        total, power = pieces[0], scale[0][0:1]
        if not apart:
            total = lax.psum_scatter(total, "dp", scatter_dimension=0, tiled=True)
            power = exponents(jnp.max(jnp.abs(total), axis=0, keepdims=True))
            riders = [lax.psum(value, "dp") for value in riders]
        for sent in got:
            value, other, more = unpacked(sent, [rider.shape[0] for rider in riders])
            total, power = total + value, jnp.maximum(power, other)
            riders = [one + two for one, two in zip(riders, more)]
        return total, power + (parts - 1).bit_length(), riders

    def chunks(totals, power, riders=()):
        size = totals[0].shape[0] // ctxs
        rows = [jnp.concatenate([piece(total, z ^ j, size) for total in totals], axis=1) for j in range(ctxs)]
        return rows[:1] + [packed(value, power, jnp.exp2(-power), riders) for value in rows[1:]]

    def over_positions(cut):
        return [across(cut[j], j) for j in range(1, ctxs)]

    def settled(own, got):
        opposite = got[0]
        for j in range(2, ctxs):
            if j % 2 == 0:
                own = own + got[j - 1]
            else:
                opposite = opposite + got[j - 1]
        return jnp.where(lo == 0, own, opposite), jnp.where(lo == 0, opposite, own)

    def decoded(got, counts=()):
        return [unpacked(sent, counts)[0] for sent in got]

    def ridden(got, counts):
        return [unpacked(sent, counts)[2][0] for sent in got]

    taps_x = jnp.concatenate([mine(conv_main, 1, inner), conv_state], axis=1)
    bias_x = jnp.concatenate([mine(bias_main, 0, inner), bias_state])[None]
    rate_own = -jnp.exp(mine(log_rate, 0, heads))

    def in_heads(value):
        return jnp.pad(value, (HEAD0, 128 - HEAD0 - heads))[None]

    rate_row = in_heads(rate_own)
    dbias_row = in_heads(mine(delta_bias, 0, heads))
    skip_row = jnp.repeat(mine(skip_gain, 0, heads), inner // heads)[None]
    ggain_row = mine(gate_gain, 0, inner)[None]
    gain_row = norm_gain[None]
    edge, scalars, taps_x, bias_x, rate_row, dbias_row, _ = lax.optimization_barrier(
        (hidden[steps - 16 :], scalars, taps_x, bias_x, rate_row, dbias_row, first)
    )
    route = [
        ((z0 - 1) * tps + c, (z0 + c) * tps + c) for z0 in range(2, ctxs, 2) for c in range(2)
    ]
    edge = lax.ppermute(edge, ("ctx", "tp"), route)
    halo = jnp.where(core == lo, edge, swap(edge))

    near, cot_later = lax.optimization_barrier((near, cotangent))
    ws1, near, main_gate, out_later = lax.optimization_barrier((ws1, near, main_part[:, 0], proj_out))
    second = jnp.concatenate([main_gate, mine(out_later, 1, inner)], axis=1)
    ws2 = gathered(second)
    cot_near = across(piece(cot_later, core, halfway), 1)

    own_spec = pl.BlockSpec(
        (BLOCK, model), lambda b, s: (jnp.clip(b - s[LO] * 2 * quarter, 0, 2 * quarter - 1), 0)
    )
    part_spec = pl.BlockSpec((BLOCK, model), lambda b, s: (b % quarter, 0))
    subs = BLOCK // SUB
    last = count * subs
    state_block = pl.BlockSpec((subs, states, inner), lambda b, s: (b, 0, 0))
    pre_block = pl.BlockSpec((subs, 8, inner), lambda b, s: (b, 0, 0))

    normed, u, uh, conv, per_head, hloc, pre, own_end = grid_call(
        functools.partial(front_body, parts, inner, states, quarter),
        (count,),
        [own_spec, part_spec, part_spec, whole((16, model)), whole((1, model)), whole((4, wide)),
         whole((1, wide)), whole((1, 128)), whole((1, 128))] + [whole((shard, wide + 128))] * parts,
        [rows_spec(model), rows_spec(wide), whole((8, wide)), rows_spec(wide), rows_spec(128),
         state_block, whole((last + 1, 8, inner)), whole((states, inner))],
        [shaped((tokens, model), BF16), shaped((tokens, wide)), shaped((8, wide)), shaped((tokens, wide)),
         shaped((tokens, 128)), shaped((last, states, inner)), shaped((last + 1, 8, inner)),
         shaped((states, inner))],
        [pltpu.VMEM((16, model), BF16), pltpu.VMEM((8 + BLOCK, wide), F32), pltpu.VMEM((states, inner), F32),
         pltpu.VMEM((8, inner), F32), pltpu.VMEM((384, inner), BF16), pltpu.VMEM((model, wide + 128), BF16)],
        name="front",
    )(scalars, hidden, near, far, halo, gain_row, taps_x, bias_x, dbias_row, rate_row, *ws1)

    cot_near, own_end = lax.optimization_barrier((cot_near, own_end))
    cot_far = swap(cot_near)
    growth = jnp.exp(pre[last][0:1])
    carried = jnp.zeros_like(own_end)
    sending = own_end
    for hop in range(pairs - 1):
        carried = along(sending, 2)
        if hop < pairs - 2:
            sending = own_end + growth * carried

    (inside,) = grid_call(
        functools.partial(within_body, inner, states),
        (count,),
        [rows_spec(wide), rows_spec(128)],
        [rows_spec(inner)],
        [shaped((tokens, inner))],
        [pltpu.VMEM((384, inner), BF16)] * 2,
        name="within",
        limit=20 << 20,
    )(scalars, *streamed(conv, per_head))

    gate, gated_grad, branch_grad = grid_call(
        functools.partial(gates_body, parts, quarter),
        (count,),
        [rows_spec(model), own_spec, part_spec, part_spec] + [whole((shard, 2 * inner))] * parts,
        [rows_spec(inner), rows_spec(inner), rows_spec(model)],
        [shaped((tokens, inner)), shaped((tokens, inner)), kept((tokens, model), BF16)],
        [pltpu.VMEM((model, 2 * inner), BF16)],
        name="gates",
        limit=20 << 20,
    )(scalars, *streamed(normed, cotangent, cot_near, cot_far, *ws2))

    y, sums = grid_call(
        functools.partial(output_body, inner, states),
        (count,),
        [rows_spec(wide), rows_spec(128), rows_spec(inner), rows_spec(inner), rows_spec(inner), state_block,
         pre_block, whole((states, inner)), whole((1, inner)), whole((1, inner))],
        [rows_spec(inner), pl.BlockSpec((16, BLOCK), lambda b, s: (0, b))],
        [shaped((tokens, inner)), shaped((16, tokens))],
        [pltpu.VMEM((384, inner), BF16)],
        name="output",
        limit=20 << 20,
    )(scalars, *streamed(conv, per_head), inside, gate, gated_grad, *streamed(hloc), pre, carried, skip_row, ggain_row)

    corner = [(n, ((n // tps) ^ 1) * tps + (n % tps + 1) % tps) for n in range(ctxs * tps)]
    all_sums = [sums, swap(sums), across(sums, 1), lax.ppermute(sums, ("ctx", "tp"), corner)]

    def back(width, rows=BLOCK):
        return pl.BlockSpec((rows, width), lambda b, s: (count - 1 - b, 0))

    back_sums = pl.BlockSpec((16, BLOCK), lambda b, s: (0, count - 1 - b))
    gated, gate_grad, out_grad, gloc, own_start, turn_cols = grid_call(
        functools.partial(turn_body, inner, states, 2 * tps * inner),
        (count,),
        [back(wide), back(128), back(inner), back(inner), back(inner),
         back_sums, back_sums, back_sums, back_sums, whole((1, inner)), whole((1, inner))],
        [back(inner), back(inner), back(inner),
         pl.BlockSpec((subs, states, inner), lambda b, s: (count - 1 - b, 0, 0)), whole((states, inner)),
         whole((8, inner))],
        [shaped((tokens, inner), BF16), shaped((tokens, inner), BF16), kept((tokens, inner)),
         kept((last, states, inner)), shaped((states, inner)), shaped((8, inner))],
        [pltpu.VMEM((states, inner), F32), pltpu.VMEM((384, inner), BF16)],
        name="turn",
        limit=20 << 20,
    )(scalars, *streamed(conv, per_head), y, gate, gated_grad, *all_sums, skip_row, ggain_row)

    returned = jnp.zeros_like(own_start)
    sending = own_start
    for hop in range(pairs - 1):
        returned = along(sending, -2)
        if hop < pairs - 2:
            sending = own_start + growth * returned

    turned = pl.BlockSpec((tokens, shard), lambda j, s: (0, s[SLOT0 + j]))
    dealt_specs = [whole((halfway, model))] * 4
    dealt_shapes = [shaped((halfway, model))] * 4
    def grads(lefts, rights, name, limit=None):
        sources = []
        for left, right in zip(lefts, rights):
            sources += [left, right]
        width = sum(right.shape[1] for right in rights)
        specs = [turned if n % 2 == 0 else whole(source.shape) for n, source in enumerate(sources)]
        *pieces, powers, inverse = grid_call(
            functools.partial(grads_body, parts, [(n, n + 1) for n in range(0, len(sources), 2)]),
            (parts,),
            specs,
            [whole((shard, width))] * parts + [whole((16, width)), whole((1, width))],
            [shaped((shard, width))] * parts + [shaped((16, width)), shaped((1, width))],
            [pltpu.VMEM((8, width), F32)],
            name=name,
            limit=limit,
        )(scalars, *sources)
        return pieces, (powers, inverse)

    early, early_scale = grads(streamed(normed, branch_grad), [gate_grad, gated], "grad_early", 20 << 20)
    early_got = over_sequences(payloads(early, early_scale))
    early, out_grad = lax.optimization_barrier((early, out_grad))

    zed, dbc = grid_call(
        functools.partial(back_body, inner, states),
        (count,),
        [rows_spec(wide), rows_spec(128), rows_spec(inner), state_block, pre_block, whole((states, inner))],
        [rows_spec(inner), rows_spec(2 * states)],
        [shaped((tokens, inner)), shaped((tokens, 2 * states))],
        [pltpu.VMEM((384, inner), BF16)] * 2,
        name="back",
    )(scalars, conv, per_head, out_grad, hloc, pre, carried)

    gated_later, zed = lax.optimization_barrier((gated, zed))
    branch = grid_call(
        functools.partial(branch_body, parts, quarter),
        (count,),
        [rows_spec(inner)] + [whole((shard, 2 * inner))] * parts,
        dealt_specs,
        dealt_shapes,
        [pltpu.VMEM((BLOCK, model), F32)],
        name="branch",
    )(scalars, gated_later, *ws2)

    returned, early_got, branch = lax.optimization_barrier((returned, early_got, branch))
    front_rows = halfway // 4
    branch_give = swap(branch[3])
    branch_theirs = [branch[1][:front_rows] + branch_give[:front_rows], branch[1][front_rows:] + branch_give[front_rows:]]
    returned, branch_theirs = lax.optimization_barrier((returned, branch_theirs))
    branch_back = [across(branch_theirs[0], 1)]
    all_pre = whole((last + 1, 8, inner))
    per = BLOCK // 8
    half_rows = tokens // 2

    def back_lanes(width, lanes):
        return [
            pl.BlockSpec((BLOCK, width), lambda b, s: (count - 1 - b, lanes(s))),
            pl.BlockSpec((8, width), lambda b, s: (jnp.maximum((count - 1 - b) * per - 1, 0), lanes(s))),
            pl.BlockSpec((8, width), lambda b, s: (0, lanes(s))),
        ]

    def table(rows, width, lanes):
        return pl.BlockSpec((rows, width), lambda b, s: (0, lanes(s)))

    zed, ends, dbc_keep, dbc_give, head = grid_call(
        functools.partial(meet_body, inner, states),
        (count,),
        [rows_spec(wide), rows_spec(128), rows_spec(inner), rows_spec(2 * states), state_block,
         pl.BlockSpec((1, states, inner), lambda b, s: (jnp.minimum((b + 1) * subs, last - 1), 0, 0)),
         whole((states, inner)), all_pre, state_block, whole((states, inner)), whole((states, inner)), whole((8, inner)), whole((1, inner))],
        [rows_spec(inner), rows_spec(inner, 8), whole((half_rows, 2 * states)), whole((half_rows, 2 * states)),
         whole((8, inner))],
        [shaped((tokens, inner)), shaped((8 * count, inner)), shaped((half_rows, 2 * states)),
         shaped((half_rows, 2 * states)), shaped((8, inner))],
        [pltpu.VMEM((384, inner), BF16)] * 2,
        name="meet",
        limit=20 << 20,
    )(scalars, *streamed(conv, per_head, zed, dbc, hloc, hloc), own_end, *streamed(pre, gloc), returned, carried, *streamed(out_grad), skip_row)

    zed, ends, dbc_keep, dbc_give, branch_back = lax.optimization_barrier((zed, ends, dbc_keep, dbc_give, branch_back))
    early_total, early_power, _ = totalled(early, early_scale, early_got)
    early_cut = chunks([early_total], early_power)
    early_far = over_positions(early_cut)
    signal_pre, tail, raw_grad, head_cols, signal_cols = grid_call(
        functools.partial(join_body, inner),
        (count,),
        [back(inner), back(128), back(inner), back(inner), back(inner), back(inner, 8)]
        + back_lanes(inner, lambda s: 0)
        + [table(4, inner, lambda s: 0), whole((1, 128)), whole((1, inner))],
        [back(inner), whole((8, inner)), back(128), whole((8, 128)), whole((8, inner))],
        [shaped((tokens, inner), BF16), shaped((8, inner)), shaped((tokens, 128)),
         shaped((8, 128)), shaped((8, inner))],
        [pltpu.VMEM((3 * inner, 128), BF16), pltpu.VMEM((BLOCK + 8, inner), F32),
         pltpu.VMEM((BLOCK + 8, inner), F32), pltpu.VMEM((384, inner), BF16)],
        name="join",
        limit=20 << 20,
    )(scalars, *streamed(conv, per_head, out_grad, y), zed, ends, *streamed(u, u), uh, taps_x, rate_row, skip_row)

    tail, early_far = lax.optimization_barrier((tail, early_far))
    early_sum = settled(early_cut[0], decoded(early_far))
    out_sum = jnp.concatenate([part[:, inner:] for part in early_sum], axis=1)
    gate_sum = jnp.concatenate([part[:, :inner] for part in early_sum], axis=1)

    ahead, out_sum, gate_sum = lax.optimization_barrier((along(head, -2), out_sum, gate_sum))
    ahead = jnp.where(hi < pairs - 1, ahead, 0.0)
    for k in range(3):
        tail = tail + taps_x[k, :inner] * jnp.concatenate([jnp.zeros((5 + k, inner), F32), ahead[: 3 - k]])
    signal_pre = lax.dynamic_update_slice_in_dim(signal_pre, tail.astype(BF16), tokens - 8, 0)

    dbc = dbc_keep + swap(dbc_give)
    signal_pre, dbc = lax.optimization_barrier((signal_pre, dbc))
    dbc_back = across(lax.dynamic_slice_in_dim(dbc, (1 - lo) * states, states, 1), 1)
    signal_small = jnp.concatenate([signal_cols, turn_cols])
    signal, signal_scale = grads(streamed(normed), streamed(signal_pre), "grad_signal", 20 << 20)
    signal, dbc_back = lax.optimization_barrier((signal, dbc_back))
    signal_payload = payloads(signal, signal_scale, [signal_small])

    dbc = mine(dbc, 1, states) + dbc_back
    dbc_other = swap(dbc)
    head_rows = jnp.where(core == 0, dbc[:8], dbc_other[:8])
    head_conv = lax.dynamic_slice(conv, (0, inner + lo * states), (8, states))
    state_ahead = along(head_rows * slope(head_conv, jax.nn.sigmoid(head_conv)), -2)
    branch_later, state_ahead, signal_payload = lax.optimization_barrier((branch_theirs[1], state_ahead, signal_payload))
    signal_got = over_sequences(signal_payload)
    def back_own(b, s):
        return jnp.clip(count - 1 - b - s[LO] * 2 * quarter, 0, 2 * quarter - 1), 0

    def state_lanes(s):
        return inner // states + s[LO]

    back_part = pl.BlockSpec((BLOCK, model), lambda b, s: ((count - 1 - b) % quarter, 0))
    back_half = pl.BlockSpec((BLOCK, states), lambda b, s: ((count - 1 - b) % (count // 2), 0))
    state_side = back_lanes(states, state_lanes)
    *feature, extra_pre, feature_cols, state_cols = grid_call(
        functools.partial(feature_body, parts, quarter),
        (count,),
        [pl.BlockSpec((BLOCK, model), back_own), back_part, back_part, back(inner), back(inner), back(128),
         back_half, back_half, state_side[0]] + state_side
        + [whole((8, states)), table(4, states, state_lanes)]
        + [whole((shard, wide + 128))] * parts + [whole((shard, 2 * inner))] * parts,
        dealt_specs + [back(128), whole((8, model)), whole((8, states))],
        dealt_shapes + [shaped((tokens, 128), BF16), shaped((8, model)), shaped((8, states))],
        [pltpu.VMEM((BLOCK, model), F32), pltpu.VMEM((BLOCK + 8, states), F32),
         pltpu.VMEM((BLOCK + 8, states), F32)],
        name="feature",
        limit=24 << 20,
    )(scalars, *streamed(hidden, near, far, gate_grad, signal_pre, raw_grad), dbc, dbc_other, *streamed(conv, u, u), uh,
      state_ahead, taps_x, *streamed(*ws1, *ws2))
    feature, branch_rest, signal_got = lax.optimization_barrier((feature, across(branch_later, 1), signal_got))
    branch_back = jnp.concatenate(branch_back + [branch_rest])
    feature_theirs = feature[1] + swap(feature[3])
    feature_mine = feature[0] + swap(feature[2])

    folds = model // 128
    extra_small = jnp.concatenate(
        [state_cols[:5], head_cols[:2], jnp.zeros((1, 128), F32), feature_cols[0].reshape(folds, 128)]
    )
    feature_power = exponents(jnp.max(jnp.abs(feature_theirs), axis=0, keepdims=True))
    feature_payload = packed(feature_theirs, feature_power, jnp.exp2(-feature_power))
    extra_pre, feature_payload = lax.optimization_barrier((extra_pre, feature_payload))
    extra, extra_scale = grads(streamed(normed), [extra_pre], "grad_extra", 20 << 20)
    feature_back = across(feature_payload, 1)
    signal_total, signal_power, (signal_here,) = totalled(signal, signal_scale, signal_got, [signal_small])
    extra_got = over_sequences(payloads(extra, extra_scale, [extra_small]))
    extra_got, feature_back = lax.optimization_barrier((extra_got, feature_back))
    extra_total, extra_power, (extra_here,) = totalled(extra, extra_scale, extra_got, [extra_small])
    late_power = jnp.concatenate([signal_power, extra_power], axis=1)
    small_here = jnp.concatenate([signal_here, extra_here], axis=1)
    late_cut = chunks([signal_total, extra_total], late_power, [small_here])
    feature_back, late_cut = lax.optimization_barrier((feature_back, late_cut))
    late_far = over_positions(late_cut)
    feature_back = unpacked(feature_back)[0]

    def both_halves(value):
        other = swap(value)
        return jnp.where(core == 0, jnp.concatenate([value, other]), jnp.concatenate([other, value]))

    residual = piece(hidden, core, halfway).astype(F32)
    place = z * steps + core * halfway + lax.broadcasted_iota(jnp.int32, (halfway, 1), 0)
    valid = (place < lengths[0]).astype(F32)
    mixed = both_halves((residual + valid * (branch[0] + swap(branch[2]) + branch_back)).astype(BF16))

    feature_grad = feature_mine + feature_back
    inverse = lax.rsqrt(jnp.mean(residual * residual, axis=1, keepdims=True) + EPSILON)
    scaled_own = residual * inverse
    scaled_grad = feature_grad * norm_gain
    upstream = piece(cotangent, core, halfway).astype(F32)
    grad_hidden = both_halves(
        upstream + inverse * (scaled_grad - scaled_own * jnp.mean(scaled_grad * scaled_own, axis=1, keepdims=True))
    )

    mixed, grad_hidden, late_far = lax.optimization_barrier((mixed, grad_hidden, late_far))
    late_sum = settled(late_cut[0], decoded(late_far, [16]))
    small_sum = settled(small_here, ridden(late_far, [16]))

    def side_by_side(pair):
        return jnp.concatenate(pair, axis=-1)

    taps_sum, bias_sum, ggain_sum, state_taps, state_bias, raw_sum, rate_sum, skip_sum, gain_here = grid_call(
        functools.partial(finish_body, inner),
        (1,),
        [whole((16, inner + 128)), whole((16, inner + 128)), whole((1, 2 * heads))],
        [whole((4, 2 * inner)), whole((1, 2 * inner)), whole((1, 2 * inner)), whole((4, 2 * states)),
         whole((1, 2 * states)), whole((1, 2 * heads)), whole((1, 2 * heads)), whole((1, 2 * heads)),
         whole((8, 128))],
        [shaped((4, 2 * inner)), shaped((1, 2 * inner)), shaped((1, 2 * inner)), shaped((4, 2 * states)),
         shaped((1, 2 * states)), shaped((1, 2 * heads)), shaped((1, 2 * heads)), shaped((1, 2 * heads)),
         shaped((8, 128))],
        name="finish",
    )(scalars, *small_sum, -jnp.exp(log_rate)[None])
    gain_here = gain_here.reshape(model)
    state_here = jnp.stack([part[:, inner : inner + HEAD0] for part in late_sum])
    gain_there, state_there = swap(gain_here), swap(state_here)
    gain_size = model // (dps * ctxs)
    gain_sum = piece(gain_here + gain_there, dp * ctxs + z, gain_size)
    in_order = jnp.where(
        core == 0, jnp.stack([state_here, state_there], 1), jnp.stack([state_there, state_here], 1)
    )
    state_sum = jnp.transpose(in_order, (2, 0, 1, 3)).reshape(-1, 2 * states)
    main_sum = jnp.stack([gate_sum, side_by_side([part[:, :inner] for part in late_sum])], axis=1)
    delta_sum = side_by_side([part[:, inner + HEAD0 : inner + HEAD0 + heads] for part in late_sum])

    return (
        mixed[None],
        grad_hidden[None],
        gain_sum,
        main_sum,
        state_sum,
        delta_sum,
        taps_sum,
        state_taps,
        bias_sum[0],
        state_bias[0],
        raw_sum[0],
        rate_sum[0],
        skip_sum[0],
        ggain_sum[0],
        out_sum,
    )


def solution(mesh):
    in_specs = (
        P("dp", "ctx", None), P("dp"), P("dp", "ctx", None), P(), P("dp", None, "tp"), P("dp", None),
        P("dp", "tp"), P(None, "tp"), P(), P("tp"), P(), P("tp"), P("tp"), P("tp"), P("tp"), P("dp", "tp"),
    )
    out_specs = (
        P("dp", "ctx", None), P("dp", "ctx", None), P(("dp", "ctx")), P(("dp", "ctx"), None, "tp"),
        P(("dp", "ctx"), None), P(("dp", "ctx"), "tp"), P(None, "tp"), P(), P("tp"), P(), P("tp"), P("tp"),
        P("tp"), P("tp"), P(("dp", "ctx"), "tp"),
    )
    return jax.shard_map(
        per_device, mesh=mesh, in_specs=in_specs, out_specs=out_specs, check_vma=False
    )
```

```python
import functools

import jax
import jax.numpy as jnp
from jax import lax
from jax.experimental import pallas as pl
from jax.experimental.pallas import tpu as pltpu
from jax.sharding import PartitionSpec as P

BLOCK = 256
SUB = 128
EPSILON = 1e-05
HIGH = lax.Precision.HIGH
HIGHEST = lax.Precision.HIGHEST
F32 = jnp.float32
BF16 = jnp.bfloat16
F16 = jnp.float16
NN = (((1,), (0,)), ((), ()))
NT = (((1,), (1,)), ((), ()))
TN = (((0,), (0,)), ((), ()))
HEAD0 = 64
STEP = 16
LO, CORE, BASE, LENGTH, HASPREV, HASNEXT, SLOT0 = range(7)


def mm(a, b, dims=NN, precision=None):
    return lax.dot_general(a, b, dims, precision=precision, preferred_element_type=F32)


def grid_call(body, grid, in_specs, out_specs, out_shape, scratch=(), name=None, limit=None):
    return pl.pallas_call(
        body,
        grid_spec=pltpu.PrefetchScalarGridSpec(
            num_scalar_prefetch=1,
            grid=grid,
            in_specs=in_specs,
            out_specs=out_specs,
            scratch_shapes=list(scratch),
        ),
        out_shape=out_shape,
        compiler_params=pltpu.CompilerParams(
            dimension_semantics=("arbitrary",) * len(grid), vmem_limit_bytes=limit
        ),
        name=name,
    )


def streamed(*arrays):
    return [pltpu.with_memory_space_constraint(array, pltpu.HBM) for array in arrays]


def rows_spec(width, rows=BLOCK, lane=0):
    return pl.BlockSpec((rows, width), lambda b, s: (b, lane))


def whole(shape):
    return pl.BlockSpec(shape, lambda b, s: (0,) * len(shape))


def shaped(shape, dtype=F32):
    return jax.ShapeDtypeStruct(shape, dtype)


def kept(shape, dtype=F32):
    return pltpu.HBM(shape, dtype)


def slope(v, sig):
    return sig * (1.0 + v * (1.0 - sig))


def lanes_of(s_ref, slot, width):
    return pl.ds(pl.multiple_of(s_ref[SLOT0 + slot] * width, width), width)


def normalize(x, gain):
    value = x.astype(F32)
    inverse = lax.rsqrt(jnp.mean(value * value, axis=1, keepdims=True) + EPSILON)
    scaled = value * inverse
    return scaled, (scaled * gain).astype(BF16)


def pick(s_ref, b, quarter, own, near, far):
    lo, core = s_ref[LO], s_ref[CORE]
    place = b // quarter
    mine = (place // 2) == lo
    from_near = (place % 2) == core
    return jnp.where(mine, own, jnp.where(from_near, near, far))


def valid_rows(s_ref, b):
    position = s_ref[BASE] + b * BLOCK + lax.broadcasted_iota(jnp.int32, (BLOCK, 1), 0)
    return (position < s_ref[LENGTH]).astype(F32)


def expander(inner, shift=0):
    lane = lax.broadcasted_iota(jnp.int32, (384, inner), 0) % 128 - HEAD0 - shift
    head = lax.broadcasted_iota(jnp.int32, (384, inner), 1) // 64
    return (lane == head).astype(F32).astype(BF16)


def collector(inner):
    head = lax.broadcasted_iota(jnp.int32, (3 * inner, 128), 0) % inner // 64
    lane = lax.broadcasted_iota(jnp.int32, (3 * inner, 128), 1) - HEAD0
    return (lane == head).astype(F32).astype(BF16)


def two(x):
    high = x.astype(BF16)
    return high, (x - high.astype(F32)).astype(BF16)


def three(x, axis=1):
    high = x.astype(BF16)
    rest = x - high.astype(F32)
    middle = rest.astype(BF16)
    return jnp.concatenate([high, middle, (rest - middle.astype(F32)).astype(BF16)], axis=axis)


def running(tri, x):
    width = x.shape[1]
    wide = mm(tri, three(x))
    return wide[:, :width] + wide[:, width : 2 * width] + wide[:, 2 * width :]


def triangle(forward):
    row = lax.broadcasted_iota(jnp.int32, (BLOCK, BLOCK), 0)
    col = lax.broadcasted_iota(jnp.int32, (BLOCK, BLOCK), 1)
    same = (row // SUB) == (col // SUB)
    keep = (row >= col) if forward else (col >= row)
    return (same & keep).astype(F32).astype(BF16)


def stacked_heads(x):
    half = lax.broadcasted_iota(jnp.int32, (1, 128), 1) < 64
    return two(jnp.concatenate([jnp.where(half, x, 0.0), jnp.where(half, 0.0, x)], axis=0))


def faded(keep, level, level_t, level_x, pair, forward):
    out = []
    for side in range(2):
        h = HEAD0 + 2 * pair + side
        at = pair * 128 + side * 64
        column, row = level_x[:, at : at + 1], level_t[h : h + 1, :]
        diff = column - row if forward else row - column
        out.append(jnp.exp(jnp.where(keep, diff, -1e30)))
    return jnp.concatenate(out, axis=1)


def mixed_heads(mix, high, low):
    mh, ml = two(mix)
    wide = mm(mh, jnp.concatenate([high, low], axis=1))
    return wide[:, :128] + wide[:, 128:] + mm(ml, high)


def head_lanes(inner):
    lane = lax.broadcasted_iota(jnp.int32, (1, 128), 1)
    return (lane >= HEAD0) & (lane < HEAD0 + inner // 64)


def front_body(parts, inner, states, quarter, s_ref, own, near, far, halo, gain, taps, bias, dbias, rate,
               *rest):
    ws = rest[:parts]
    normed_ref, u_ref, uh_ref, co_ref, hd_ref, hloc_ref, pre_ref, end_ref = rest[parts : parts + 8]
    hsc, usc, state, pre, esc, wsc = rest[parts + 8 :]
    b = pl.program_id(0)
    wide = inner + 2 * states
    shard = ws[0].shape[0]
    normed_ref[...] = normalize(pick(s_ref, b, quarter, own[...], near[...], far[...]), gain[...])[1]

    @pl.when(b == 0)
    def _():
        hsc[...] = normalize(halo[...], gain[...])[1]
        for j in range(parts):
            wsc[lanes_of(s_ref, j, shard)] = ws[j][...]
        edge = mm(hsc[...], wsc[:, :wide])
        edge = jnp.where(s_ref[HASPREV] > 0, edge[8:], 0.0)
        usc[0:8] = edge
        uh_ref[...] = edge
        state[...] = jnp.zeros_like(state)
        pre[...] = jnp.zeros_like(pre)
        esc[...] = expander(inner)

    @pl.when(b > 0)
    def _():
        usc[0:8] = usc[BLOCK : BLOCK + 8]

    u = mm(normed_ref[...], wsc[...])
    usc[8 : 8 + BLOCK] = u[:, :wide]
    u_ref[...] = u[:, :wide]
    conv = bias[...] + taps[0:1] * usc[5 : 5 + BLOCK]
    for k in range(1, 4):
        conv = conv + taps[k : k + 1] * usc[5 + k : 5 + k + BLOCK]
    co_ref[...] = conv
    raw = u[:, wide:] + dbias[...]
    delta = jnp.where(head_lanes(inner), jnp.maximum(raw, 0.0) + jnp.log1p(jnp.exp(-jnp.abs(raw))), 0.0)
    delta = delta * valid_rows(s_ref, b)
    level = running(triangle(True), delta * rate[...])
    raw = jnp.where(head_lanes(inner), raw, 0.0)
    hd_ref[...] = level + pltpu.roll(delta, STEP, 1) + pltpu.roll(raw, 2 * STEP, 1)
    both = mm(jnp.concatenate([three(level), three(delta)], axis=0), esc[...])
    level_x, delta_x = both[:BLOCK], both[BLOCK:]
    act = conv * jax.nn.sigmoid(conv)
    source = delta_x * act[:, :inner]
    inject_t = act[:, inner : inner + states].T
    for i in range(BLOCK // SUB):
        at = slice(i * SUB, (i + 1) * SUB)
        last = level_x[(i + 1) * SUB - 1 : (i + 1) * SUB]
        fresh = mm(inject_t[:, at], jnp.exp(last - level_x[at]) * source[at], precision=HIGH)
        before = state[...]
        n = b * (BLOCK // SUB) + i
        hloc_ref[i] = before
        pre_ref[n] = pre[...]
        state[...] = jnp.exp(last) * before + fresh
        pre[...] = pre[...] + last

    @pl.when(b == pl.num_programs(0) - 1)
    def _():
        end_ref[...] = state[...]
        pre_ref[n + 1] = pre[...]


def start_expanders(inner, *scs):
    @pl.when(pl.program_id(0) == 0)
    def _():
        for shift, sc in scs:
            sc[...] = expander(inner, shift)


def within_body(inner, states, s_ref, co, hd, yw_ref, lsc, dsc):
    start_expanders(inner, (0, lsc), (STEP, dsc))
    conv = co[...]
    act = conv * jax.nn.sigmoid(conv)
    level = hd[...]
    exact = three(level)
    lx = mm(exact, lsc[...])
    xs = mm(exact, dsc[...]) * act[:, :inner]
    keep = lax.broadcasted_iota(jnp.int32, (SUB, SUB), 0) >= lax.broadcasted_iota(jnp.int32, (SUB, SUB), 1)
    for i in range(BLOCK // SUB):
        at = slice(i * SUB, (i + 1) * SUB)
        affinity = mm(act[at, inner + states :], act[at, inner : inner + states], NT, HIGH)
        affinity = jnp.concatenate([affinity, affinity], axis=1)
        level_t = level[at].T
        level_x = lx[at]
        for pair in range(inner // 128):
            lanes = slice(pair * 128, pair * 128 + 128)
            mix = faded(keep, level, level_t, level_x, pair, True) * affinity
            yw_ref[at, lanes] = mixed_heads(mix, *stacked_heads(xs[at, lanes]))


def gates_body(parts, quarter, s_ref, normed, own, near, far, *rest):
    ws = rest[:parts]
    gate_ref, gg_ref, bg_ref, wsc = rest[parts:]
    b = pl.program_id(0)
    shard = ws[0].shape[0]
    inner = gate_ref.shape[1]
    up = pick(s_ref, b, quarter, own[...], near[...], far[...])
    bg_ref[...] = (up.astype(F32) * valid_rows(s_ref, b)).astype(BF16)

    @pl.when(b == 0)
    def _():
        for j in range(parts):
            wsc[lanes_of(s_ref, j, shard)] = ws[j][...]

    gate_ref[...] = mm(normed[...], wsc[:, :inner])
    gg_ref[...] = mm(bg_ref[...], wsc[:, inner:])


def entering(hloc, pre, hin):
    return hloc + jnp.exp(pre[0:1]) * hin


def output_body(inner, states, s_ref, co, hd, yw, gate, gg, hloc, pre, hin, skip, ggain, y_ref, sum_ref, lsc):
    start_expanders(inner, (0, lsc))
    lx = mm(three(hd[...]), lsc[...])
    conv = co[...]
    act = conv * jax.nn.sigmoid(conv)
    for i in range(BLOCK // SUB):
        at = slice(i * SUB, (i + 1) * SUB)
        held = entering(hloc[i], pre[i], hin[...])
        y_ref[at] = yw[at] + jnp.exp(lx[at]) * mm(act[at, inner + states :], held, precision=HIGH)
    out = y_ref[...] + skip[...] * act[:, :inner]
    g = gate[...]
    product = out * (g * jax.nn.sigmoid(g))
    ones = jnp.ones((8, 3 * inner), BF16)
    sum_ref[0:8] = mm(ones, three(product * product), NT)
    sum_ref[8:16] = mm(ones, three(gg[...] * ggain[...] * product), NT)


def turn_body(inner, states, total, s_ref, co, hd, y, gate, gg, sums, sums1, sums2, sums3, skip, ggain,
              gated_ref, ggrad_ref, og_ref, gloc_ref, start_ref, cols_ref, chain, lsc):
    start_expanders(inner, (0, lsc))
    lx = mm(three(hd[...]), lsc[...])
    step = pl.program_id(0)
    conv = co[...]
    act = conv * jax.nn.sigmoid(conv)
    x = act[:, :inner]
    readout_t = act[:, inner + states :].T
    both = (sums[...] + sums1[...] + sums2[...] + sums3[...]).T
    ginv = lax.rsqrt(both[:, 0:1] / total + EPSILON)
    dot = ginv * both[:, 8:9] / total
    g = gate[...]
    sig = jax.nn.sigmoid(g)
    ga = g * sig
    out = y[...] + skip[...] * x
    unit = out * ga * ginv
    gated_ref[...] = (unit * ggain[...]).astype(BF16)
    grad = gg[...]
    pg = ginv * (grad * ggain[...] - unit * dot)
    og = pg * ga
    og_ref[...] = og
    ggrad_ref[...] = (pg * out * slope(g, sig)).astype(BF16)

    @pl.when(step == 0)
    def _():
        chain[...] = jnp.zeros_like(chain)
        cols_ref[...] = jnp.zeros_like(cols_ref)

    cols_ref[0:1] += jnp.sum(grad * unit, axis=0, keepdims=True)
    cols_ref[1:2] += jnp.sum(og * x, axis=0, keepdims=True)
    b = pl.num_programs(0) - 1 - step
    for i in reversed(range(BLOCK // SUB)):
        at = slice(i * SUB, (i + 1) * SUB)
        held = chain[...]
        gloc_ref[i] = held
        level_x = lx[at]
        chain[...] = jnp.exp(level_x[SUB - 1 : SUB]) * held + mm(
            readout_t[:, at], jnp.exp(level_x) * og[at], precision=HIGH
        )

    @pl.when(b == 0)
    def _():
        start_ref[...] = chain[...]


def back_body(inner, states, s_ref, co, hd, og, hloc, pre, hin, z_ref, dbc_ref, lsc, dsc):
    start_expanders(inner, (0, lsc), (STEP, dsc))
    conv = co[...]
    act = conv * jax.nn.sigmoid(conv)
    level = hd[...]
    exact = three(level)
    lx = mm(exact, lsc[...])
    xs = mm(exact, dsc[...]) * act[:, :inner]
    keep = lax.broadcasted_iota(jnp.int32, (SUB, SUB), 1) >= lax.broadcasted_iota(jnp.int32, (SUB, SUB), 0)
    for i in range(BLOCK // SUB):
        at = slice(i * SUB, (i + 1) * SUB)
        inject, readout = act[at, inner : inner + states], act[at, inner + states :]
        affinity = mm(inject, readout, NT, HIGH)
        affinity = jnp.concatenate([affinity, affinity], axis=1)
        level_t = level[at].T
        level_x = lx[at]
        grad = jnp.zeros((SUB, SUB), F32)
        for pair in range(inner // 128):
            lanes = slice(pair * 128, pair * 128 + 128)
            fade = faded(keep, level, level_t, level_x, pair, False)
            g = og[at, lanes]
            z_ref[at, lanes] = mixed_heads(fade * affinity, *stacked_heads(g))
            xh, xl = stacked_heads(xs[at, lanes])
            gh, gl = two(g)
            outer = mm(
                jnp.concatenate([xh, xl], axis=1), jnp.concatenate([gh, gh], axis=1), NT
            ) + mm(xh, gl, NT)
            grad += fade[:, :SUB] * outer[:SUB] + fade[:, SUB:] * outer[SUB:]
        held = entering(hloc[i], pre[i], hin[...])
        dbc_ref[at, :states] = mm(grad, readout, precision=HIGH)
        dbc_ref[at, states:] = mm(grad.T, inject, precision=HIGH) + mm(
            jnp.exp(level_x) * og[at], held, NT, HIGH
        )


def conv_back(grad, csc, usc, taps, cols_ref):
    csc[0:BLOCK] = grad
    pre = taps[0:1] * csc[3 : 3 + BLOCK]
    for k in range(1, 4):
        pre = pre + taps[k : k + 1] * csc[3 - k : 3 - k + BLOCK]
    for k in range(4):
        cols_ref[k : k + 1] += jnp.sum(grad * usc[5 + k : 5 + k + BLOCK], axis=0, keepdims=True)
    cols_ref[4:5] += jnp.sum(grad, axis=0, keepdims=True)
    csc[BLOCK : BLOCK + 8] = grad[0:8]
    return pre


def meet_body(inner, states, s_ref, co, hd, z, dbc, hloc, hnext, hend, pre, gloc, gin, hin, og, skip, zed_ref, ends_ref, keep_ref,
              give_ref, head_ref, lsc, dsc):
    start_expanders(inner, (0, lsc), (STEP, dsc))
    exact = three(hd[...])
    lx = mm(exact, lsc[...])
    subs = BLOCK // SUB
    count = pl.num_programs(0)
    b = pl.program_id(0)
    conv = co[...]
    act = conv * jax.nn.sigmoid(conv)
    delta_x = mm(exact, dsc[...])
    source = delta_x * act[:, :inner]
    ends = []
    inject_grads = []
    for i in range(subs):
        at = slice(i * SUB, (i + 1) * SUB)
        n = b * subs + i + 1
        level_x = lx[at]
        later = gloc[i] + jnp.exp(pre[subs * count][0:1] - pre[n][0:1]) * gin[...]
        after = hloc[i + 1] if i < subs - 1 else jnp.where(b == count - 1, hend[...], hnext[0])
        fade = jnp.exp(level_x[SUB - 1 : SUB] - level_x)
        zed_ref[at] = z[at] + fade * mm(act[at, inner : inner + states], later, precision=HIGH)
        inject_grads.append(dbc[at, :states] + mm(fade * source[at], later, NT, HIGH))
        ends.append(jnp.sum(later * entering(after, pre[n], hin[...]), axis=0, keepdims=True))

    @pl.when(b == 0)
    def _():
        first = conv[0:8, :inner]
        grad = delta_x[0:8] * zed_ref[0:8] + skip[...] * og[...]
        head_ref[...] = grad * slope(first, jax.nn.sigmoid(first))

    ends_ref[...] = jnp.concatenate(ends + [jnp.zeros((8 - subs, inner), F32)], axis=0)
    inject_grad = jnp.concatenate(inject_grads, axis=0)
    half = count // 2
    rows = pl.ds(pl.multiple_of((b % half) * BLOCK, BLOCK), BLOCK)

    @pl.when(b // half == s_ref[CORE])
    def _():
        keep_ref[rows, :states] = inject_grad
        keep_ref[rows, states:] = dbc[:, states:]

    @pl.when(b // half != s_ref[CORE])
    def _():
        give_ref[rows, :states] = inject_grad
        give_ref[rows, states:] = dbc[:, states:]


def join_body(inner, s_ref, co, hd, og, y, zed_in, ends_in, u, prior, uh, taps, rate, skip, mg_ref,
              tail_ref, rg_ref, cols_ref, sig_ref, col_sc, csc, usc, dsc):
    start_expanders(inner, (STEP, dsc))
    step = pl.program_id(0)
    subs = BLOCK // SUB
    count = pl.num_programs(0)
    b = count - 1 - step

    @pl.when(step == 0)
    def _():
        cols_ref[...] = jnp.zeros_like(cols_ref)
        sig_ref[...] = jnp.zeros_like(sig_ref)
        col_sc[...] = collector(inner)
        csc[BLOCK : BLOCK + 8] = jnp.zeros((8, inner), F32)

    conv = co[...]
    sig = jax.nn.sigmoid(conv)
    x = conv * sig
    packed_heads = hd[...]
    delta_x = mm(three(packed_heads), dsc[...])
    zed = zed_in[...]
    ends = ends_in[...]
    g = og[...]
    sums = mm(three(jnp.concatenate([x * zed, g * y[...], ends], axis=0)), col_sc[...])
    direct, read, ends = sums[:BLOCK], sums[BLOCK : 2 * BLOCK], sums[2 * BLOCK :]
    dlt = jnp.where(head_lanes(inner), pltpu.roll(packed_heads, 128 - STEP, 1), 0.0)
    draw = pltpu.roll(packed_heads, 128 - 2 * STEP, 1)
    q = running(triangle(False), read - dlt * direct)
    q = jnp.concatenate([q[i * SUB : (i + 1) * SUB] + ends[i : i + 1] for i in range(subs)], axis=0)
    rg = (direct + rate[...] * q) * valid_rows(s_ref, b) * jax.nn.sigmoid(draw)
    rg = jnp.where(head_lanes(inner), rg, 0.0)
    rg_ref[...] = rg
    cols_ref[0:1] += jnp.sum(rg, axis=0, keepdims=True)
    cols_ref[1:2] += jnp.sum(dlt * q, axis=0, keepdims=True)

    usc[0:8] = jnp.where(b == 0, uh[...], prior[...])
    usc[8 : 8 + BLOCK] = u[...]
    grad = (delta_x * zed + skip[...] * g) * slope(conv, sig)
    pre_grad = conv_back(grad, csc, usc, taps, sig_ref)
    mg_ref[...] = pre_grad.astype(BF16)

    @pl.when(step == 0)
    def _():
        tail_ref[...] = pre_grad[BLOCK - 8 :]


def exponents(peak):
    return jnp.clip(jnp.ceil(jnp.log(jnp.maximum(peak, 1e-36)) * 1.4426950408889634) - 14.0, -100.0, 100.0)


def packed(value, power, inverse, riders=()):
    rows = [(value * inverse).astype(F16), jnp.broadcast_to(power, (16, value.shape[1])).astype(F16)]
    for more in riders:
        each = exponents(jnp.abs(more))
        rows += [(more * jnp.exp2(-each)).astype(F16), each.astype(F16)]
    return jnp.concatenate(rows)


def unpacked(sent, counts=()):
    rows = sent.shape[0] - 16 - 2 * sum(counts)
    power = sent[rows : rows + 1].astype(F32)
    more = []
    at = rows + 16
    for size in counts:
        more.append(sent[at : at + size].astype(F32) * jnp.exp2(sent[at + size : at + 2 * size].astype(F32)))
        at += 2 * size
    return sent[:rows].astype(F32) * jnp.exp2(power), power, more


def grads_body(parts, pairs, s_ref, *refs):
    inputs = 1 + max(max(pair) for pair in pairs)
    outs = refs[inputs : inputs + parts]
    powers, inverse, peak = refs[inputs + parts :]
    j = pl.program_id(0)

    @pl.when(j == 0)
    def _():
        peak[...] = jnp.zeros_like(peak)

    at = 0
    for left, right in pairs:
        value = mm(refs[left][...], refs[right][...], TN)
        lanes = slice(at, at + value.shape[1])
        at += value.shape[1]
        peak[0:1, lanes] = jnp.maximum(peak[0:1, lanes], jnp.max(jnp.abs(value), axis=0, keepdims=True))
        for k in range(parts):

            @pl.when(j == k)
            def _():
                outs[k][:, lanes] = value

    @pl.when(j == parts - 1)
    def _():
        power = exponents(peak[...])
        powers[...] = jnp.broadcast_to(power[0:1], (16, at))
        inverse[...] = jnp.exp2(-power[0:1])


def deal(s_ref, b, quarter, value, outs):
    place = b // quarter
    rows = pl.ds(pl.multiple_of((b % quarter) * BLOCK, BLOCK), BLOCK)
    at = (place % 2 != s_ref[CORE]).astype(jnp.int32) * 2 + (place // 2 != s_ref[LO]).astype(jnp.int32)
    for k in range(4):

        @pl.when(at == k)
        def _():
            outs[k][rows] = value


def feature_body(parts, quarter, s_ref, own, near, far, ggrad, mg, rg, dbc, dbc_other, co, u, prior, uh, ahead,
                 taps, *rest):
    ws1 = rest[:parts]
    ws2 = rest[parts : 2 * parts]
    outs = rest[2 * parts : 2 * parts + 4]
    xg_ref, cols_ref, state_ref, whole_sc, csc, usc = rest[2 * parts + 4 :]
    step = pl.program_id(0)
    count = pl.num_programs(0)
    b = count - 1 - step
    inner = ggrad.shape[1]
    shard = ws1[0].shape[0]

    @pl.when(step == 0)
    def _():
        cols_ref[...] = jnp.zeros_like(cols_ref)
        state_ref[...] = jnp.zeros_like(state_ref)
        csc[BLOCK : BLOCK + 8] = jnp.where(s_ref[HASNEXT] > 0, ahead[...], 0.0)

    usc[0:8] = jnp.where(b == 0, uh[...], prior[...])
    usc[8 : 8 + BLOCK] = u[...]
    conv = co[...]
    grad = jnp.where(b // (count // 2) == s_ref[CORE], dbc[...], dbc_other[...])
    grad = grad * slope(conv, jax.nn.sigmoid(conv))
    pre = conv_back(grad, csc, usc, taps, state_ref)
    pre = jnp.where(s_ref[CORE] > 0, pltpu.roll(pre, 64, 1), pre)
    lane = lax.broadcasted_iota(jnp.int32, (BLOCK, 128), 1)
    xg = jnp.where(lane < HEAD0, pre, rg[...]).astype(BF16)
    xg_ref[...] = xg
    for j in range(parts):
        at = lanes_of(s_ref, j, shard)
        whole_sc[:, at] = (
            mm(ggrad[...], ws2[j][:, :inner], NT)
            + mm(mg[...], ws1[j][:, :inner], NT)
            + mm(xg, ws1[j][:, -128:], NT)
        )
    value = whole_sc[...]
    scaled = normalize(pick(s_ref, b, quarter, own[...], near[...], far[...]), 1.0)[0]
    cols_ref[0:1] += jnp.sum(value * scaled, axis=0, keepdims=True)
    deal(s_ref, b, quarter, value, outs)


def branch_body(parts, quarter, s_ref, gated, *rest):
    ws2 = rest[:parts]
    outs = rest[parts : parts + 4]
    whole_sc = rest[parts + 4]
    inner = gated.shape[1]
    shard = ws2[0].shape[0]
    for j in range(parts):
        whole_sc[:, lanes_of(s_ref, j, shard)] = mm(gated[...], ws2[j][:, inner:], NT)
    deal(s_ref, pl.program_id(0), quarter, whole_sc[...], outs)


def finish_body(inner, s_ref, first, second, rate, taps_ref, bias_ref, gain_ref, staps_ref, sbias_ref, raw_ref,
                rate_ref, skip_ref, norm_ref):
    both = (first, second)
    heads = inner // 64
    lane = lax.broadcasted_iota(jnp.int32, (8, 128), 1)
    pairs, skips = [], []
    for n, part in enumerate(both):
        at = slice(n * inner, (n + 1) * inner)
        taps_ref[:, at] = part[0:4, :inner]
        bias_ref[:, at] = part[4:5, :inner]
        gain_ref[:, at] = part[8:9, :inner]
        here = slice(n * 128, (n + 1) * 128)
        staps_ref[:, here] = part[0:4, inner:]
        sbias_ref[:, here] = part[4:5, inner:]
        turn = (128 - HEAD0 + n * heads) % 128
        pairs.append(pltpu.roll(part[0:8, inner:], turn, 1))
        skips.append(pltpu.roll(mm(three(part[8:16, :inner]), collector(inner)), turn, 1))
    values = jnp.where(lane < heads, pairs[0], pairs[1])
    skip = jnp.where(lane < heads, skips[0], skips[1])
    raw_ref[...] = values[5:6, : 2 * heads]
    rate_ref[...] = values[6:7, : 2 * heads] * rate[...]
    skip_ref[...] = skip[1:2, : 2 * heads]
    norm_ref[...] = first[8:16, inner:] + second[8:16, inner:]


def per_device(
    hidden, lengths, cotangent, norm_gain, proj_main, proj_state, proj_delta, conv_main, conv_state,
    bias_main, bias_state, delta_bias, log_rate, skip_gain, gate_gain, proj_out,
):
    _, steps, model = hidden.shape
    hidden, cotangent = hidden[0], cotangent[0]
    dps, ctxs, tps = lax.axis_size("dp"), lax.axis_size("ctx"), lax.axis_size("tp")
    dp, z, core = lax.axis_index("dp"), lax.axis_index("ctx"), lax.axis_index("tp")
    lo, hi = z % 2, z // 2
    pairs = ctxs // 2
    tokens = 2 * steps
    count = tokens // BLOCK
    quarter = count // 4
    inner = bias_main.shape[0] // 2
    heads = delta_bias.shape[0] // 2
    states = bias_state.shape[0] // 2
    wide = inner + 2 * states

    def swap(value):
        return lax.ppermute(value, "tp", [(0, 1), (1, 0)])

    def across(value, j):
        return lax.ppermute(value, "ctx", [(i, i ^ j) for i in range(ctxs)])

    def along(value, step):
        return lax.ppermute(
            value, "ctx", [(i, i + step) for i in range(ctxs) if 0 <= i + step < ctxs]
        )

    def spread(value, j):
        return lax.ppermute(value, "dp", [(i, i ^ j) for i in range(dps)])

    def mine(value, axis, size):
        return lax.dynamic_slice_in_dim(value, lo * size, size, axis)

    def piece(value, at, size):
        return lax.dynamic_slice_in_dim(value, at * size, size, 0)

    apart = proj_main.shape[0] % 128 == 0
    parts = dps if apart else 1
    shard = proj_main.shape[0] * (dps // parts)

    def gathered(value):
        if not apart:
            return [lax.all_gather(value, "dp", axis=0, tiled=True)]
        return [value] + [spread(value, j) for j in range(1, dps)]

    scalars = jnp.stack(
        [lo, core, hi * tokens, lengths[0], (hi > 0).astype(jnp.int32), (hi < pairs - 1).astype(jnp.int32)]
        + [dp ^ j if apart else 0 * dp for j in range(parts)]
    ).astype(jnp.int32)

    state_own = lax.dynamic_slice_in_dim(proj_state, lo * states + core * (states // 2), states // 2, 1)
    delta_own = mine(proj_delta, 1, heads)
    main_part = mine(proj_main, 2, inner)
    first = jnp.concatenate(
        [main_part[:, 1], proj_state, state_own, delta_own,
         jnp.zeros((proj_main.shape[0], 64 - heads), BF16)], axis=1
    )
    halfway = steps // 2
    near = across(piece(hidden, core, halfway), 1)
    far = swap(near)
    ws1 = gathered(first)

    def payloads(pieces, scale, riders=()):
        return [packed(pieces[j], scale[0], scale[1], riders) for j in range(1, parts)]

    def over_sequences(payload):
        return [spread(payload[j - 1], j) for j in range(1, parts)]

    def totalled(pieces, scale, got, riders=()):
        total, power = pieces[0], scale[0][0:1]
        if not apart:
            total = lax.psum_scatter(total, "dp", scatter_dimension=0, tiled=True)
            power = exponents(jnp.max(jnp.abs(total), axis=0, keepdims=True))
            riders = [lax.psum(value, "dp") for value in riders]
        for sent in got:
            value, other, more = unpacked(sent, [rider.shape[0] for rider in riders])
            total, power = total + value, jnp.maximum(power, other)
            riders = [one + two for one, two in zip(riders, more)]
        return total, power + (parts - 1).bit_length(), riders

    def chunks(totals, power, riders=()):
        size = totals[0].shape[0] // ctxs
        rows = [jnp.concatenate([piece(total, z ^ j, size) for total in totals], axis=1) for j in range(ctxs)]
        return rows[:1] + [packed(value, power, jnp.exp2(-power), riders) for value in rows[1:]]

    def over_positions(cut):
        return [across(cut[j], j) for j in range(1, ctxs)]

    def settled(own, got):
        opposite = got[0]
        for j in range(2, ctxs):
            if j % 2 == 0:
                own = own + got[j - 1]
            else:
                opposite = opposite + got[j - 1]
        return jnp.where(lo == 0, own, opposite), jnp.where(lo == 0, opposite, own)

    def decoded(got, counts=()):
        return [unpacked(sent, counts)[0] for sent in got]

    def ridden(got, counts):
        return [unpacked(sent, counts)[2][0] for sent in got]

    taps_x = jnp.concatenate([mine(conv_main, 1, inner), conv_state], axis=1)
    bias_x = jnp.concatenate([mine(bias_main, 0, inner), bias_state])[None]
    rate_own = -jnp.exp(mine(log_rate, 0, heads))

    def in_heads(value):
        return jnp.pad(value, (HEAD0, 128 - HEAD0 - heads))[None]

    rate_row = in_heads(rate_own)
    dbias_row = in_heads(mine(delta_bias, 0, heads))
    skip_row = jnp.repeat(mine(skip_gain, 0, heads), inner // heads)[None]
    ggain_row = mine(gate_gain, 0, inner)[None]
    gain_row = norm_gain[None]
    edge, scalars, taps_x, bias_x, rate_row, dbias_row, _ = lax.optimization_barrier(
        (hidden[steps - 16 :], scalars, taps_x, bias_x, rate_row, dbias_row, first)
    )
    route = [
        ((z0 - 1) * tps + c, (z0 + c) * tps + c) for z0 in range(2, ctxs, 2) for c in range(2)
    ]
    edge = lax.ppermute(edge, ("ctx", "tp"), route)
    halo = jnp.where(core == lo, edge, swap(edge))

    near, cot_later = lax.optimization_barrier((near, cotangent))
    ws1, near, main_gate, out_later = lax.optimization_barrier((ws1, near, main_part[:, 0], proj_out))
    second = jnp.concatenate([main_gate, mine(out_later, 1, inner)], axis=1)
    ws2 = gathered(second)
    cot_near = across(piece(cot_later, core, halfway), 1)

    own_spec = pl.BlockSpec(
        (BLOCK, model), lambda b, s: (jnp.clip(b - s[LO] * 2 * quarter, 0, 2 * quarter - 1), 0)
    )
    part_spec = pl.BlockSpec((BLOCK, model), lambda b, s: (b % quarter, 0))
    subs = BLOCK // SUB
    last = count * subs
    state_block = pl.BlockSpec((subs, states, inner), lambda b, s: (b, 0, 0))
    pre_block = pl.BlockSpec((subs, 8, inner), lambda b, s: (b, 0, 0))

    normed, u, uh, conv, per_head, hloc, pre, own_end = grid_call(
        functools.partial(front_body, parts, inner, states, quarter),
        (count,),
        [own_spec, part_spec, part_spec, whole((16, model)), whole((1, model)), whole((4, wide)),
         whole((1, wide)), whole((1, 128)), whole((1, 128))] + [whole((shard, wide + 128))] * parts,
        [rows_spec(model), rows_spec(wide), whole((8, wide)), rows_spec(wide), rows_spec(128),
         state_block, whole((last + 1, 8, inner)), whole((states, inner))],
        [shaped((tokens, model), BF16), shaped((tokens, wide)), shaped((8, wide)), shaped((tokens, wide)),
         shaped((tokens, 128)), shaped((last, states, inner)), shaped((last + 1, 8, inner)),
         shaped((states, inner))],
        [pltpu.VMEM((16, model), BF16), pltpu.VMEM((8 + BLOCK, wide), F32), pltpu.VMEM((states, inner), F32),
         pltpu.VMEM((8, inner), F32), pltpu.VMEM((384, inner), BF16), pltpu.VMEM((model, wide + 128), BF16)],
        name="front",
    )(scalars, hidden, near, far, halo, gain_row, taps_x, bias_x, dbias_row, rate_row, *ws1)

    cot_near, own_end = lax.optimization_barrier((cot_near, own_end))
    cot_far = swap(cot_near)
    growth = jnp.exp(pre[last][0:1])
    carried = jnp.zeros_like(own_end)
    sending = own_end
    for hop in range(pairs - 1):
        carried = along(sending, 2)
        if hop < pairs - 2:
            sending = own_end + growth * carried

    (inside,) = grid_call(
        functools.partial(within_body, inner, states),
        (count,),
        [rows_spec(wide), rows_spec(128)],
        [rows_spec(inner)],
        [shaped((tokens, inner))],
        [pltpu.VMEM((384, inner), BF16)] * 2,
        name="within",
        limit=20 << 20,
    )(scalars, *streamed(conv, per_head))

    gate, gated_grad, branch_grad = grid_call(
        functools.partial(gates_body, parts, quarter),
        (count,),
        [rows_spec(model), own_spec, part_spec, part_spec] + [whole((shard, 2 * inner))] * parts,
        [rows_spec(inner), rows_spec(inner), rows_spec(model)],
        [shaped((tokens, inner)), shaped((tokens, inner)), kept((tokens, model), BF16)],
        [pltpu.VMEM((model, 2 * inner), BF16)],
        name="gates",
        limit=20 << 20,
    )(scalars, *streamed(normed, cotangent, cot_near, cot_far, *ws2))

    y, sums = grid_call(
        functools.partial(output_body, inner, states),
        (count,),
        [rows_spec(wide), rows_spec(128), rows_spec(inner), rows_spec(inner), rows_spec(inner), state_block,
         pre_block, whole((states, inner)), whole((1, inner)), whole((1, inner))],
        [rows_spec(inner), pl.BlockSpec((16, BLOCK), lambda b, s: (0, b))],
        [shaped((tokens, inner)), shaped((16, tokens))],
        [pltpu.VMEM((384, inner), BF16)],
        name="output",
        limit=20 << 20,
    )(scalars, *streamed(conv, per_head), inside, gate, gated_grad, *streamed(hloc), pre, carried, skip_row, ggain_row)

    corner = [(n, ((n // tps) ^ 1) * tps + (n % tps + 1) % tps) for n in range(ctxs * tps)]
    all_sums = [sums, swap(sums), across(sums, 1), lax.ppermute(sums, ("ctx", "tp"), corner)]

    def back(width, rows=BLOCK):
        return pl.BlockSpec((rows, width), lambda b, s: (count - 1 - b, 0))

    back_sums = pl.BlockSpec((16, BLOCK), lambda b, s: (0, count - 1 - b))
    gated, gate_grad, out_grad, gloc, own_start, turn_cols = grid_call(
        functools.partial(turn_body, inner, states, 2 * tps * inner),
        (count,),
        [back(wide), back(128), back(inner), back(inner), back(inner),
         back_sums, back_sums, back_sums, back_sums, whole((1, inner)), whole((1, inner))],
        [back(inner), back(inner), back(inner),
         pl.BlockSpec((subs, states, inner), lambda b, s: (count - 1 - b, 0, 0)), whole((states, inner)),
         whole((8, inner))],
        [shaped((tokens, inner), BF16), shaped((tokens, inner), BF16), kept((tokens, inner)),
         kept((last, states, inner)), shaped((states, inner)), shaped((8, inner))],
        [pltpu.VMEM((states, inner), F32), pltpu.VMEM((384, inner), BF16)],
        name="turn",
        limit=20 << 20,
    )(scalars, *streamed(conv, per_head), y, gate, gated_grad, *all_sums, skip_row, ggain_row)

    returned = jnp.zeros_like(own_start)
    sending = own_start
    for hop in range(pairs - 1):
        returned = along(sending, -2)
        if hop < pairs - 2:
            sending = own_start + growth * returned

    turned = pl.BlockSpec((tokens, shard), lambda j, s: (0, s[SLOT0 + j]))
    dealt_specs = [whole((halfway, model))] * 4
    dealt_shapes = [shaped((halfway, model))] * 4
    def grads(lefts, rights, name, limit=None):
        sources = []
        for left, right in zip(lefts, rights):
            sources += [left, right]
        width = sum(right.shape[1] for right in rights)
        specs = [turned if n % 2 == 0 else whole(source.shape) for n, source in enumerate(sources)]
        *pieces, powers, inverse = grid_call(
            functools.partial(grads_body, parts, [(n, n + 1) for n in range(0, len(sources), 2)]),
            (parts,),
            specs,
            [whole((shard, width))] * parts + [whole((16, width)), whole((1, width))],
            [shaped((shard, width))] * parts + [shaped((16, width)), shaped((1, width))],
            [pltpu.VMEM((8, width), F32)],
            name=name,
            limit=limit,
        )(scalars, *sources)
        return pieces, (powers, inverse)

    early, early_scale = grads(streamed(normed, branch_grad), [gate_grad, gated], "grad_early", 20 << 20)
    early_got = over_sequences(payloads(early, early_scale))
    early, out_grad = lax.optimization_barrier((early, out_grad))

    zed, dbc = grid_call(
        functools.partial(back_body, inner, states),
        (count,),
        [rows_spec(wide), rows_spec(128), rows_spec(inner), state_block, pre_block, whole((states, inner))],
        [rows_spec(inner), rows_spec(2 * states)],
        [shaped((tokens, inner)), shaped((tokens, 2 * states))],
        [pltpu.VMEM((384, inner), BF16)] * 2,
        name="back",
    )(scalars, conv, per_head, out_grad, hloc, pre, carried)

    gated_later, zed = lax.optimization_barrier((gated, zed))
    branch = grid_call(
        functools.partial(branch_body, parts, quarter),
        (count,),
        [rows_spec(inner)] + [whole((shard, 2 * inner))] * parts,
        dealt_specs,
        dealt_shapes,
        [pltpu.VMEM((BLOCK, model), F32)],
        name="branch",
    )(scalars, gated_later, *ws2)

    returned, early_got, branch = lax.optimization_barrier((returned, early_got, branch))
    front_rows = halfway // 16 * 5
    branch_give = swap(branch[3])
    branch_theirs = [branch[1][:front_rows] + branch_give[:front_rows], branch[1][front_rows:] + branch_give[front_rows:]]
    returned, branch_theirs = lax.optimization_barrier((returned, branch_theirs))
    branch_back = [across(branch_theirs[0], 1)]
    all_pre = whole((last + 1, 8, inner))
    per = BLOCK // 8
    half_rows = tokens // 2

    def back_lanes(width, lanes):
        return [
            pl.BlockSpec((BLOCK, width), lambda b, s: (count - 1 - b, lanes(s))),
            pl.BlockSpec((8, width), lambda b, s: (jnp.maximum((count - 1 - b) * per - 1, 0), lanes(s))),
            pl.BlockSpec((8, width), lambda b, s: (0, lanes(s))),
        ]

    def table(rows, width, lanes):
        return pl.BlockSpec((rows, width), lambda b, s: (0, lanes(s)))

    zed, ends, dbc_keep, dbc_give, head = grid_call(
        functools.partial(meet_body, inner, states),
        (count,),
        [rows_spec(wide), rows_spec(128), rows_spec(inner), rows_spec(2 * states), state_block,
         pl.BlockSpec((1, states, inner), lambda b, s: (jnp.minimum((b + 1) * subs, last - 1), 0, 0)),
         whole((states, inner)), all_pre, state_block, whole((states, inner)), whole((states, inner)), whole((8, inner)), whole((1, inner))],
        [rows_spec(inner), rows_spec(inner, 8), whole((half_rows, 2 * states)), whole((half_rows, 2 * states)),
         whole((8, inner))],
        [shaped((tokens, inner)), shaped((8 * count, inner)), shaped((half_rows, 2 * states)),
         shaped((half_rows, 2 * states)), shaped((8, inner))],
        [pltpu.VMEM((384, inner), BF16)] * 2,
        name="meet",
        limit=20 << 20,
    )(scalars, *streamed(conv, per_head, zed, dbc, hloc, hloc), own_end, *streamed(pre, gloc), returned, carried, *streamed(out_grad), skip_row)

    zed, ends, dbc_keep, dbc_give, branch_back = lax.optimization_barrier((zed, ends, dbc_keep, dbc_give, branch_back))
    early_total, early_power, _ = totalled(early, early_scale, early_got)
    early_cut = chunks([early_total], early_power)
    early_far = over_positions(early_cut)
    signal_pre, tail, raw_grad, head_cols, signal_cols = grid_call(
        functools.partial(join_body, inner),
        (count,),
        [back(inner), back(128), back(inner), back(inner), back(inner), back(inner, 8)]
        + back_lanes(inner, lambda s: 0)
        + [table(4, inner, lambda s: 0), whole((1, 128)), whole((1, inner))],
        [back(inner), whole((8, inner)), back(128), whole((8, 128)), whole((8, inner))],
        [shaped((tokens, inner), BF16), shaped((8, inner)), shaped((tokens, 128)),
         shaped((8, 128)), shaped((8, inner))],
        [pltpu.VMEM((3 * inner, 128), BF16), pltpu.VMEM((BLOCK + 8, inner), F32),
         pltpu.VMEM((BLOCK + 8, inner), F32), pltpu.VMEM((384, inner), BF16)],
        name="join",
        limit=20 << 20,
    )(scalars, *streamed(conv, per_head, out_grad, y), zed, ends, *streamed(u, u), uh, taps_x, rate_row, skip_row)

    tail, early_far = lax.optimization_barrier((tail, early_far))
    early_sum = settled(early_cut[0], decoded(early_far))
    out_sum = jnp.concatenate([part[:, inner:] for part in early_sum], axis=1)
    gate_sum = jnp.concatenate([part[:, :inner] for part in early_sum], axis=1)

    ahead, out_sum, gate_sum = lax.optimization_barrier((along(head, -2), out_sum, gate_sum))
    ahead = jnp.where(hi < pairs - 1, ahead, 0.0)
    for k in range(3):
        tail = tail + taps_x[k, :inner] * jnp.concatenate([jnp.zeros((5 + k, inner), F32), ahead[: 3 - k]])
    signal_pre = lax.dynamic_update_slice_in_dim(signal_pre, tail.astype(BF16), tokens - 8, 0)

    dbc = dbc_keep + swap(dbc_give)
    signal_pre, dbc = lax.optimization_barrier((signal_pre, dbc))
    dbc_back = across(lax.dynamic_slice_in_dim(dbc, (1 - lo) * states, states, 1), 1)
    signal_small = jnp.concatenate([signal_cols, turn_cols])
    signal, signal_scale = grads(streamed(normed), streamed(signal_pre), "grad_signal", 20 << 20)
    signal, dbc_back = lax.optimization_barrier((signal, dbc_back))
    signal_payload = payloads(signal, signal_scale, [signal_small])

    dbc = mine(dbc, 1, states) + dbc_back
    dbc_other = swap(dbc)
    head_rows = jnp.where(core == 0, dbc[:8], dbc_other[:8])
    head_conv = lax.dynamic_slice(conv, (0, inner + lo * states), (8, states))
    state_ahead = along(head_rows * slope(head_conv, jax.nn.sigmoid(head_conv)), -2)
    branch_later, state_ahead, signal_payload = lax.optimization_barrier((branch_theirs[1], state_ahead, signal_payload))
    signal_got = over_sequences(signal_payload)
    def back_own(b, s):
        return jnp.clip(count - 1 - b - s[LO] * 2 * quarter, 0, 2 * quarter - 1), 0

    def state_lanes(s):
        return inner // states + s[LO]

    back_part = pl.BlockSpec((BLOCK, model), lambda b, s: ((count - 1 - b) % quarter, 0))
    back_half = pl.BlockSpec((BLOCK, states), lambda b, s: ((count - 1 - b) % (count // 2), 0))
    state_side = back_lanes(states, state_lanes)
    *feature, extra_pre, feature_cols, state_cols = grid_call(
        functools.partial(feature_body, parts, quarter),
        (count,),
        [pl.BlockSpec((BLOCK, model), back_own), back_part, back_part, back(inner), back(inner), back(128),
         back_half, back_half, state_side[0]] + state_side
        + [whole((8, states)), table(4, states, state_lanes)]
        + [whole((shard, wide + 128))] * parts + [whole((shard, 2 * inner))] * parts,
        dealt_specs + [back(128), whole((8, model)), whole((8, states))],
        dealt_shapes + [shaped((tokens, 128), BF16), shaped((8, model)), shaped((8, states))],
        [pltpu.VMEM((BLOCK, model), F32), pltpu.VMEM((BLOCK + 8, states), F32),
         pltpu.VMEM((BLOCK + 8, states), F32)],
        name="feature",
        limit=24 << 20,
    )(scalars, *streamed(hidden, near, far, gate_grad, signal_pre, raw_grad), dbc, dbc_other, *streamed(conv, u, u), uh,
      state_ahead, taps_x, *streamed(*ws1, *ws2))
    feature, branch_rest, signal_got = lax.optimization_barrier((feature, across(branch_later, 1), signal_got))
    branch_back = jnp.concatenate(branch_back + [branch_rest])
    feature_theirs = feature[1] + swap(feature[3])
    feature_mine = feature[0] + swap(feature[2])

    folds = model // 128
    extra_small = jnp.concatenate(
        [state_cols[:5], head_cols[:2], jnp.zeros((1, 128), F32), feature_cols[0].reshape(folds, 128)]
    )
    feature_power = exponents(jnp.max(jnp.abs(feature_theirs), axis=0, keepdims=True))
    feature_payload = packed(feature_theirs, feature_power, jnp.exp2(-feature_power))
    extra_pre, feature_payload = lax.optimization_barrier((extra_pre, feature_payload))
    extra, extra_scale = grads(streamed(normed), [extra_pre], "grad_extra", 20 << 20)
    feature_back = across(feature_payload, 1)
    signal_total, signal_power, (signal_here,) = totalled(signal, signal_scale, signal_got, [signal_small])
    extra_got = over_sequences(payloads(extra, extra_scale, [extra_small]))
    extra_got, feature_back = lax.optimization_barrier((extra_got, feature_back))
    extra_total, extra_power, (extra_here,) = totalled(extra, extra_scale, extra_got, [extra_small])
    late_power = jnp.concatenate([signal_power, extra_power], axis=1)
    small_here = jnp.concatenate([signal_here, extra_here], axis=1)
    late_cut = chunks([signal_total, extra_total], late_power, [small_here])
    feature_back, late_cut = lax.optimization_barrier((feature_back, late_cut))
    late_far = over_positions(late_cut)
    feature_back = unpacked(feature_back)[0]

    def both_halves(value):
        other = swap(value)
        return jnp.where(core == 0, jnp.concatenate([value, other]), jnp.concatenate([other, value]))

    residual = piece(hidden, core, halfway).astype(F32)
    place = z * steps + core * halfway + lax.broadcasted_iota(jnp.int32, (halfway, 1), 0)
    valid = (place < lengths[0]).astype(F32)
    mixed = both_halves((residual + valid * (branch[0] + swap(branch[2]) + branch_back)).astype(BF16))

    feature_grad = feature_mine + feature_back
    inverse = lax.rsqrt(jnp.mean(residual * residual, axis=1, keepdims=True) + EPSILON)
    scaled_own = residual * inverse
    scaled_grad = feature_grad * norm_gain
    upstream = piece(cotangent, core, halfway).astype(F32)
    grad_hidden = both_halves(
        upstream + inverse * (scaled_grad - scaled_own * jnp.mean(scaled_grad * scaled_own, axis=1, keepdims=True))
    )

    mixed, grad_hidden, late_far = lax.optimization_barrier((mixed, grad_hidden, late_far))
    late_sum = settled(late_cut[0], decoded(late_far, [16]))
    small_sum = settled(small_here, ridden(late_far, [16]))

    def side_by_side(pair):
        return jnp.concatenate(pair, axis=-1)

    taps_sum, bias_sum, ggain_sum, state_taps, state_bias, raw_sum, rate_sum, skip_sum, gain_here = grid_call(
        functools.partial(finish_body, inner),
        (1,),
        [whole((16, inner + 128)), whole((16, inner + 128)), whole((1, 2 * heads))],
        [whole((4, 2 * inner)), whole((1, 2 * inner)), whole((1, 2 * inner)), whole((4, 2 * states)),
         whole((1, 2 * states)), whole((1, 2 * heads)), whole((1, 2 * heads)), whole((1, 2 * heads)),
         whole((8, 128))],
        [shaped((4, 2 * inner)), shaped((1, 2 * inner)), shaped((1, 2 * inner)), shaped((4, 2 * states)),
         shaped((1, 2 * states)), shaped((1, 2 * heads)), shaped((1, 2 * heads)), shaped((1, 2 * heads)),
         shaped((8, 128))],
        name="finish",
    )(scalars, *small_sum, -jnp.exp(log_rate)[None])
    gain_here = gain_here.reshape(model)
    state_here = jnp.stack([part[:, inner : inner + HEAD0] for part in late_sum])
    gain_there, state_there = swap(gain_here), swap(state_here)
    gain_size = model // (dps * ctxs)
    gain_sum = piece(gain_here + gain_there, dp * ctxs + z, gain_size)
    in_order = jnp.where(
        core == 0, jnp.stack([state_here, state_there], 1), jnp.stack([state_there, state_here], 1)
    )
    state_sum = jnp.transpose(in_order, (2, 0, 1, 3)).reshape(-1, 2 * states)
    main_sum = jnp.stack([gate_sum, side_by_side([part[:, :inner] for part in late_sum])], axis=1)
    delta_sum = side_by_side([part[:, inner + HEAD0 : inner + HEAD0 + heads] for part in late_sum])

    return (
        mixed[None],
        grad_hidden[None],
        gain_sum,
        main_sum,
        state_sum,
        delta_sum,
        taps_sum,
        state_taps,
        bias_sum[0],
        state_bias[0],
        raw_sum[0],
        rate_sum[0],
        skip_sum[0],
        ggain_sum[0],
        out_sum,
    )


def solution(mesh):
    in_specs = (
        P("dp", "ctx", None), P("dp"), P("dp", "ctx", None), P(), P("dp", None, "tp"), P("dp", None),
        P("dp", "tp"), P(None, "tp"), P(), P("tp"), P(), P("tp"), P("tp"), P("tp"), P("tp"), P("dp", "tp"),
    )
    out_specs = (
        P("dp", "ctx", None), P("dp", "ctx", None), P(("dp", "ctx")), P(("dp", "ctx"), None, "tp"),
        P(("dp", "ctx"), None), P(("dp", "ctx"), "tp"), P(None, "tp"), P(), P("tp"), P(), P("tp"), P("tp"),
        P("tp"), P("tp"), P(("dp", "ctx"), "tp"),
    )
    return jax.shard_map(
        per_device, mesh=mesh, in_specs=in_specs, out_specs=out_specs, check_vma=False
    )
```
